128 devices in a mesh: section: 4 (over y_lo, core), seq: 32 (over y_hi, z, x).
Axes of the slice: x: 4, y: 4 (y_hi: 2, y_lo: 2; y = y_hi * 2 + y_lo), z: 4, core: 2. Of those that a mesh axis runs over, the one named last changes fastest.
Arguments:
- context: bfloat16 [8192, 8192], P('seq'), may hold values from -24 to 24, as said below
- memory: bfloat16 [2048, 8192], P('seq'), may hold values from -24 to 24, as said below
- query_weight: bfloat16 [8192, 4096], P(None, 'section'), may hold values from -0.0625 to 0.0625
- key_weight: bfloat16 [8192, 512], P('seq', 'section'), may hold values from -0.0625 to 0.0625
- value_weight: bfloat16 [8192, 512], P('seq', 'section'), may hold values from -0.0625 to 0.0625
- query_down_map: bfloat16 [8192, 128], replicated, may hold values from -0.0625 to 0.0625
- query_up_map: bfloat16 [128, 4096], P(None, 'section'), may hold values from -0.5 to 0.5
- value_down_map: bfloat16 [8192, 128], P('seq'), may hold values from -0.0625 to 0.0625
- value_up_map: bfloat16 [128, 512], P(None, 'section'), may hold values from -0.5 to 0.5
- output_weight: bfloat16 [4096, 8192], P('section', 'seq'), may hold values from -1 to 1
- decoder_gain: float32 [8192], P('seq'), may hold values from 0.25 to 1.75
- document_slots: int32 [8], replicated, may hold values from 1 to 1088, 2048 in all
- normed_gradient: bfloat16 [2048, 8192], P('section', 'seq'), may hold values from -6 to 6
Outputs:
- normed: bfloat16 [2048, 8192], P('section', 'seq')
- grad_qa: float32 [8192, 128], P(('section', 'seq'))
- grad_va: float32 [8192, 128], P(('section', 'seq'))
- query_up_gradient: float32 [128, 4096], P(None, 'section')
- value_up_gradient: float32 [128, 512], P(None, 'section')
The draws below stay inside these ranges and needn't reach their ends.
Inputs may be any that keep to these rules, and one draw needn't show every extreme that they name: `context`: values of the normed inputs lie in this range. `memory`: values of the normed inputs lie in this range. Documents lie end to end in order; document d has document_slots[d] memory slots and 4 document_slots[d] context tokens; the counts sum to 2048.
All inputs are finite; a program needn't handle non-finite values.
Results may differ from the reference program's by a relative error of at most 0.014.
The reference program's roundings to bfloat16 on the way count: a program that leaves them out, or rounds other values in their place, can miss the bound.
Values may be sent and summed in bfloat16 or wider, within the bound.
A program may use at most 192 MiB of HBM per device.

```python
import math
import jax
import jax.numpy as jnp
import numpy as np
from jax import lax

MODEL_DIM = 8192
HEADS = 32
KV_HEADS = 4
HD = 128
ADAPTER_RANK = 128
DOCS = 8
SLOT_DEV = 64
LEN = 8192
SLOTS = 2048
KEYS = 10240
QUERY_FEATURES = 4096
KEY_FEATURES = 512


def input_rows(key, row_total):
    base = jnp.clip(jax.random.normal(jax.random.fold_in(key, 11), (row_total, MODEL_DIM), jnp.float32), -4.0, 4.0)
    return base


def draw_context(key, part):
    return input_rows(jax.random.fold_in(key, 21), LEN).astype(jnp.bfloat16)


def draw_memory(key, part):
    return input_rows(jax.random.fold_in(key, 22), SLOTS).astype(jnp.bfloat16)


def draw_output_weight(key, part):
    ramp = 0.6 + 1.2 * jnp.arange(MODEL_DIM, dtype=jnp.float32) / MODEL_DIM
    base = jnp.clip(jax.random.normal(jax.random.fold_in(key, 32), (QUERY_FEATURES, MODEL_DIM), jnp.float32), -4.0, 4.0)
    return jnp.clip(base * ramp[None, :] * QUERY_FEATURES ** (-0.5), -1.0, 1.0).astype(jnp.bfloat16)


def raised(entries, key, source, target, blocks, factor):
    owner, partner = [(jnp.arange(entries.shape[position]) // (entries.shape[position] // blocks)).reshape([-1 if axis == position else 1 for axis in range(entries.ndim)]) for position in (source, target)]
    chosen = jax.random.permutation(key, blocks)[partner]
    strong = (owner == chosen) | (owner == (partner + blocks // 2) % blocks)
    return jnp.where(strong, factor * entries, entries)


def levels(key, extent, split, smallest, top_value):
    level = 1.0
    for dim, shards_of in split:
        heights = jax.random.uniform(jax.random.fold_in(jax.random.fold_in(key, 6), dim), (shards_of,), jnp.float32, smallest / len(split), top_value / len(split))
        level = level * jnp.repeat(jnp.exp(heights), extent[dim] // shards_of).reshape((-1,) + (1,) * (len(extent) - 1 - dim))
    return level


def length_profile(amount, total, limit, lean):
    loads = [(1 << 20) // math.isqrt(rank ** lean) + 1 for rank in range(2, amount + 1)]
    spare, holding = total - limit - (amount - 1), [1] * (amount - 1)
    while spare > 0:
        free = [i for i in range(amount - 1) if holding[i] < limit]
        mass, budget = sum([loads[i] for i in free]), spare
        for i in free:
            addition = min(limit - holding[i], max(1, budget * loads[i] // mass), spare)
            holding[i] = holding[i] + addition
            spare = spare - addition
    return np.array([limit] + holding)


def ragged_sizes(rng, count, total, most, slope):
    if count == 2:
        one = jax.random.randint(rng, (), max(1, total - most), min(most, total - 1) + 1)
        return jnp.stack([one, total - one])
    lengths = jnp.asarray(length_profile(count, total, most, slope), jnp.int32)
    twos = (count - 1) // 2
    donor, taker = lengths[1:1 + 2 * twos:2], lengths[2:2 + 2 * twos:2]
    margin = jnp.minimum(donor - 1, most - taker)
    shifted = jax.random.randint(jax.random.fold_in(rng, 1), (twos,), 0, 1 << 20) % (margin + 1)
    lengths = lengths.at[1:1 + 2 * twos:2].set(donor - shifted).at[2:2 + 2 * twos:2].set(taker + shifted)
    return lengths[jax.random.permutation(jax.random.fold_in(rng, 2), count)]


def normal_values(key, extent, width, reach, pieces=(), held_as=jnp.bfloat16):
    array = width * jax.random.normal(key, extent, jnp.float32)
    if pieces:
        array = array * levels(key, extent, pieces, -0.22, 0.18)
    return jnp.clip(array, -reach, reach).astype(held_as)


def gaussian_with(stream_key, extent, deviation, limit, split, heavy, kind=jnp.bfloat16):
    result = deviation * jax.random.normal(stream_key, extent, jnp.float32)
    if split:
        result = result * levels(stream_key, extent, split, -0.22, 0.18)
    return jnp.clip(raised(result, jax.random.fold_in(stream_key, 3), *heavy), -limit, limit).astype(kind)


def setup_inputs(seed: int = 0) -> dict:
    key_of = jax.random.split(jax.random.key(seed), 14)
    return {
        "context": draw_context(jax.random.fold_in(key_of[13], 71), 0),
        "memory": draw_memory(jax.random.fold_in(key_of[13], 71), 0),
        "query_weight": normal_values(key_of[2], (MODEL_DIM, QUERY_FEATURES), MODEL_DIM ** -0.5, 0.0625, ((1, 4),)),
        "key_weight": normal_values(key_of[3], (MODEL_DIM, KEY_FEATURES), MODEL_DIM ** -0.5, 0.0625, ((0, 32), (1, 4))),
        "value_weight": normal_values(key_of[4], (MODEL_DIM, KEY_FEATURES), MODEL_DIM ** -0.5, 0.0625, ((0, 32), (1, 4))),
        "query_down_map": normal_values(key_of[5], (MODEL_DIM, ADAPTER_RANK), MODEL_DIM ** -0.5, 0.0625),
        "query_up_map": normal_values(key_of[6], (ADAPTER_RANK, QUERY_FEATURES), ADAPTER_RANK ** -0.5, 0.5, ((1, 4),)),
        "value_down_map": normal_values(key_of[7], (MODEL_DIM, ADAPTER_RANK), MODEL_DIM ** -0.5, 0.0625, ((0, 32),)),
        "value_up_map": normal_values(key_of[8], (ADAPTER_RANK, KEY_FEATURES), ADAPTER_RANK ** -0.5, 0.5, ((1, 4),)),
        "output_weight": draw_output_weight(jax.random.fold_in(key_of[13], 71), 0),
        "decoder_gain": jnp.clip(1.0 + 0.15 * jax.random.normal(key_of[10], (MODEL_DIM,), jnp.float32), 0.25, 1.75),
        "document_slots": ragged_sizes(key_of[11], DOCS, SLOTS, SLOTS // 2 + SLOT_DEV, 2).astype(jnp.int32),
        "normed_gradient": gaussian_with(key_of[12], (SLOTS, MODEL_DIM), 1.0, 6.0, ((0, 4), (1, 32)), (1, 0, 32, 2.75)),
    }


adapter_scale = 0.25
epsilon = 1e-05
mask_fill = -1e+30

def doc_index(units, doc_ends):
    return lax.optimization_barrier(jnp.sum((units[:, None] >= doc_ends[None, :]).astype(jnp.int32), axis=1)).astype(jnp.int32)

def block_probs(query_block, keys_head, slot_unit, key_unit, key_doc, is_context, doc_ends, group_heads):
    query_rows = query_block.reshape(-1, HD)
    row_unit = jnp.repeat(slot_unit, group_heads)
    row_doc = doc_index(row_unit, doc_ends)
    allowed = (key_doc[None, :] == row_doc[:, None]) & (is_context[None, :] | (key_unit[None, :] <= row_unit[:, None]))
    scores = jnp.dot(query_rows, keys_head.T, preferred_element_type=jnp.float32) * HD ** (-0.5)
    scores = jnp.where(allowed, scores, mask_fill)
    row_top = lax.optimization_barrier(jnp.max(scores, axis=1, keepdims=True))
    exponent = jnp.exp(scores - row_top)
    return exponent / lax.optimization_barrier(jnp.sum(exponent, axis=1, keepdims=True))

def reference(context, memory, query_weight, key_weight, value_weight, query_down_map, query_up_map, value_down_map, value_up_map, output_weight, decoder_gain, document_slots, normed_gradient):
    doc_ends = jnp.cumsum(document_slots).astype(jnp.int32)
    every_row = jnp.concatenate([context, memory], axis=0)
    query_reduced = jnp.dot(memory, query_down_map, preferred_element_type=jnp.float32).astype(jnp.bfloat16)
    value_reduced = jnp.dot(every_row, value_down_map, preferred_element_type=jnp.float32).astype(jnp.bfloat16)
    query_rows_out = (jnp.dot(memory, query_weight, preferred_element_type=jnp.float32) + adapter_scale * jnp.dot(query_reduced, query_up_map, preferred_element_type=jnp.float32)).astype(jnp.bfloat16)
    keys_all = jnp.dot(every_row, key_weight, preferred_element_type=jnp.float32).astype(jnp.bfloat16)
    value_rows_all = (jnp.dot(every_row, value_weight, preferred_element_type=jnp.float32) + adapter_scale * jnp.dot(value_reduced, value_up_map, preferred_element_type=jnp.float32)).astype(jnp.bfloat16)
    key_unit = jnp.concatenate([jnp.arange(LEN, dtype=jnp.int32) // 4, jnp.arange(SLOTS, dtype=jnp.int32)])
    is_context = jnp.concatenate([jnp.ones((LEN,), dtype=bool), jnp.zeros((SLOTS,), dtype=bool)])
    key_doc = doc_index(key_unit, doc_ends)
    group_heads = HEADS // KV_HEADS
    group_width = group_heads * HD
    slot_block = SLOT_DEV
    block_total = SLOTS // slot_block

    def forward_head(head_index):
        query_head = lax.dynamic_slice_in_dim(query_rows_out, head_index * group_width, group_width, 1)
        keys_head = lax.dynamic_slice_in_dim(keys_all, head_index * HD, HD, 1)
        values_head = lax.dynamic_slice_in_dim(value_rows_all, head_index * HD, HD, 1)

        def per_block(block_index):
            begin_row = block_index * slot_block
            query_block = lax.dynamic_slice_in_dim(query_head, begin_row, slot_block, 0)
            slot_unit = begin_row + jnp.arange(slot_block, dtype=jnp.int32)
            probs = block_probs(query_block, keys_head, slot_unit, key_unit, key_doc, is_context, doc_ends, group_heads)
            output = jnp.dot(probs.astype(jnp.bfloat16), values_head, preferred_element_type=jnp.float32)
            return output.reshape(slot_block, group_width).astype(jnp.bfloat16)
        return lax.map(per_block, jnp.arange(block_total, dtype=jnp.int32)).reshape(SLOTS, group_width)
    attended = lax.map(forward_head, jnp.arange(KV_HEADS, dtype=jnp.int32))
    attended = jnp.transpose(attended, (1, 0, 2)).reshape(SLOTS, QUERY_FEATURES)
    hidden = jnp.dot(attended, output_weight, preferred_element_type=jnp.float32)
    inv_rms = lax.rsqrt(lax.optimization_barrier(jnp.mean(hidden * hidden, axis=1)) + epsilon)
    normed = (hidden * inv_rms[:, None] * decoder_gain).astype(jnp.bfloat16)
    weighted = SLOTS ** (-0.5) * normed_gradient.astype(jnp.float32) * decoder_gain
    cross = lax.optimization_barrier(jnp.sum(weighted * hidden, axis=1))
    d_hidden = (inv_rms[:, None] * weighted - hidden * (inv_rms ** 3 * cross / MODEL_DIM)[:, None]).astype(jnp.bfloat16)
    d_attended = jnp.dot(d_hidden, output_weight.T, preferred_element_type=jnp.float32).astype(jnp.bfloat16)

    def backward_head(head_index):
        query_head = lax.dynamic_slice_in_dim(query_rows_out, head_index * group_width, group_width, 1)
        grad_head = lax.dynamic_slice_in_dim(d_attended, head_index * group_width, group_width, 1)
        keys_head = lax.dynamic_slice_in_dim(keys_all, head_index * HD, HD, 1)
        values_head = lax.dynamic_slice_in_dim(value_rows_all, head_index * HD, HD, 1)

        def per_block(value_sum, block_index):
            begin_row = block_index * slot_block
            query_block = lax.dynamic_slice_in_dim(query_head, begin_row, slot_block, 0)
            grad_block = lax.dynamic_slice_in_dim(grad_head, begin_row, slot_block, 0).reshape(-1, HD)
            slot_unit = begin_row + jnp.arange(slot_block, dtype=jnp.int32)
            probs = block_probs(query_block, keys_head, slot_unit, key_unit, key_doc, is_context, doc_ends, group_heads)
            d_probs = jnp.dot(grad_block, values_head.T, preferred_element_type=jnp.float32)
            center = lax.optimization_barrier(jnp.sum(probs * d_probs, axis=1, keepdims=True))
            d_scores = (probs * (d_probs - center)).astype(jnp.bfloat16)
            d_query = (HD ** (-0.5) * jnp.dot(d_scores, keys_head, preferred_element_type=jnp.float32)).reshape(slot_block, group_width).astype(jnp.bfloat16)
            value_sum = value_sum + jnp.dot(probs.astype(jnp.bfloat16).T, grad_block, preferred_element_type=jnp.float32)
            return (value_sum, d_query)
        value_sum, query_blocks = lax.scan(per_block, jnp.zeros((KEYS, HD), jnp.float32), jnp.arange(block_total, dtype=jnp.int32))
        return (query_blocks.reshape(SLOTS, group_width), value_sum.astype(jnp.bfloat16))
    query_parts, value_parts = lax.map(backward_head, jnp.arange(KV_HEADS, dtype=jnp.int32))
    query_gradient = jnp.transpose(query_parts, (1, 0, 2)).reshape(SLOTS, QUERY_FEATURES)
    value_gradient = jnp.transpose(value_parts, (1, 0, 2)).reshape(KEYS, KEY_FEATURES)
    query_up_gradient = adapter_scale * jnp.dot(query_reduced.T, query_gradient, preferred_element_type=jnp.float32)
    value_up_gradient = adapter_scale * jnp.dot(value_reduced.T, value_gradient, preferred_element_type=jnp.float32)
    query_backward = (adapter_scale * jnp.dot(query_gradient, query_up_map.T, preferred_element_type=jnp.float32)).astype(jnp.bfloat16)
    value_backward = (adapter_scale * jnp.dot(value_gradient, value_up_map.T, preferred_element_type=jnp.float32)).astype(jnp.bfloat16)
    grad_qa = jnp.dot(memory.T, query_backward, preferred_element_type=jnp.float32)
    grad_va = jnp.dot(every_row.T, value_backward, preferred_element_type=jnp.float32)
    return (normed, grad_qa, grad_va, query_up_gradient, value_up_gradient)
```

```python
import functools

import jax
import jax.numpy as jnp
from jax import lax
from jax.experimental import pallas as pl
from jax.experimental.pallas import tpu as pltpu
from jax.sharding import PartitionSpec as P

MODEL_DIM = 8192
HEADS_HERE = 8
HD = 128
ROWS = 512
GROUP = 2

adapter_scale = 0.25
epsilon = 1e-05
mask_fill = -1e30
score_scale = HD ** (-0.5)
exp2_scale = score_scale * 1.4426950408889634

MESH = pl.DeviceIdType.MESH
ANY = pl.BlockSpec(memory_space=pl.ANY)
VMEM = pl.BlockSpec(memory_space=pltpu.VMEM)

SIZES = {"y": 2, "z": 4, "x": 4}
AXES = "yzx"


def seq_coords():
    me = lax.axis_index("seq")
    return [me // 16, (me // 4) % 4, me % 4]


def peer(section, me, axis, step):
    at = list(me)
    k = AXES.index(axis)
    at[k] = lax.rem(at[k] + step, SIZES[axis])
    return (section, at[0] * 16 + at[1] * 4 + at[2])


def greet(devices):
    barrier = pltpu.get_barrier_semaphore()
    for device in devices:
        pl.semaphore_signal(barrier, inc=1, device_id=device, device_id_type=MESH)
    pl.semaphore_wait(barrier, len(devices))


def axis_peers(section, me):
    return [peer(section, me, a, d) for a in AXES for d in range(1, SIZES[a])]


def gather_kernel(pieces, x_ref, o_ref, send, recv, local):
    section = lax.axis_index("section")
    me = seq_coords()
    greet(axis_peers(section, me))
    own = pltpu.make_async_copy(x_ref, o_ref.at[tuple(me)], local)
    own.start()
    copies, latest = [], {}
    for phase in range(3):
        for i, (lo, size, order) in enumerate(pieces):
            if phase:
                for copy in latest[i]:
                    copy.wait_recv()
                if phase == 1 and i == 0:
                    own.wait()
            held = [slice(None) if a in order[:phase] else me[AXES.index(a)] for a in AXES]
            region = o_ref.at[tuple(held) + (pl.ds(lo, size),)]
            source = region if phase else x_ref.at[pl.ds(lo, size)]
            latest[i] = []
            for d in range(1, SIZES[order[phase]]):
                at = (i * 3 + phase) * 3 + d - 1
                copy = pltpu.make_async_remote_copy(
                    src_ref=source,
                    dst_ref=region,
                    send_sem=send.at[at],
                    recv_sem=recv.at[at],
                    device_id=peer(section, me, order[phase], d),
                    device_id_type=MESH,
                )
                copy.start()
                latest[i].append(copy)
            copies += latest[i]
    for i in range(len(pieces)):
        for copy in latest[i]:
            copy.wait_recv()
    for copy in copies:
        copy.wait_send()


def cut(rows, orders):
    step = 16
    units = rows // step
    base, extra = divmod(units, len(orders))
    pieces, at = [], 0
    for i, order in enumerate(orders):
        size = (base + (1 if i < extra else 0)) * step
        if size:
            pieces.append((at, size, order))
        at += size
    return pieces


def seq_gather(x, collective_id, name):
    rows, cols = x.shape
    pieces = cut(rows, ("xzy", "zyx", "yxz"))
    n = 9 * len(pieces)
    return pl.pallas_call(
        functools.partial(gather_kernel, pieces),
        out_shape=jax.ShapeDtypeStruct((2, 4, 4, rows, cols), x.dtype),
        in_specs=[ANY],
        out_specs=ANY,
        scratch_shapes=[
            pltpu.SemaphoreType.DMA((n,)),
            pltpu.SemaphoreType.DMA((n,)),
            pltpu.SemaphoreType.DMA,
        ],
        compiler_params=pltpu.CompilerParams(
            collective_id=collective_id, has_side_effects=True, vmem_limit_bytes=1 << 20
        ),
        name=name,
    )(x).reshape(32, rows, cols)


def scatter_kernel(pieces, x_ref, o_ref, send, recv, *bufs):
    section = lax.axis_index("section")
    me = seq_coords()
    greet(axis_peers(section, me))
    arrived = [bufs[3 * i : 3 * i + 3] for i in range(len(pieces))]
    partial = [bufs[3 * len(pieces) + 2 * i :][:2] for i in range(len(pieces))]
    copies, latest = [], {}

    def source(phase, i):
        lo, size, order = pieces[i]
        if phase == 0:
            return x_ref, (pl.ds(lo, size),)
        return partial[i][phase - 1], ()

    def block(phase, i, coord):
        lo, size, order = pieces[i]
        left = [a for a in AXES if a not in order[:phase]]
        ref, tail = source(phase, i)
        return ref.at[tuple(coord if a == order[phase] else slice(None) for a in left) + tail]

    def launch(phase, i):
        order = pieces[i][2]
        axis = order[phase]
        latest[i] = []
        for d in range(1, SIZES[axis]):
            at = (i * 3 + phase) * 3 + d - 1
            coord = lax.rem(me[AXES.index(axis)] + d, SIZES[axis])
            copy = pltpu.make_async_remote_copy(
                src_ref=block(phase, i, coord),
                dst_ref=arrived[i][phase].at[d - 1],
                send_sem=send.at[at],
                recv_sem=recv.at[at],
                device_id=peer(section, me, axis, d),
                device_id_type=MESH,
            )
            copy.start()
            latest[i].append(copy)
        copies.extend(latest[i])

    def total(phase, i):
        lo, size, order = pieces[i]
        axis = order[phase]
        for copy in latest[i]:
            copy.wait_recv()
        mine = block(phase, i, me[AXES.index(axis)])
        inbox = arrived[i][phase]
        left = [SIZES[a] for a in AXES if a not in order[: phase + 1]]
        count = 1
        for extent in left:
            count *= extent

        def add(k, carry):
            at = (k // left[1], k % left[1]) if len(left) == 2 else ((k,) if left else ())
            whole = mine[at].astype(jnp.float32) if at else mine[...].astype(jnp.float32)
            for d in range(SIZES[axis] - 1):
                whole = whole + inbox[(d,) + at].astype(jnp.float32)
            if phase == 2:
                o_ref[pl.ds(lo, size), :] = whole.astype(o_ref.dtype)
            else:
                partial[i][phase][at] = whole.astype(jnp.bfloat16)
            return carry

        if count == 1:
            add(0, 0)
        else:
            lax.fori_loop(0, count, add, 0)

    for i in range(len(pieces)):
        launch(0, i)
    for phase in range(3):
        for i in range(len(pieces)):
            total(phase, i)
            if phase < 2:
                launch(phase + 1, i)
    for copy in copies:
        copy.wait_send()


def seq_scatter(x, out_dtype, collective_id, name):
    _, rows, cols = x.shape
    pieces = cut(rows, ("yzx", "xyz", "zxy"))
    n = 9 * len(pieces)
    inboxes, partials = [], []
    for lo, size, order in pieces:
        for phase in range(3):
            left = [SIZES[a] for a in AXES if a not in order[: phase + 1]]
            inboxes.append(pltpu.VMEM((SIZES[order[phase]] - 1, *left, size, cols), jnp.bfloat16))
            if phase < 2:
                partials.append(pltpu.VMEM((*left, size, cols), jnp.bfloat16))
    return pl.pallas_call(
        functools.partial(scatter_kernel, pieces),
        out_shape=jax.ShapeDtypeStruct((rows, cols), out_dtype),
        in_specs=[VMEM],
        out_specs=VMEM,
        scratch_shapes=[
            pltpu.SemaphoreType.DMA((n,)),
            pltpu.SemaphoreType.DMA((n,)),
            *inboxes,
            *partials,
        ],
        compiler_params=pltpu.CompilerParams(
            collective_id=collective_id, has_side_effects=True, vmem_limit_bytes=40 << 20
        ),
        name=name,
    )(x.reshape(2, 4, 4, rows, cols))


def exchange_kernel(axis, count, apart, x_ref, o_ref, send, recv, local):
    me = lax.axis_index(axis)
    others = [lax.rem(me + d, count) for d in range(1, count)]
    device = lambda k: (
        (lax.axis_index("section"), k) if axis == "seq" else (k, lax.axis_index("seq"))
    )
    greet([device(k) for k in others])
    own = pltpu.make_async_copy(x_ref.at[me] if apart else x_ref, o_ref.at[me], local)
    own.start()
    copies = []
    for d, k in enumerate(others):
        copy = pltpu.make_async_remote_copy(
            src_ref=x_ref.at[k] if apart else x_ref,
            dst_ref=o_ref.at[me],
            send_sem=send.at[d],
            recv_sem=recv.at[d],
            device_id=device(k),
            device_id_type=MESH,
        )
        copy.start()
        copies.append(copy)
    own.wait()
    for copy in copies:
        copy.wait()


def exchange(x, axis, count, apart, collective_id, name):
    shape = x.shape[1:] if apart else x.shape
    return pl.pallas_call(
        functools.partial(exchange_kernel, axis, count, apart),
        out_shape=jax.ShapeDtypeStruct((count, *shape), x.dtype),
        in_specs=[ANY],
        out_specs=ANY,
        scratch_shapes=[
            pltpu.SemaphoreType.DMA((count - 1,)),
            pltpu.SemaphoreType.DMA((count - 1,)),
            pltpu.SemaphoreType.DMA,
        ],
        compiler_params=pltpu.CompilerParams(
            collective_id=collective_id, has_side_effects=True, vmem_limit_bytes=1 << 20
        ),
        name=name,
    )(x)


def contract(left, right, l, r):
    return lax.dot_general(
        left, right, (((l,), (r,)), ((), ())), preferred_element_type=jnp.float32
    )


def head_rows(ref):
    return jnp.concatenate([ref[:, h * HD : (h + 1) * HD] for h in range(HEADS_HERE)], axis=0)


def key_block(kv_ref, g, cols, context_rows):
    slots = kv_ref.shape[1] - context_rows
    context = kv_ref[pl.ds(g * GROUP, GROUP), :context_rows, cols]
    memory = kv_ref[pl.ds(g * GROUP, GROUP), context_rows:, cols]
    return jnp.concatenate(
        [context.reshape(GROUP * context_rows, HD), memory.reshape(GROUP * slots, HD)], axis=0
    )


def seen(g, rows_ref, context_rows, slots):
    token = g * (GROUP * context_rows) + lax.broadcasted_iota(
        jnp.int32, (GROUP * context_rows, ROWS), 0
    )
    slot = g * (GROUP * slots) + lax.broadcasted_iota(jnp.int32, (GROUP * slots, ROWS), 0)
    context = (token >= rows_ref[0:1, :]) & (token < rows_ref[1:2, :])
    memory = (slot >= rows_ref[2:3, :]) & (slot <= rows_ref[3:4, :])
    return context, memory


def attend_kernel(context_rows, span, rows_ref, q_ref, kv_ref, o_ref, ot_ref, top_ref, mass_ref):
    slots = kv_ref.shape[1] - context_rows
    edge = GROUP * context_rows
    q = head_rows(q_ref)
    ot_ref[...] = jnp.zeros_like(ot_ref)
    top_ref[...] = jnp.full_like(top_ref, mask_fill)
    mass_ref[...] = jnp.zeros_like(mass_ref)

    def step(g, carry):
        scores = contract(key_block(kv_ref, g, slice(0, HD), context_rows), q, 1, 1)
        context, memory = seen(g, rows_ref, context_rows, slots)
        scores = jnp.concatenate(
            [
                jnp.where(context, scores[:edge], mask_fill),
                jnp.where(memory, scores[edge:], mask_fill),
            ],
            axis=0,
        )
        before = top_ref[0:1, :]
        top = jnp.maximum(before, jnp.max(scores, axis=0, keepdims=True))
        keep = jnp.exp2((before - top) * exp2_scale)
        weight = jnp.exp2((scores - top) * exp2_scale)
        top_ref[0:1, :] = top
        mass_ref[0:1, :] = mass_ref[0:1, :] * keep + jnp.sum(weight, axis=0, keepdims=True)
        values = key_block(kv_ref, g, slice(HD, 2 * HD), context_rows)
        ot_ref[...] = ot_ref[...] * keep + contract(values, weight.astype(jnp.bfloat16), 0, 0)
        return carry

    lax.fori_loop(span[0], span[1], step, 0)
    ot_ref[...] = ot_ref[...] / mass_ref[0:1, :]
    rows = jnp.transpose(ot_ref[...]).astype(jnp.bfloat16)
    here = q_ref.shape[0]
    for h in range(HEADS_HERE):
        o_ref[:, h * HD : (h + 1) * HD] = rows[h * here : (h + 1) * here]


def backward_kernel(
    context_rows, span, rows_ref, q_ref, g_ref, kv_ref, ot_ref, top_ref, mass_ref, dq_ref, dv_ref, acc
):
    slots = kv_ref.shape[1] - context_rows
    edge = GROUP * context_rows
    q = head_rows(q_ref)
    grad = head_rows(g_ref)
    center = jnp.sum(jnp.transpose(grad.astype(jnp.float32)) * ot_ref[...], axis=0, keepdims=True)
    top = top_ref[0:1, :]
    share = 1.0 / mass_ref[0:1, :]
    acc[...] = jnp.zeros_like(acc)
    dv_ref[...] = jnp.zeros_like(dv_ref)

    def step(g, carry):
        keys = key_block(kv_ref, g, slice(0, HD), context_rows)
        scores = contract(keys, q, 1, 1)
        context, memory = seen(g, rows_ref, context_rows, slots)
        probs = jnp.exp2((scores - top) * exp2_scale) * share
        probs = jnp.concatenate(
            [jnp.where(context, probs[:edge], 0.0), jnp.where(memory, probs[edge:], 0.0)], axis=0
        )
        values = key_block(kv_ref, g, slice(HD, 2 * HD), context_rows)
        d_probs = contract(values, grad, 1, 1)
        d_scores = (probs * (d_probs - center)).astype(jnp.bfloat16)
        d_values = contract(probs.astype(jnp.bfloat16), grad, 1, 0).astype(jnp.bfloat16)
        dv_ref[pl.ds(g * GROUP, GROUP), :context_rows, :] = d_values[:edge].reshape(
            GROUP, context_rows, HD
        )
        dv_ref[pl.ds(g * GROUP, GROUP), context_rows:, :] = d_values[edge:].reshape(
            GROUP, slots, HD
        )
        acc[...] += contract(keys, d_scores, 0, 0)
        return carry

    lax.fori_loop(span[0], span[1], step, 0)
    rows = jnp.transpose(acc[...] * score_scale).astype(jnp.bfloat16)
    here = q_ref.shape[0]
    for h in range(HEADS_HERE):
        dq_ref[:, h * HD : (h + 1) * HD] = rows[h * here : (h + 1) * here]


SMEM = pl.BlockSpec(memory_space=pltpu.SMEM)
BIG = pltpu.CompilerParams(vmem_limit_bytes=48 << 20)


def attend(span, rows, q, kv, context_rows):
    f32 = jnp.float32
    return pl.pallas_call(
        functools.partial(attend_kernel, context_rows),
        out_shape=(
            jax.ShapeDtypeStruct(q.shape, jnp.bfloat16),
            jax.ShapeDtypeStruct((HD, ROWS), f32),
            jax.ShapeDtypeStruct((8, ROWS), f32),
            jax.ShapeDtypeStruct((8, ROWS), f32),
        ),
        in_specs=[SMEM, VMEM, VMEM, VMEM],
        out_specs=(VMEM, VMEM, VMEM, VMEM),
        compiler_params=BIG,
        name="attend",
    )(span, rows, q, kv)


def attend_backward(span, rows, q, grad, kv, ot, top, mass, context_rows):
    return pl.pallas_call(
        functools.partial(backward_kernel, context_rows),
        out_shape=(
            jax.ShapeDtypeStruct(q.shape, jnp.bfloat16),
            jax.ShapeDtypeStruct((*kv.shape[:2], HD), jnp.bfloat16),
        ),
        in_specs=[SMEM] + [VMEM] * 7,
        out_specs=(VMEM, VMEM),
        scratch_shapes=[pltpu.VMEM((HD, ROWS), jnp.float32)],
        compiler_params=BIG,
        name="attend_backward",
    )(span, rows, q, grad, kv, ot, top, mass)


def row_bounds(document_slots, first, slot_dev, seq_size):
    docs = document_slots.shape[0]
    order = jnp.arange(docs, dtype=jnp.int32)
    ends = jnp.sum(jnp.where(order[None, :] <= order[:, None], document_slots[None, :], 0), axis=1)
    slot = first + jnp.arange(slot_dev, dtype=jnp.int32)
    passed = ends[None, :] <= slot[:, None]
    low = jnp.max(jnp.where(passed, ends[None, :], 0), axis=1)
    high = jnp.min(jnp.where(passed, slot_dev * seq_size, ends[None, :]), axis=1)
    one = jnp.stack([4 * low, 4 * high, low, slot] + [slot] * 4).astype(jnp.int32)
    unit = GROUP * slot_dev
    span = jnp.stack([jnp.min(low) // unit, (jnp.max(high) + unit - 1) // unit])
    return span.astype(jnp.int32), jnp.tile(one, (1, HEADS_HERE))


def body(
    context,
    memory,
    query_weight,
    key_weight,
    value_weight,
    query_down_map,
    query_up_map,
    value_down_map,
    value_up_map,
    output_weight,
    decoder_gain,
    document_slots,
    normed_gradient,
):
    bf16, f32 = jnp.bfloat16, jnp.float32
    tok_dev = context.shape[0]
    slot_dev = memory.shape[0]
    seq_size = lax.axis_size("seq")
    seq_index = lax.axis_index("seq")
    section_extent = lax.axis_size("section")
    section_index = lax.axis_index("section")
    every_row = jnp.concatenate([context, memory], axis=0)
    weights = seq_gather(
        jnp.concatenate([key_weight, value_weight, value_down_map], axis=1), 1, "gather_weights"
    ).reshape(MODEL_DIM, 3 * HD)
    projected = jnp.dot(every_row, weights, preferred_element_type=f32)
    query_low = jnp.dot(memory, query_down_map, preferred_element_type=f32).astype(bf16)
    value_low = projected[:, 2 * HD :].astype(bf16)
    queries = (
        jnp.dot(memory, query_weight, preferred_element_type=f32)
        + adapter_scale * jnp.dot(query_low, query_up_map, preferred_element_type=f32)
    ).astype(bf16)
    keys = projected[:, :HD].astype(bf16)
    values = (
        projected[:, HD : 2 * HD]
        + adapter_scale * jnp.dot(value_low, value_up_map, preferred_element_type=f32)
    ).astype(bf16)
    kv = seq_gather(jnp.concatenate([keys, values], axis=1), 2, "gather_keys")
    span, rows = row_bounds(document_slots, seq_index * slot_dev, slot_dev, seq_size)
    attended, ot, top, mass = attend(span, rows, queries, kv, tok_dev)
    slots_all = seq_gather(attended, 3, "gather_attended").reshape(seq_size * slot_dev, -1)
    hidden_part = jnp.dot(slots_all, output_weight, preferred_element_type=f32).astype(bf16)
    pieces = exchange(
        hidden_part.reshape(section_extent, -1, hidden_part.shape[1]),
        "section", 4, True, 4, "sum_hidden",
    )
    hidden = jnp.sum(pieces.astype(f32), axis=0)
    total_slots = slot_dev * seq_size
    weighted = total_slots ** (-0.5) * normed_gradient.astype(f32) * decoder_gain[None, :]
    stats = jnp.stack([jnp.sum(hidden * hidden, axis=1), jnp.sum(weighted * hidden, axis=1)])
    stats = jnp.sum(
        exchange(stats.reshape(8, 128), "seq", 32, False, 5, "sum_stats"), axis=0
    ).reshape(2, -1)
    square_sum, cross_sum = stats[0], stats[1]
    inv_rms = lax.rsqrt(square_sum / MODEL_DIM + epsilon)
    normed = (hidden * inv_rms[:, None] * decoder_gain[None, :]).astype(bf16)
    d_hidden = (
        inv_rms[:, None] * weighted - hidden * (inv_rms**3 * cross_sum / MODEL_DIM)[:, None]
    ).astype(bf16)
    grads_all = exchange(d_hidden, "section", 4, False, 6, "gather_grads").reshape(
        total_slots, -1
    )
    d_part = contract(grads_all, output_weight, 1, 1).astype(bf16)
    d_attended = seq_scatter(
        d_part.reshape(seq_size, slot_dev, -1), bf16, 7, "scatter_attended"
    )
    d_queries, dv_part = attend_backward(
        span, rows, queries, d_attended, kv, ot, top, mass, tok_dev
    )
    d_values = seq_scatter(dv_part, bf16, 8, "scatter_values")
    query_up_part = adapter_scale * contract(query_low, d_queries, 0, 0)
    value_up_part = adapter_scale * contract(value_low, d_values, 0, 0)
    query_part = adapter_scale * contract(d_queries, query_up_map, 1, 1)
    value_part = adapter_scale * contract(d_values, value_up_map, 1, 1)
    backs = jnp.sum(
        exchange(
            jnp.concatenate([query_part, value_part], axis=0), "section", 4, False, 9, "sum_backs"
        ),
        axis=0,
    ).astype(bf16)
    width = memory.shape[1] // section_extent
    memory_cols = lax.dynamic_slice_in_dim(memory, section_index * width, width, 1)
    row_cols = lax.dynamic_slice_in_dim(every_row, section_index * width, width, 1)
    down_parts = [
        contract(memory_cols, backs[:slot_dev], 0, 0),
        contract(row_cols, backs[slot_dev:], 0, 0),
    ]
    ups = jnp.concatenate([query_up_part, value_up_part], axis=1)
    lanes = ups.shape[1] // 128
    ups = jnp.moveaxis(ups.reshape(128, lanes, 128), 1, 0).reshape(seq_size, -1, 128)
    up_rows = ups.shape[1]
    final_parts = jnp.concatenate(
        [part.reshape(seq_size, -1, 128).astype(bf16) for part in down_parts]
        + [jnp.pad(ups.astype(bf16), ((0, 0), (0, -up_rows % 16), (0, 0)))],
        axis=1,
    )
    final = seq_scatter(final_parts, f32, 10, "scatter_final")
    down_rows = MODEL_DIM // section_extent // seq_size
    grad_qa, grad_va = final[:down_rows], final[down_rows : 2 * down_rows]
    ups = exchange(final[2 * down_rows :], "seq", 32, False, 11, "gather_ups")[:, :up_rows]
    ups = jnp.moveaxis(ups.reshape(lanes, 128, 128), 0, 1).reshape(128, lanes * 128)
    split = query_up_part.shape[1]
    return (normed, grad_qa, grad_va, ups[:, :split], ups[:, split:])


def solution(mesh):
    in_specs = (
        P("seq", None),
        P("seq", None),
        P(None, "section"),
        P("seq", "section"),
        P("seq", "section"),
        P(),
        P(None, "section"),
        P("seq", None),
        P(None, "section"),
        P("section", "seq"),
        P("seq"),
        P(),
        P("section", "seq"),
    )
    out_specs = (
        P("section", "seq"),
        P(("section", "seq"), None),
        P(("section", "seq"), None),
        P(None, "section"),
        P(None, "section"),
    )
    return jax.shard_map(body, mesh=mesh, in_specs=in_specs, out_specs=out_specs, check_vma=False)
```

```python
import functools

import jax
import jax.numpy as jnp
from jax import lax
from jax.experimental import pallas as pl
from jax.experimental.pallas import tpu as pltpu
from jax.sharding import PartitionSpec as P

MODEL_DIM = 8192
HEADS_HERE = 8
HD = 128
ROWS = 512
GROUP = 2

adapter_scale = 0.25
epsilon = 1e-05
mask_fill = -1e30
score_scale = HD ** (-0.5)
exp2_scale = score_scale * 1.4426950408889634

MESH = pl.DeviceIdType.MESH
ANY = pl.BlockSpec(memory_space=pl.ANY)
VMEM = pl.BlockSpec(memory_space=pltpu.VMEM)
HBM = pl.BlockSpec(memory_space=pltpu.HBM)

SIZES = {"y": 2, "z": 4, "x": 4, "h": 2, "c": 2}
PLAIN, PAIRED = "yzx", "yzhc"


def coords(axes):
    seq, section = lax.axis_index("seq"), lax.axis_index("section")
    here = {"y": seq // 16, "z": (seq // 4) % 4, "x": seq % 4, "m": section // 2, "c": section % 2}
    here["h"], here["l"] = here["x"] // 2, here["x"] % 2
    return here


def device_at(axes, here):
    x = here["x"] if "x" in axes else here["h"] * 2 + here["l"]
    return (here["m"] * 2 + here["c"], here["y"] * 16 + here["z"] * 4 + x)


def moved(here, axis, step):
    return {**here, axis: lax.rem(here[axis] + step, SIZES[axis])}


def greet(devices, here=None):
    barrier = pltpu.get_barrier_semaphore()
    for device in devices:
        pl.semaphore_signal(barrier, inc=1, device_id=device, device_id_type=MESH)
    if here is not None:

        @pl.when(here["c"] != here["l"])
        def _():
            pl.semaphore_signal(
                barrier, inc=1, device_id=swap_device(here), device_id_type=MESH
            )

    extra = 0 if here is None else lax.rem(here["c"] + here["l"], 2)
    pl.semaphore_wait(barrier, len(devices) + extra)


def swap_device(here):
    return device_at("h", {**here, "c": here["l"], "l": here["c"]})


class Swap:
    def __init__(self, here, source, target, send, recv, local):
        self.apart = here["c"] != here["l"]
        self.there = lambda: pltpu.make_async_remote_copy(
            src_ref=source,
            dst_ref=target,
            send_sem=send,
            recv_sem=recv,
            device_id=swap_device(here),
            device_id_type=MESH,
        )
        self.stays = lambda: pltpu.make_async_copy(source, target, local)

    def start(self):
        @pl.when(self.apart)
        def _():
            self.there().start()

        @pl.when(jnp.logical_not(self.apart))
        def _():
            self.stays().start()

    def wait(self):
        @pl.when(self.apart)
        def _():
            self.there().wait()

        @pl.when(jnp.logical_not(self.apart))
        def _():
            self.stays().wait()


def axis_peers(axes, here):
    return [device_at(axes, moved(here, a, d)) for a in axes for d in range(1, SIZES[a])]


def remote(source, target, send, recv, device):
    copy = pltpu.make_async_remote_copy(
        src_ref=source,
        dst_ref=target,
        send_sem=send,
        recv_sem=recv,
        device_id=device,
        device_id_type=MESH,
    )
    copy.start()
    return copy


class Gather:
    def __init__(self, here, axes, pieces, source, target, sems, base):
        self.here, self.axes, self.pieces, self.base = here, axes, pieces, base
        self.source, self.target = source, target
        self.send, self.recv, self.fore, self.back = sems
        self.place = tuple(here[a] for a in axes)
        self.paired = "c" in axes
        self.partner = device_at(axes, moved(here, "c", 1)) if self.paired else None
        self.copies, self.latest, self.passed = [], {}, []

    def at(self, phase, i, d):
        return self.base + (i * 3 + phase) * 3 + d

    def begin(self):
        if self.paired:
            own = self.target.at[self.place]
            sem = self.base + 9 * len(self.pieces)
            self.passed.append(
                remote(
                    own if self.source is None else self.source,
                    own,
                    self.fore.at[sem],
                    self.back.at[sem],
                    self.partner,
                )
            )

    def arrived(self, phase, i):
        lo, size, order = self.pieces[i]
        axis = order[phase]
        for d, copy in enumerate(self.latest[i]):
            copy.wait_recv()
            if self.paired:
                came = {**self.here, axis: lax.rem(self.here[axis] + SIZES[axis] - d - 1, SIZES[axis])}
                region = self.target.at[
                    tuple(slice(None) if a in order[:phase] else came[a] for a in self.axes)
                    + (pl.ds(lo, size),)
                ]
                at = self.at(phase, i, d)
                self.passed.append(
                    remote(region, region, self.fore.at[at], self.back.at[at], self.partner)
                )

    def launch(self, phase, i):
        lo, size, order = self.pieces[i]
        held = tuple(slice(None) if a in order[:phase] else self.here[a] for a in self.axes)
        region = self.target.at[held + (pl.ds(lo, size),)]
        source = region if phase or self.source is None else self.source.at[pl.ds(lo, size)]
        self.latest[i] = []
        for d in range(1, SIZES[order[phase]]):
            at = self.at(phase, i, d - 1)
            device = device_at(self.axes, moved(self.here, order[phase], d))
            self.latest[i].append(remote(source, region, self.send.at[at], self.recv.at[at], device))
        self.copies += self.latest[i]

    def finish(self):
        for i in range(len(self.pieces)):
            self.arrived(2, i)
        for copy in self.passed:
            copy.wait_recv()
        for copy in self.copies + self.passed:
            copy.wait_send()


def run_gathers(gathers, owns, between):
    for gather in gathers:
        gather.begin()
    for phase in range(3):
        for gather in gathers:
            for i in range(len(gather.pieces)):
                if phase:
                    gather.arrived(phase - 1, i)
                    if phase == 1:
                        while owns:
                            owns.pop().wait()
                gather.launch(phase, i)
        between(phase)
    for gather in gathers:
        gather.finish()


def semaphores(count):
    return [pltpu.SemaphoreType.DMA((count,)) for _ in range(4)]


def opening_kernel(
    pieces, half_pieces, kv_ref, down_ref, memory_ref, weight_ref, wo_ref, ng_ref, gain_ref,
    kv_all, down_all, acc_ref, wo_out, ng_out, gain_out,
    send, recv, fore, back, buffer, loads, local, swap_send, swap_recv, swap_local,
):
    here = coords(PLAIN)
    depth = buffer.shape[1]
    count = weight_ref.shape[0] // depth

    def load(k):
        return pltpu.make_async_copy(
            weight_ref.at[pl.ds(k * depth, depth)], buffer.at[k % 3], loads.at[k % 3]
        )

    for k in range(2):
        load(k).start()
    greet(axis_peers(PLAIN + "c", here), here)
    swaps = [
        Swap(here, a, b, swap_send.at[i], swap_recv.at[i], swap_local.at[i])
        for i, (a, b) in enumerate(((wo_ref, wo_out), (ng_ref, ng_out), (gain_ref, gain_out)))
    ]
    half = down_ref.shape[0] // 2
    own_half = down_ref.at[pl.ds(here["c"] * half, half)]
    sems = (send, recv, fore, back)
    plain = Gather(here, PLAIN, pieces, kv_ref, kv_all, sems, 0)
    shared = Gather(
        here, PLAIN + "c", half_pieces, own_half, down_all, sems, 9 * len(pieces) + 1
    )
    owns = [
        pltpu.make_async_copy(kv_ref, kv_all.at[plain.place], local.at[0]),
        pltpu.make_async_copy(own_half, down_all.at[shared.place], local.at[1]),
    ]
    for own in owns:
        own.start()
    acc_ref[...] = jnp.zeros_like(acc_ref)

    def between(phase):
        if phase == 0:
            for swap in swaps:
                swap.start()
        edges = (0, count // 4, count // 2 + count // 8, count)
        for k in range(edges[phase], edges[phase + 1]):
            load(k).wait()
            if k + 2 < count:
                load(k + 2).start()
            acc_ref[...] += jnp.dot(
                memory_ref[:, k * depth : (k + 1) * depth],
                buffer[k % 3],
                preferred_element_type=jnp.float32,
            )

    run_gathers([plain, shared], owns, between)
    for swap in swaps:
        swap.wait()


def opening(kv_weight, down, memory, query_weight, output_weight, normed_gradient, gain, collective_id):
    rows, cols = kv_weight.shape
    half = down.shape[0] // 2
    pieces = cut(rows, ("xzy", "zyx", "yxz"))
    half_pieces = cut(half, ("xzy", "zyx", "yxz"))
    n = 9 * len(pieces) + 1 + 9 * len(half_pieces) + 1
    like = lambda a: jax.ShapeDtypeStruct(a.shape, a.dtype)
    outs = pl.pallas_call(
        functools.partial(opening_kernel, pieces, half_pieces),
        out_shape=(
            jax.ShapeDtypeStruct((2, 4, 4, rows, cols), kv_weight.dtype),
            jax.ShapeDtypeStruct((2, 4, 4, 2, half, down.shape[1]), down.dtype),
            jax.ShapeDtypeStruct((memory.shape[0], query_weight.shape[1]), jnp.float32),
            like(output_weight),
            like(normed_gradient),
            like(gain),
        ),
        in_specs=[ANY, ANY, VMEM, HBM, ANY, ANY, ANY],
        out_specs=(ANY, ANY, VMEM, ANY, ANY, ANY),
        scratch_shapes=semaphores(n)
        + [
            pltpu.VMEM((3, 1024, query_weight.shape[1]), jnp.bfloat16),
            pltpu.SemaphoreType.DMA((3,)),
            pltpu.SemaphoreType.DMA((2,)),
            pltpu.SemaphoreType.DMA((3,)),
            pltpu.SemaphoreType.DMA((3,)),
            pltpu.SemaphoreType.DMA((3,)),
        ],
        compiler_params=pltpu.CompilerParams(
            collective_id=collective_id, has_side_effects=True, vmem_limit_bytes=52 << 20
        ),
        name="opening",
    )(kv_weight, down, memory, query_weight, output_weight, normed_gradient, gain)
    return (
        outs[0].reshape(32 * rows, cols),
        outs[1].reshape(32 * 2 * half, down.shape[1]),
        *outs[2:],
    )


def keys_kernel(
    pieces, x_ref, q_ref, o_ref, q_out, send, recv, fore, back, swap_send, swap_recv, swap_local
):
    here = coords(PAIRED)
    greet(axis_peers(PAIRED, here), here)
    home = o_ref.at[here["y"], here["z"], here["h"], here["l"]]
    first = Swap(here, x_ref, home, swap_send.at[0], swap_recv.at[0], swap_local.at[0])
    second = Swap(here, q_ref, q_out, swap_send.at[1], swap_recv.at[1], swap_local.at[1])
    first.start()
    first.wait()
    gather = Gather(here, PAIRED, pieces, None, o_ref, (send, recv, fore, back), 0)
    run_gathers([gather], [], lambda phase: second.start() if phase == 0 else None)
    second.wait()


def gather_keys(x, q, collective_id):
    rows, cols = x.shape
    pieces = cut(rows, ("hzy", "zyh", "yhz"))
    n = 9 * len(pieces) + 1
    sizes = [SIZES[a] for a in PAIRED]
    kv, q_out = pl.pallas_call(
        functools.partial(keys_kernel, pieces),
        out_shape=(
            jax.ShapeDtypeStruct((*sizes, rows, cols), x.dtype),
            jax.ShapeDtypeStruct(q.shape, q.dtype),
        ),
        in_specs=[ANY, ANY],
        out_specs=(ANY, ANY),
        scratch_shapes=semaphores(n) + [pltpu.SemaphoreType.DMA((2,))] * 3,
        compiler_params=pltpu.CompilerParams(
            collective_id=collective_id, has_side_effects=True, vmem_limit_bytes=1 << 20
        ),
        name="gather_keys",
    )(x, q)
    return kv.reshape(32, rows, cols), q_out


def gather_kernel(axes, pieces, x_ref, o_ref, send, recv, fore, back, local):
    here = coords(axes)
    greet(axis_peers(axes, here))
    gather = Gather(here, axes, pieces, x_ref, o_ref, (send, recv, fore, back), 0)
    own = pltpu.make_async_copy(x_ref, o_ref.at[gather.place], local)
    own.start()
    run_gathers([gather], [own], lambda phase: None)


def cut(rows, orders):
    step = 16
    units = rows // step
    base, extra = divmod(units, len(orders))
    pieces, at = [], 0
    for i, order in enumerate(orders):
        size = (base + (1 if i < extra else 0)) * step
        if size:
            pieces.append((at, size, order))
        at += size
    return pieces


def seq_gather(x, axes, collective_id, name):
    rows, cols = x.shape
    pieces = cut(rows, ("xzy", "zyx", "yxz") if axes == PLAIN else ("hzy", "zyh", "yhz"))
    n = 9 * len(pieces)
    sizes = [SIZES[a] for a in axes]
    return pl.pallas_call(
        functools.partial(gather_kernel, axes, pieces),
        out_shape=jax.ShapeDtypeStruct((*sizes, rows, cols), x.dtype),
        in_specs=[ANY],
        out_specs=ANY,
        scratch_shapes=semaphores(n + 1) + [pltpu.SemaphoreType.DMA],
        compiler_params=pltpu.CompilerParams(
            collective_id=collective_id, has_side_effects=True, vmem_limit_bytes=1 << 20
        ),
        name=name,
    )(x).reshape(32, rows, cols)


class Scatter:
    def __init__(self, here, axes, pieces, x_ref, o_ref, send, recv, bufs):
        self.here, self.axes, self.pieces, self.x, self.o = here, axes, pieces, x_ref, o_ref
        self.send, self.recv, self.depth = send, recv, len(axes)
        n, depth = len(pieces), len(axes)
        self.inbox = [bufs[depth * i : depth * (i + 1)] for i in range(n)]
        self.partial = [bufs[depth * n + (depth - 1) * i :][: depth - 1] for i in range(n)]
        self.copies, self.latest = [], {}

    def block(self, phase, i, coord):
        lo, size, order = self.pieces[i]
        left = [a for a in self.axes if a not in order[:phase]]
        ref = self.partial[i][phase - 1] if phase else self.x
        tail = () if phase else (pl.ds(lo, size),)
        return ref.at[tuple(coord if a == order[phase] else slice(None) for a in left) + tail]

    def launch(self, phase, i):
        axis = self.pieces[i][2][phase]
        self.latest[i] = []
        for d in range(1, SIZES[axis]):
            at = (i * self.depth + phase) * 3 + d - 1
            self.latest[i].append(
                remote(
                    self.block(phase, i, lax.rem(self.here[axis] + d, SIZES[axis])),
                    self.inbox[i][phase].at[d - 1],
                    self.send.at[at],
                    self.recv.at[at],
                    device_at(self.axes, moved(self.here, axis, d)),
                )
            )
        self.copies.extend(self.latest[i])

    def total(self, phase, i):
        lo, size, order = self.pieces[i]
        axis = order[phase]
        for copy in self.latest[i]:
            copy.wait_recv()
        mine, inbox = self.block(phase, i, self.here[axis]), self.inbox[i][phase]
        left = [SIZES[a] for a in self.axes if a not in order[: phase + 1]]
        count = 1
        for extent in left:
            count *= extent

        def add(k, carry):
            at = ()
            for extent in reversed(left):
                at, k = (k % extent,) + at, k // extent
            whole = mine[at].astype(jnp.float32) if at else mine[...].astype(jnp.float32)
            for d in range(SIZES[axis] - 1):
                whole = whole + inbox[(d,) + at].astype(jnp.float32)
            if phase == self.depth - 1:
                self.o[pl.ds(lo, size), :] = whole.astype(self.o.dtype)
            else:
                self.partial[i][phase][at] = whole.astype(jnp.bfloat16)
            return carry

        if count == 1:
            add(0, 0)
        else:
            lax.fori_loop(0, count, add, 0)

    def run(self):
        for i in range(len(self.pieces)):
            self.launch(0, i)
        for phase in range(self.depth):
            for i in range(len(self.pieces)):
                self.total(phase, i)
                if phase < self.depth - 1:
                    self.launch(phase + 1, i)
        for copy in self.copies:
            copy.wait_send()


def scatter_plan(rows, cols, axes):
    pieces = cut(rows, ("yzx", "xyz", "zxy") if axes == PLAIN else ("cyzh", "chyz", "czhy"))
    depth = len(axes)
    n = 3 * depth * len(pieces)
    inboxes, partials = [], []
    for lo, size, order in pieces:
        for phase in range(depth):
            left = [SIZES[a] for a in axes if a not in order[: phase + 1]]
            inboxes.append(pltpu.VMEM((SIZES[order[phase]] - 1, *left, size, cols), jnp.bfloat16))
            if phase < depth - 1:
                partials.append(pltpu.VMEM((*left, size, cols), jnp.bfloat16))
    sems = [pltpu.SemaphoreType.DMA((n,)), pltpu.SemaphoreType.DMA((n,))]
    return pieces, sems, inboxes + partials


def scatter_kernel(axes, pieces, x_ref, o_ref, send, recv, *bufs):
    here = coords(axes)
    greet(axis_peers(axes, here))
    Scatter(here, axes, pieces, x_ref, o_ref, send, recv, bufs).run()


def split_axes(x, axes):
    return x.reshape(*[SIZES[a] for a in axes], *x.shape[1:])


def seq_scatter(x, axes, out_dtype, collective_id, name):
    _, rows, cols = x.shape
    pieces, sems, bufs = scatter_plan(rows, cols, axes)
    return pl.pallas_call(
        functools.partial(scatter_kernel, axes, pieces),
        out_shape=jax.ShapeDtypeStruct((rows, cols), out_dtype),
        in_specs=[VMEM],
        out_specs=VMEM,
        scratch_shapes=sems + bufs,
        compiler_params=pltpu.CompilerParams(
            collective_id=collective_id, has_side_effects=True, vmem_limit_bytes=40 << 20
        ),
        name=name,
    )(split_axes(x, axes))


def values_kernel(
    pieces, x_ref, dq_ref, o_ref, dq_out, send, recv, swap_send, swap_recv, swap_local, own, *bufs
):
    here = coords(PAIRED)
    greet(axis_peers(PAIRED, here), here)
    first = Swap(here, dq_ref, dq_out, swap_send.at[0], swap_recv.at[0], swap_local.at[0])
    second = Swap(here, own, o_ref, swap_send.at[1], swap_recv.at[1], swap_local.at[1])
    first.start()
    Scatter(here, PAIRED, pieces, x_ref, own, send, recv, bufs).run()
    second.start()
    first.wait()
    second.wait()


def scatter_values(x, d_queries, collective_id):
    _, rows, cols = x.shape
    pieces, sems, bufs = scatter_plan(rows, cols, PAIRED)
    return pl.pallas_call(
        functools.partial(values_kernel, pieces),
        out_shape=(
            jax.ShapeDtypeStruct((rows, cols), jnp.bfloat16),
            jax.ShapeDtypeStruct(d_queries.shape, d_queries.dtype),
        ),
        in_specs=[VMEM, ANY],
        out_specs=(ANY, ANY),
        scratch_shapes=sems
        + [pltpu.SemaphoreType.DMA((2,))] * 3
        + [pltpu.VMEM((rows, cols), jnp.bfloat16)]
        + bufs,
        compiler_params=pltpu.CompilerParams(
            collective_id=collective_id, has_side_effects=True, vmem_limit_bytes=40 << 20
        ),
        name="scatter_values",
    )(split_axes(x, PAIRED), d_queries)


def final_kernel(
    pieces, spread, down_rows, x_ref, o_ref, up_ref, send, recv, g_send, g_recv, g_fore, g_back, local,
    *bufs,
):
    here = coords(PLAIN)
    greet(axis_peers(PLAIN, here))
    Scatter(here, PLAIN, pieces, x_ref, o_ref, send, recv, bufs).run()
    own = o_ref.at[pl.ds(down_rows, x_ref.shape[-2] - down_rows)]
    gather = Gather(here, PLAIN, spread, own, up_ref, (g_send, g_recv, g_fore, g_back), 0)
    copy = pltpu.make_async_copy(own, up_ref.at[gather.place], local)
    copy.start()
    run_gathers([gather], [copy], lambda phase: None)


def scatter_final(x, down_rows, collective_id):
    _, rows, cols = x.shape
    pieces, sems, bufs = scatter_plan(rows, cols, PLAIN)
    spread = cut(rows - down_rows, ("xzy", "zyx", "yxz"))
    out, ups = pl.pallas_call(
        functools.partial(final_kernel, pieces, spread, down_rows),
        out_shape=(
            jax.ShapeDtypeStruct((rows, cols), jnp.float32),
            jax.ShapeDtypeStruct((2, 4, 4, rows - down_rows, cols), jnp.float32),
        ),
        in_specs=[VMEM],
        out_specs=(VMEM, VMEM),
        scratch_shapes=sems + semaphores(9 * len(spread) + 1) + [pltpu.SemaphoreType.DMA] + bufs,
        compiler_params=pltpu.CompilerParams(
            collective_id=collective_id, has_side_effects=True, vmem_limit_bytes=40 << 20
        ),
        name="scatter_final",
    )(split_axes(x, PLAIN))
    return out[:down_rows], ups.reshape(32, rows - down_rows, cols)


def stats_kernel(x_ref, o_ref, near_ref, far_ref, send, recv):
    here = coords(PAIRED)
    near = [{**here, "h": (here["h"] + a) % 2, "c": (here["c"] + b) % 2} for a, b in ((0, 1), (1, 0), (1, 1))]
    far = [
        {**here, "y": (here["y"] + a) % 2, "z": (here["z"] + b) % 4}
        for a in range(2)
        for b in range(4)
        if a or b
    ]
    greet([device_at(PAIRED, place) for place in near + far])
    total = x_ref[...]
    o_ref[...] = total
    at = 0
    for places, inbox in ((near, near_ref), (far, far_ref)):
        copies = [
            remote(o_ref, inbox.at[k], send.at[at + k], recv.at[at + k], device_at(PAIRED, place))
            for k, place in enumerate(places)
        ]
        at += len(places)
        for copy in copies:
            copy.wait()
        for k in range(len(places)):
            total = total + inbox[k]
        o_ref[...] = total


def sum_stats(x, collective_id):
    return pl.pallas_call(
        stats_kernel,
        out_shape=jax.ShapeDtypeStruct(x.shape, x.dtype),
        in_specs=[VMEM],
        out_specs=VMEM,
        scratch_shapes=[
            pltpu.VMEM((3, *x.shape), x.dtype),
            pltpu.VMEM((7, *x.shape), x.dtype),
            pltpu.SemaphoreType.DMA((10,)),
            pltpu.SemaphoreType.DMA((10,)),
        ],
        compiler_params=pltpu.CompilerParams(
            collective_id=collective_id, has_side_effects=True, vmem_limit_bytes=4 << 20
        ),
        name="sum_stats",
    )(x)


def grads_kernel(x_ref, normed_ref, o_ref, normed_out, send, recv, local, swap_send, swap_recv, swap_local):
    here = coords(PAIRED)
    me, device = group_place("paired section", here)
    others = [lax.rem(me + d, 4) for d in range(1, 4)]
    greet([device(k) for k in others], here)
    own = pltpu.make_async_copy(x_ref, o_ref.at[me], local)
    own.start()
    copies = [
        remote(x_ref, o_ref.at[me], send.at[d], recv.at[d], device(k)) for d, k in enumerate(others)
    ]
    swap = Swap(here, normed_ref, normed_out, swap_send, swap_recv, swap_local)
    swap.start()
    own.wait()
    for copy in copies:
        copy.wait()
    swap.wait()


def gather_grads(x, normed, collective_id):
    return pl.pallas_call(
        grads_kernel,
        out_shape=(
            jax.ShapeDtypeStruct((4, *x.shape), x.dtype),
            jax.ShapeDtypeStruct(normed.shape, normed.dtype),
        ),
        in_specs=[ANY, ANY],
        out_specs=(ANY, ANY),
        scratch_shapes=[pltpu.SemaphoreType.DMA((3,))] * 2 + [pltpu.SemaphoreType.DMA] * 4,
        compiler_params=pltpu.CompilerParams(
            collective_id=collective_id, has_side_effects=True, vmem_limit_bytes=1 << 20
        ),
        name="gather_grads",
    )(x, normed)


def group_place(group, here):
    if group == "section":
        return here["m"] * 2 + here["c"], lambda k: device_at("x", {**here, "m": k // 2, "c": k % 2})
    return here["m"] * 2 + here["l"], lambda k: device_at("h", {**here, "m": k // 2, "l": k % 2})

def exchange_kernel(group, count, apart, x_ref, o_ref, send, recv, local):
    me, device = group_place(group, coords(PLAIN))
    others = [lax.rem(me + d, count) for d in range(1, count)]
    greet([device(k) for k in others])
    own = pltpu.make_async_copy(x_ref.at[me] if apart else x_ref, o_ref.at[me], local)
    own.start()
    copies = [
        remote(x_ref.at[k] if apart else x_ref, o_ref.at[me], send.at[d], recv.at[d], device(k))
        for d, k in enumerate(others)
    ]
    own.wait()
    for copy in copies:
        copy.wait()


def exchange(x, group, apart, collective_id, name):
    count = 4
    shape = x.shape[1:] if apart else x.shape
    return pl.pallas_call(
        functools.partial(exchange_kernel, group, count, apart),
        out_shape=jax.ShapeDtypeStruct((count, *shape), x.dtype),
        in_specs=[ANY],
        out_specs=ANY,
        scratch_shapes=[
            pltpu.SemaphoreType.DMA((count - 1,)),
            pltpu.SemaphoreType.DMA((count - 1,)),
            pltpu.SemaphoreType.DMA,
        ],
        compiler_params=pltpu.CompilerParams(
            collective_id=collective_id, has_side_effects=True, vmem_limit_bytes=1 << 20
        ),
        name=name,
    )(x)


def contract(left, right, l, r):
    return lax.dot_general(
        left, right, (((l,), (r,)), ((), ())), preferred_element_type=jnp.float32
    )


def head_rows(ref):
    return jnp.concatenate([ref[:, h * HD : (h + 1) * HD] for h in range(HEADS_HERE)], axis=0)


def key_block(kv_ref, g, cols, context_rows):
    slots = kv_ref.shape[1] - context_rows
    context = kv_ref[pl.ds(g * GROUP, GROUP), :context_rows, cols]
    memory = kv_ref[pl.ds(g * GROUP, GROUP), context_rows:, cols]
    return jnp.concatenate(
        [context.reshape(GROUP * context_rows, HD), memory.reshape(GROUP * slots, HD)], axis=0
    )


def seen(g, rows_ref, context_rows, slots):
    token = g * (GROUP * context_rows) + lax.broadcasted_iota(
        jnp.int32, (GROUP * context_rows, ROWS), 0
    )
    slot = g * (GROUP * slots) + lax.broadcasted_iota(jnp.int32, (GROUP * slots, ROWS), 0)
    context = (token >= rows_ref[0:1, :]) & (token < rows_ref[1:2, :])
    memory = (slot >= rows_ref[2:3, :]) & (slot <= rows_ref[3:4, :])
    return context, memory


def attend_kernel(context_rows, span, rows_ref, q_ref, kv_ref, o_ref, ot_ref, top_ref, mass_ref):
    slots = kv_ref.shape[1] - context_rows
    edge = GROUP * context_rows
    q = head_rows(q_ref)
    ot_ref[...] = jnp.zeros_like(ot_ref)
    top_ref[...] = jnp.full_like(top_ref, mask_fill)
    mass_ref[...] = jnp.zeros_like(mass_ref)

    def step(g, carry):
        scores = contract(key_block(kv_ref, g, slice(0, HD), context_rows), q, 1, 1)
        context, memory = seen(g, rows_ref, context_rows, slots)
        scores = jnp.concatenate(
            [
                jnp.where(context, scores[:edge], mask_fill),
                jnp.where(memory, scores[edge:], mask_fill),
            ],
            axis=0,
        )
        before = top_ref[0:1, :]
        top = jnp.maximum(before, jnp.max(scores, axis=0, keepdims=True))
        keep = jnp.exp2((before - top) * exp2_scale)
        weight = jnp.exp2((scores - top) * exp2_scale)
        top_ref[0:1, :] = top
        mass_ref[0:1, :] = mass_ref[0:1, :] * keep + jnp.sum(weight, axis=0, keepdims=True)
        values = key_block(kv_ref, g, slice(HD, 2 * HD), context_rows)
        ot_ref[...] = ot_ref[...] * keep + contract(values, weight.astype(jnp.bfloat16), 0, 0)
        return carry

    lax.fori_loop(span[0], span[1], step, 0)
    ot_ref[...] = ot_ref[...] / mass_ref[0:1, :]
    rows = jnp.transpose(ot_ref[...]).astype(jnp.bfloat16)
    here = q_ref.shape[0]
    for h in range(HEADS_HERE):
        o_ref[:, h * HD : (h + 1) * HD] = rows[h * here : (h + 1) * here]


def backward_kernel(
    context_rows, span, rows_ref, q_ref, g_ref, kv_ref, ot_ref, top_ref, mass_ref, dq_ref, dv_ref, acc
):
    slots = kv_ref.shape[1] - context_rows
    edge = GROUP * context_rows
    q = head_rows(q_ref)
    grad = head_rows(g_ref)
    center = jnp.sum(jnp.transpose(grad.astype(jnp.float32)) * ot_ref[...], axis=0, keepdims=True)
    top = top_ref[0:1, :]
    share = 1.0 / mass_ref[0:1, :]
    acc[...] = jnp.zeros_like(acc)
    dv_ref[...] = jnp.zeros_like(dv_ref)

    def step(g, carry):
        keys = key_block(kv_ref, g, slice(0, HD), context_rows)
        scores = contract(keys, q, 1, 1)
        context, memory = seen(g, rows_ref, context_rows, slots)
        probs = jnp.exp2((scores - top) * exp2_scale) * share
        probs = jnp.concatenate(
            [jnp.where(context, probs[:edge], 0.0), jnp.where(memory, probs[edge:], 0.0)], axis=0
        )
        values = key_block(kv_ref, g, slice(HD, 2 * HD), context_rows)
        d_probs = contract(values, grad, 1, 1)
        d_scores = (probs * (d_probs - center)).astype(jnp.bfloat16)
        d_values = contract(probs.astype(jnp.bfloat16), grad, 1, 0).astype(jnp.bfloat16)
        dv_ref[pl.ds(g * GROUP, GROUP), :context_rows, :] = d_values[:edge].reshape(
            GROUP, context_rows, HD
        )
        dv_ref[pl.ds(g * GROUP, GROUP), context_rows:, :] = d_values[edge:].reshape(
            GROUP, slots, HD
        )
        acc[...] += contract(keys, d_scores, 0, 0)
        return carry

    lax.fori_loop(span[0], span[1], step, 0)
    rows = jnp.transpose(acc[...] * score_scale).astype(jnp.bfloat16)
    here = q_ref.shape[0]
    for h in range(HEADS_HERE):
        dq_ref[:, h * HD : (h + 1) * HD] = rows[h * here : (h + 1) * here]


SMEM = pl.BlockSpec(memory_space=pltpu.SMEM)
BIG = pltpu.CompilerParams(vmem_limit_bytes=48 << 20)


def attend(span, rows, q, kv, context_rows):
    f32 = jnp.float32
    return pl.pallas_call(
        functools.partial(attend_kernel, context_rows),
        out_shape=(
            jax.ShapeDtypeStruct(q.shape, jnp.bfloat16),
            jax.ShapeDtypeStruct((HD, ROWS), f32),
            jax.ShapeDtypeStruct((8, ROWS), f32),
            jax.ShapeDtypeStruct((8, ROWS), f32),
        ),
        in_specs=[SMEM, VMEM, VMEM, VMEM],
        out_specs=(VMEM, VMEM, VMEM, VMEM),
        compiler_params=BIG,
        name="attend",
    )(span, rows, q, kv)


def attend_backward(span, rows, q, grad, kv, ot, top, mass, context_rows):
    return pl.pallas_call(
        functools.partial(backward_kernel, context_rows),
        out_shape=(
            jax.ShapeDtypeStruct(q.shape, jnp.bfloat16),
            jax.ShapeDtypeStruct((*kv.shape[:2], HD), jnp.bfloat16),
        ),
        in_specs=[SMEM] + [VMEM] * 7,
        out_specs=(VMEM, VMEM),
        scratch_shapes=[pltpu.VMEM((HD, ROWS), jnp.float32)],
        compiler_params=BIG,
        name="attend_backward",
    )(span, rows, q, grad, kv, ot, top, mass)


def row_bounds(document_slots, first, slot_dev, seq_size):
    docs = document_slots.shape[0]
    order = jnp.arange(docs, dtype=jnp.int32)
    ends = jnp.sum(jnp.where(order[None, :] <= order[:, None], document_slots[None, :], 0), axis=1)
    slot = first + jnp.arange(slot_dev, dtype=jnp.int32)
    passed = ends[None, :] <= slot[:, None]
    low = jnp.max(jnp.where(passed, ends[None, :], 0), axis=1)
    high = jnp.min(jnp.where(passed, slot_dev * seq_size, ends[None, :]), axis=1)
    one = jnp.stack([4 * low, 4 * high, low, slot] + [slot] * 4).astype(jnp.int32)
    unit = GROUP * slot_dev
    span = jnp.stack([jnp.min(low) // unit, (jnp.max(high) + unit - 1) // unit])
    return span.astype(jnp.int32), jnp.tile(one, (1, HEADS_HERE))


def body(
    context,
    memory,
    query_weight,
    key_weight,
    value_weight,
    query_down_map,
    query_up_map,
    value_down_map,
    value_up_map,
    output_weight,
    decoder_gain,
    document_slots,
    normed_gradient,
):
    bf16, f32 = jnp.bfloat16, jnp.float32
    tok_dev = context.shape[0]
    slot_dev = memory.shape[0]
    seq_size = lax.axis_size("seq")
    here = coords(PLAIN)
    paired_index = here["y"] * 16 + here["z"] * 4 + here["h"] * 2 + here["c"]
    section_extent = lax.axis_size("section")
    section_index = lax.axis_index("section")
    every_row = jnp.concatenate([context, memory], axis=0)
    kv_weight, down, query_sum, output_weight, normed_gradient, decoder_gain = opening(
        jnp.concatenate([key_weight, value_weight], axis=1),
        value_down_map,
        memory,
        query_weight,
        output_weight,
        normed_gradient,
        decoder_gain.reshape(-1, 128),
        1,
    )
    decoder_gain = decoder_gain.reshape(-1)
    projected = jnp.dot(every_row, kv_weight, preferred_element_type=f32)
    query_low = jnp.dot(memory, query_down_map, preferred_element_type=f32).astype(bf16)
    value_low = jnp.dot(every_row, down, preferred_element_type=f32).astype(bf16)
    queries = (
        query_sum + adapter_scale * jnp.dot(query_low, query_up_map, preferred_element_type=f32)
    ).astype(bf16)
    keys = projected[:, :HD].astype(bf16)
    values = (
        projected[:, HD : 2 * HD]
        + adapter_scale * jnp.dot(value_low, value_up_map, preferred_element_type=f32)
    ).astype(bf16)
    kv, queries_here = gather_keys(jnp.concatenate([keys, values], axis=1), queries, 2)
    span, rows = row_bounds(document_slots, paired_index * slot_dev, slot_dev, seq_size)
    attended, ot, top, mass = attend(span, rows, queries_here, kv, tok_dev)
    slots_all = seq_gather(attended, PAIRED, 3, "gather_attended").reshape(seq_size * slot_dev, -1)
    hidden_part = jnp.dot(slots_all, output_weight, preferred_element_type=f32).astype(bf16)
    pieces = exchange(
        hidden_part.reshape(section_extent, -1, hidden_part.shape[1]),
        "paired section", True, 4, "sum_hidden",
    )
    hidden = jnp.sum(pieces.astype(f32), axis=0)
    total_slots = slot_dev * seq_size
    weighted = total_slots ** (-0.5) * normed_gradient.astype(f32) * decoder_gain[None, :]
    stats = jnp.stack([jnp.sum(hidden * hidden, axis=1), jnp.sum(weighted * hidden, axis=1)])
    stats = sum_stats(stats.reshape(8, 128), 5).reshape(2, -1)
    square_sum, cross_sum = stats[0], stats[1]
    inv_rms = lax.rsqrt(square_sum / MODEL_DIM + epsilon)
    normed = (hidden * inv_rms[:, None] * decoder_gain[None, :]).astype(bf16)
    d_hidden = (
        inv_rms[:, None] * weighted - hidden * (inv_rms**3 * cross_sum / MODEL_DIM)[:, None]
    ).astype(bf16)
    grads_all, normed = gather_grads(d_hidden, normed, 6)
    grads_all = grads_all.reshape(total_slots, -1)
    d_part = contract(grads_all, output_weight, 1, 1).astype(bf16)
    d_attended = seq_scatter(
        d_part.reshape(seq_size, slot_dev, -1), PAIRED, bf16, 7, "scatter_attended"
    )
    d_queries, dv_part = attend_backward(
        span, rows, queries_here, d_attended, kv, ot, top, mass, tok_dev
    )
    d_values, d_queries = scatter_values(dv_part, d_queries, 8)
    query_up_part = adapter_scale * contract(query_low, d_queries, 0, 0)
    value_up_part = adapter_scale * contract(value_low, d_values, 0, 0)
    query_part = adapter_scale * contract(d_queries, query_up_map, 1, 1)
    value_part = adapter_scale * contract(d_values, value_up_map, 1, 1)
    backs = jnp.sum(
        exchange(
            jnp.concatenate([query_part, value_part], axis=0).astype(bf16),
            "section", False, 9, "sum_backs",
        ).astype(f32),
        axis=0,
    ).astype(bf16)
    width = memory.shape[1] // section_extent
    memory_cols = lax.dynamic_slice_in_dim(memory, section_index * width, width, 1)
    row_cols = lax.dynamic_slice_in_dim(every_row, section_index * width, width, 1)
    down_parts = [
        contract(memory_cols, backs[:slot_dev], 0, 0),
        contract(row_cols, backs[slot_dev:], 0, 0),
    ]
    ups = jnp.concatenate([query_up_part, value_up_part], axis=1)
    lanes = ups.shape[1] // 128
    ups = jnp.moveaxis(ups.reshape(128, lanes, 128), 1, 0).reshape(seq_size, -1, 128)
    up_rows = ups.shape[1]
    final_parts = jnp.concatenate(
        [part.reshape(seq_size, -1, 128).astype(bf16) for part in down_parts]
        + [jnp.pad(ups.astype(bf16), ((0, 0), (0, -up_rows % 16), (0, 0)))],
        axis=1,
    )
    down_rows = MODEL_DIM // section_extent // seq_size
    final, ups = scatter_final(final_parts, 2 * down_rows, 10)
    grad_qa, grad_va = final[:down_rows], final[down_rows:]
    ups = ups[:, :up_rows]
    ups = jnp.moveaxis(ups.reshape(lanes, 128, 128), 0, 1).reshape(128, lanes * 128)
    split = query_up_part.shape[1]
    return (normed, grad_qa, grad_va, ups[:, :split], ups[:, split:])


def solution(mesh):
    in_specs = (
        P("seq", None),
        P("seq", None),
        P(None, "section"),
        P("seq", "section"),
        P("seq", "section"),
        P(),
        P(None, "section"),
        P("seq", None),
        P(None, "section"),
        P("section", "seq"),
        P("seq"),
        P(),
        P("section", "seq"),
    )
    out_specs = (
        P("section", "seq"),
        P(("section", "seq"), None),
        P(("section", "seq"), None),
        P(None, "section"),
        P(None, "section"),
    )
    return jax.shard_map(body, mesh=mesh, in_specs=in_specs, out_specs=out_specs, check_vma=False)
```

```python
import functools

import jax
import jax.numpy as jnp
from jax import lax
from jax.experimental import pallas as pl
from jax.experimental.pallas import tpu as pltpu
from jax.sharding import PartitionSpec as P

MODEL_DIM = 8192
HEADS_HERE = 8
HD = 128
ROWS = 512
GROUP = 2

adapter_scale = 0.25
epsilon = 1e-05
mask_fill = -1e30
score_scale = HD ** (-0.5)
exp2_scale = score_scale * 1.4426950408889634

MESH = pl.DeviceIdType.MESH
ANY = pl.BlockSpec(memory_space=pl.ANY)
VMEM = pl.BlockSpec(memory_space=pltpu.VMEM)
HBM = pl.BlockSpec(memory_space=pltpu.HBM)

SIZES = {"y": 2, "z": 4, "x": 4, "h": 2, "c": 2}
PLAIN, PAIRED = "yzx", "yzhc"


def coords(axes):
    seq, section = lax.axis_index("seq"), lax.axis_index("section")
    here = {"y": seq // 16, "z": (seq // 4) % 4, "x": seq % 4, "m": section // 2, "c": section % 2}
    here["h"], here["l"] = here["x"] // 2, here["x"] % 2
    return here


def device_at(axes, here):
    x = here["x"] if "x" in axes else here["h"] * 2 + here["l"]
    return (here["m"] * 2 + here["c"], here["y"] * 16 + here["z"] * 4 + x)


def moved(here, axis, step):
    return {**here, axis: lax.rem(here[axis] + step, SIZES[axis])}


def greet(devices, here=None):
    barrier = pltpu.get_barrier_semaphore()
    for device in devices:
        pl.semaphore_signal(barrier, inc=1, device_id=device, device_id_type=MESH)
    if here is not None:

        @pl.when(here["c"] != here["l"])
        def _():
            pl.semaphore_signal(
                barrier, inc=1, device_id=swap_device(here), device_id_type=MESH
            )

    extra = 0 if here is None else lax.rem(here["c"] + here["l"], 2)
    pl.semaphore_wait(barrier, len(devices) + extra)


def swap_device(here):
    return device_at("h", {**here, "c": here["l"], "l": here["c"]})


class Swap:
    def __init__(self, here, source, target, send, recv, local):
        self.apart = here["c"] != here["l"]
        self.there = lambda: pltpu.make_async_remote_copy(
            src_ref=source,
            dst_ref=target,
            send_sem=send,
            recv_sem=recv,
            device_id=swap_device(here),
            device_id_type=MESH,
        )
        self.stays = lambda: pltpu.make_async_copy(source, target, local)

    def start(self):
        @pl.when(self.apart)
        def _():
            self.there().start()

        @pl.when(jnp.logical_not(self.apart))
        def _():
            self.stays().start()

    def wait(self):
        @pl.when(self.apart)
        def _():
            self.there().wait()

        @pl.when(jnp.logical_not(self.apart))
        def _():
            self.stays().wait()


def axis_peers(axes, here):
    return [device_at(axes, moved(here, a, d)) for a in axes for d in range(1, SIZES[a])]


def remote(source, target, send, recv, device):
    copy = pltpu.make_async_remote_copy(
        src_ref=source,
        dst_ref=target,
        send_sem=send,
        recv_sem=recv,
        device_id=device,
        device_id_type=MESH,
    )
    copy.start()
    return copy


class Gather:
    def __init__(self, here, axes, pieces, source, target, sems, base):
        self.here, self.axes, self.pieces, self.base = here, axes, pieces, base
        self.source, self.target = source, target
        self.send, self.recv, self.fore, self.back = sems
        self.place = tuple(here[a] for a in axes)
        self.paired = "c" in axes
        self.partner = device_at(axes, moved(here, "c", 1)) if self.paired else None
        self.copies, self.latest, self.passed = [], {}, []

    def at(self, phase, i, d):
        return self.base + (i * 3 + phase) * 3 + d

    def begin(self):
        if self.paired:
            own = self.target.at[self.place]
            sem = self.base + 9 * len(self.pieces)
            self.passed.append(
                remote(
                    own if self.source is None else self.source,
                    own,
                    self.fore.at[sem],
                    self.back.at[sem],
                    self.partner,
                )
            )

    def arrived(self, phase, i):
        part, order = self.pieces[i]
        axis = order[phase]
        for d, copy in enumerate(self.latest[i]):
            copy.wait_recv()
            if self.paired:
                came = {**self.here, axis: lax.rem(self.here[axis] + SIZES[axis] - d - 1, SIZES[axis])}
                region = self.target.at[
                    tuple(slice(None) if a in order[:phase] else came[a] for a in self.axes)
                    + part
                ]
                at = self.at(phase, i, d)
                self.passed.append(
                    remote(region, region, self.fore.at[at], self.back.at[at], self.partner)
                )

    def launch(self, phase, i):
        part, order = self.pieces[i]
        held = tuple(slice(None) if a in order[:phase] else self.here[a] for a in self.axes)
        region = self.target.at[held + part]
        source = region if phase or self.source is None else self.source.at[part]
        self.latest[i] = []
        for d in range(1, SIZES[order[phase]]):
            at = self.at(phase, i, d - 1)
            device = device_at(self.axes, moved(self.here, order[phase], d))
            self.latest[i].append(remote(source, region, self.send.at[at], self.recv.at[at], device))
        self.copies += self.latest[i]

    def finish(self):
        for i in range(len(self.pieces)):
            self.arrived(2, i)
        for copy in self.passed:
            copy.wait_recv()
        for copy in self.copies + self.passed:
            copy.wait_send()


def run_gathers(gathers, owns, between):
    for gather in gathers:
        gather.begin()
    for phase in range(3):
        for gather in gathers:
            for i in range(len(gather.pieces)):
                if phase:
                    gather.arrived(phase - 1, i)
                    if phase == 1:
                        while owns:
                            owns.pop().wait()
                gather.launch(phase, i)
        between(phase)
    for gather in gathers:
        gather.finish()


def semaphores(count):
    return [pltpu.SemaphoreType.DMA((count,)) for _ in range(4)]


def opening_kernel(
    pieces, half_pieces, kv_ref, down_ref, memory_ref, weight_ref, wo_ref,
    kv_all, down_all, acc_ref, wo_out,
    send, recv, fore, back, buffer, loads, local, swap_send, swap_recv, swap_local,
):
    here = coords(PLAIN)
    depth = buffer.shape[1]
    count = weight_ref.shape[0] // depth

    def load(k):
        return pltpu.make_async_copy(
            weight_ref.at[pl.ds(k * depth, depth)], buffer.at[k % 3], loads.at[k % 3]
        )

    for k in range(2):
        load(k).start()
    greet(axis_peers(PLAIN + "c", here), here)
    swap = Swap(here, wo_ref, wo_out, swap_send, swap_recv, swap_local)
    half = down_ref.shape[0] // 2
    own_half = down_ref.at[pl.ds(here["c"] * half, half)]
    sems = (send, recv, fore, back)
    plain = Gather(here, PLAIN, pieces, kv_ref, kv_all, sems, 0)
    shared = Gather(
        here, PLAIN + "c", half_pieces, own_half, down_all, sems, 9 * len(pieces) + 1
    )
    owns = [
        pltpu.make_async_copy(kv_ref, kv_all.at[plain.place], local.at[0]),
        pltpu.make_async_copy(own_half, down_all.at[shared.place], local.at[1]),
    ]
    for own in owns:
        own.start()
    acc_ref[...] = jnp.zeros_like(acc_ref)

    def between(phase):
        if phase < 2:
            return
        swap.start()
        for k in range(count):
            load(k).wait()
            if k + 2 < count:
                load(k + 2).start()
            acc_ref[...] += jnp.dot(
                memory_ref[:, k * depth : (k + 1) * depth],
                buffer[k % 3],
                preferred_element_type=jnp.float32,
            )

    run_gathers([plain, shared], owns, between)
    swap.wait()


def opening(kv_weight, down, memory, query_weight, output_weight, collective_id):
    rows, cols = kv_weight.shape
    half = down.shape[0] // 2
    pieces = cut(rows, cols, ORDERS[PLAIN])
    half_pieces = cut(half, down.shape[1], ORDERS[PLAIN])
    n = 9 * len(pieces) + 1 + 9 * len(half_pieces) + 1
    outs = pl.pallas_call(
        functools.partial(opening_kernel, pieces, half_pieces),
        out_shape=(
            jax.ShapeDtypeStruct((2, 4, 4, rows, cols), kv_weight.dtype),
            jax.ShapeDtypeStruct((2, 4, 4, 2, half, down.shape[1]), down.dtype),
            jax.ShapeDtypeStruct((memory.shape[0], query_weight.shape[1]), jnp.float32),
            jax.ShapeDtypeStruct(output_weight.shape, output_weight.dtype),
        ),
        in_specs=[ANY, ANY, VMEM, HBM, ANY],
        out_specs=(ANY, ANY, VMEM, ANY),
        scratch_shapes=semaphores(n)
        + [
            pltpu.VMEM((3, 1024, query_weight.shape[1]), jnp.bfloat16),
            pltpu.SemaphoreType.DMA((3,)),
            pltpu.SemaphoreType.DMA((2,)),
            pltpu.SemaphoreType.DMA,
            pltpu.SemaphoreType.DMA,
            pltpu.SemaphoreType.DMA,
        ],
        compiler_params=pltpu.CompilerParams(
            collective_id=collective_id, has_side_effects=True, vmem_limit_bytes=46 << 20
        ),
        name="opening",
    )(kv_weight, down, memory, query_weight, output_weight)
    return (
        outs[0].reshape(32 * rows, cols),
        outs[1].reshape(32 * 2 * half, down.shape[1]),
        *outs[2:],
    )


def keys_kernel(
    pieces, x_ref, q_ref, ng_ref, gain_ref, o_ref, q_out, ng_out, gain_out,
    send, recv, fore, back, swap_send, swap_recv, swap_local,
):
    here = coords(PAIRED)
    greet(axis_peers(PAIRED, here), here)
    home = o_ref.at[here["y"], here["z"], here["h"], here["l"]]
    ends = ((x_ref, home), (q_ref, q_out), (gain_ref, gain_out), (ng_ref, ng_out))
    swaps = [
        Swap(here, a, b, swap_send.at[i], swap_recv.at[i], swap_local.at[i])
        for i, (a, b) in enumerate(ends)
    ]
    swaps[0].start()
    swaps[0].wait()
    gather = Gather(here, PAIRED, pieces, None, o_ref, (send, recv, fore, back), 0)

    def between(phase):
        if phase == 2:
            for swap in swaps[1:]:
                swap.start()

    run_gathers([gather], [], between)
    for swap in swaps[1:]:
        swap.wait()


def gather_keys(x, q, normed_gradient, gain, collective_id):
    rows, cols = x.shape
    pieces = cut(rows, cols, ORDERS[PAIRED])
    n = 9 * len(pieces) + 1
    sizes = [SIZES[a] for a in PAIRED]
    swapped = [jax.ShapeDtypeStruct(a.shape, a.dtype) for a in (q, normed_gradient, gain)]
    kv, *rest = pl.pallas_call(
        functools.partial(keys_kernel, pieces),
        out_shape=(jax.ShapeDtypeStruct((*sizes, rows, cols), x.dtype), *swapped),
        in_specs=[ANY] * 4,
        out_specs=(ANY,) * 4,
        scratch_shapes=semaphores(n) + [pltpu.SemaphoreType.DMA((4,))] * 3,
        compiler_params=pltpu.CompilerParams(
            collective_id=collective_id, has_side_effects=True, vmem_limit_bytes=1 << 20
        ),
        name="gather_keys",
    )(x, q, normed_gradient, gain)
    return kv.reshape(32, rows, cols), *rest


ORDERS = {
    PLAIN: ("xzy", "zyx", "yxz", "zxy", "yzx", "xyz"),
    PAIRED: ("hzy", "zyh", "yhz", "zhy", "yzh", "hyz"),
}


def cut(rows, cols, orders):
    by_rows = rows // 16 >= 2 * len(orders) or cols == 128
    step = 16 if by_rows else 128
    units = (rows if by_rows else cols) // step
    base, extra = divmod(units, len(orders))
    pieces, at = [], 0
    for i, order in enumerate(orders):
        size = (base + (1 if i < extra else 0)) * step
        if size:
            part = (pl.ds(at, size), pl.ds(0, cols)) if by_rows else (pl.ds(0, rows), pl.ds(at, size))
            pieces.append((part, order))
        at += size
    return pieces


class Scatter:
    def __init__(self, here, axes, pieces, x_ref, o_ref, send, recv, bufs):
        self.here, self.axes, self.pieces, self.x, self.o = here, axes, pieces, x_ref, o_ref
        self.send, self.recv, self.depth = send, recv, len(axes)
        n, depth = len(pieces), len(axes)
        self.inbox = [bufs[depth * i : depth * (i + 1)] for i in range(n)]
        self.partial = [bufs[depth * n + (depth - 1) * i :][: depth - 1] for i in range(n)]
        self.copies, self.latest = [], {}

    def block(self, phase, i, coord):
        part, order = self.pieces[i]
        left = [a for a in self.axes if a not in order[:phase]]
        ref = self.partial[i][phase - 1] if phase else self.x
        tail = () if phase else part
        return ref.at[tuple(coord if a == order[phase] else slice(None) for a in left) + tail]

    def launch(self, phase, i):
        axis = self.pieces[i][1][phase]
        self.latest[i] = []
        for d in range(1, SIZES[axis]):
            at = (i * self.depth + phase) * 3 + d - 1
            self.latest[i].append(
                remote(
                    self.block(phase, i, lax.rem(self.here[axis] + d, SIZES[axis])),
                    self.inbox[i][phase].at[d - 1],
                    self.send.at[at],
                    self.recv.at[at],
                    device_at(self.axes, moved(self.here, axis, d)),
                )
            )
        self.copies.extend(self.latest[i])

    def total(self, phase, i):
        part, order = self.pieces[i]
        axis = order[phase]
        for copy in self.latest[i]:
            copy.wait_recv()
        mine, inbox = self.block(phase, i, self.here[axis]), self.inbox[i][phase]
        left = [SIZES[a] for a in self.axes if a not in order[: phase + 1]]
        count = 1
        for extent in left:
            count *= extent

        def add(k, carry):
            at = ()
            for extent in reversed(left):
                at, k = (k % extent,) + at, k // extent
            whole = mine[at].astype(jnp.float32) if at else mine[...].astype(jnp.float32)
            for d in range(SIZES[axis] - 1):
                whole = whole + inbox[(d,) + at].astype(jnp.float32)
            if phase == self.depth - 1:
                self.o[part] = whole.astype(self.o.dtype)
            else:
                self.partial[i][phase][at] = whole.astype(jnp.bfloat16)
            return carry

        if count == 1:
            add(0, 0)
        else:
            lax.fori_loop(0, count, add, 0)

    def run(self):
        for i in range(len(self.pieces)):
            self.launch(0, i)
        for phase in range(self.depth):
            for i in range(len(self.pieces)):
                self.total(phase, i)
                if phase < self.depth - 1:
                    self.launch(phase + 1, i)
        for copy in self.copies:
            copy.wait_send()


def scatter_plan(rows, cols, axes):
    first = "c" if axes == PAIRED else ""
    pieces = cut(rows, cols, [first + order[::-1] for order in ORDERS[axes]])
    depth = len(axes)
    n = 3 * depth * len(pieces)
    inboxes, partials = [], []
    for part, order in pieces:
        size = tuple(edge.size for edge in part)
        for phase in range(depth):
            left = [SIZES[a] for a in axes if a not in order[: phase + 1]]
            inboxes.append(pltpu.VMEM((SIZES[order[phase]] - 1, *left, *size), jnp.bfloat16))
            if phase < depth - 1:
                partials.append(pltpu.VMEM((*left, *size), jnp.bfloat16))
    sems = [pltpu.SemaphoreType.DMA((n,)), pltpu.SemaphoreType.DMA((n,))]
    return pieces, sems, inboxes + partials


def split_axes(x, axes):
    return x.reshape(*[SIZES[a] for a in axes], *x.shape[1:])


def values_kernel(
    pieces, x_ref, dq_ref, o_ref, dq_out, send, recv, swap_send, swap_recv, swap_local, own, *bufs
):
    here = coords(PAIRED)
    greet(axis_peers(PAIRED, here), here)
    first = Swap(here, dq_ref, dq_out, swap_send.at[0], swap_recv.at[0], swap_local.at[0])
    second = Swap(here, own, o_ref, swap_send.at[1], swap_recv.at[1], swap_local.at[1])
    first.start()
    Scatter(here, PAIRED, pieces, x_ref, own, send, recv, bufs).run()
    second.start()
    first.wait()
    second.wait()


def scatter_values(x, d_queries, collective_id):
    _, rows, cols = x.shape
    pieces, sems, bufs = scatter_plan(rows, cols, PAIRED)
    return pl.pallas_call(
        functools.partial(values_kernel, pieces),
        out_shape=(
            jax.ShapeDtypeStruct((rows, cols), jnp.bfloat16),
            jax.ShapeDtypeStruct(d_queries.shape, d_queries.dtype),
        ),
        in_specs=[VMEM, ANY],
        out_specs=(ANY, ANY),
        scratch_shapes=sems
        + [pltpu.SemaphoreType.DMA((2,))] * 3
        + [pltpu.VMEM((rows, cols), jnp.bfloat16)]
        + bufs,
        compiler_params=pltpu.CompilerParams(
            collective_id=collective_id, has_side_effects=True, vmem_limit_bytes=40 << 20
        ),
        name="scatter_values",
    )(split_axes(x, PAIRED), d_queries)


def final_kernel(
    pieces, up_pieces, spread, x_ref, up_ref, o_ref, all_ref,
    send, recv, up_send, up_recv, g_send, g_recv, g_fore, g_back, local, own, *bufs,
):
    here = coords(PLAIN)
    greet(axis_peers(PLAIN, here))
    cut_at = 5 * len(up_pieces)
    up = Scatter(here, PLAIN, up_pieces, up_ref, own, up_send, up_recv, bufs[:cut_at])
    down = Scatter(here, PLAIN, pieces, x_ref, o_ref, send, recv, bufs[cut_at:])
    gather = Gather(here, PLAIN, spread, own, all_ref, (g_send, g_recv, g_fore, g_back), 0)

    def stage(scatter, phase):
        for i in range(len(scatter.pieces)):
            if phase:
                scatter.total(phase - 1, i)
            if phase < 3:
                scatter.launch(phase, i)

    def spread_on(phase):
        for i in range(len(spread)):
            if phase:
                gather.arrived(phase - 1, i)
            gather.launch(phase, i)

    stage(up, 0)
    stage(down, 0)
    stage(up, 1)
    stage(up, 2)
    stage(down, 1)
    stage(up, 3)
    copy = pltpu.make_async_copy(own, all_ref.at[gather.place], local)
    copy.start()
    spread_on(0)
    stage(down, 2)
    copy.wait()
    spread_on(1)
    spread_on(2)
    stage(down, 3)
    gather.finish()
    for one in up.copies + down.copies:
        one.wait_send()


def scatter_final(x, up, collective_id):
    _, rows, cols = x.shape
    up_rows = up.shape[1]
    pieces, sems, bufs = scatter_plan(rows, cols, PLAIN)
    up_pieces, up_sems, up_bufs = scatter_plan(up_rows, cols, PLAIN)
    spread = cut(up_rows, cols, ORDERS[PLAIN])
    out, ups = pl.pallas_call(
        functools.partial(final_kernel, pieces, up_pieces, spread),
        out_shape=(
            jax.ShapeDtypeStruct((rows, cols), jnp.float32),
            jax.ShapeDtypeStruct((2, 4, 4, up_rows, cols), jnp.float32),
        ),
        in_specs=[VMEM, VMEM],
        out_specs=(VMEM, VMEM),
        scratch_shapes=sems
        + up_sems
        + semaphores(9 * len(spread) + 1)
        + [pltpu.SemaphoreType.DMA, pltpu.VMEM((up_rows, cols), jnp.float32)]
        + up_bufs
        + bufs,
        compiler_params=pltpu.CompilerParams(
            collective_id=collective_id, has_side_effects=True, vmem_limit_bytes=40 << 20
        ),
        name="scatter_final",
    )(split_axes(x, PLAIN), split_axes(up, PLAIN))
    return out, ups.reshape(32, up_rows, cols)


def middle_kernel(
    pieces, scatter_pieces, total_slots, x_ref, wo_ref, ng_ref, gain_ref, o_ref, normed_out,
    everyone, part, inbox, hidden, grads, d_part, normed, stat, near_in, far_in,
    send, recv, fore, back, local, h_send, h_recv, s_send, s_recv, g_send, g_recv,
    swap_send, swap_recv, swap_local, r_send, r_recv, *bufs,
):
    f32, bf16 = jnp.float32, jnp.bfloat16
    here = coords(PAIRED)
    me, member = group_place("paired section", here)
    others = [lax.rem(me + d, 4) for d in range(1, 4)]
    near = [{**here, "h": lax.rem(here["h"] + a, 2), "c": lax.rem(here["c"] + b, 2)} for a, b in ((0, 1), (1, 0), (1, 1))]
    far = [
        {**here, "y": lax.rem(here["y"] + a, 2), "z": lax.rem(here["z"] + b, 4)}
        for a in range(2)
        for b in range(4)
        if a or b
    ]
    devices = [member(k) for k in others] + [device_at(PAIRED, place) for place in near + far]
    greet(devices, here)

    gather = Gather(here, PAIRED, pieces, x_ref, everyone, (send, recv, fore, back), 0)
    own = pltpu.make_async_copy(x_ref, everyone.at[gather.place], local)
    own.start()
    run_gathers([gather], [own], lambda phase: None)

    def slab(ref, k):
        return ref.at[k // 2, pl.ds(2 * (k % 2), 2)]

    copies = []
    for d in (2, 1, 3, 0):
        k = lax.rem(me + d, 4)
        rows = slab(everyone, k)[...].reshape(ROWS, x_ref.shape[1])
        part[k] = jnp.dot(rows, wo_ref[...], preferred_element_type=f32).astype(bf16)
        if d:
            copies.append(
                remote(part.at[k], inbox.at[d - 1], h_send.at[d - 1], h_recv.at[d - 1], member(k))
            )
    scaled = (total_slots ** (-0.5)) * ng_ref[...].astype(f32) * gain_ref[...]
    for copy in copies:
        copy.wait()
    summed = part[me].astype(f32)
    for d in range(3):
        summed = summed + inbox[d].astype(f32)
    hidden[...] = summed

    ones = jnp.ones((8, summed.shape[1]), f32)
    row_sums = lambda v: lax.dot_general(
        ones, v, (((1,), (1,)), ((), ())), preferred_element_type=f32, precision=lax.Precision.HIGHEST
    )
    first = lax.broadcasted_iota(jnp.int32, (8, ROWS), 0) == 0
    total = jnp.where(first, row_sums(summed * summed), row_sums(scaled * summed))
    stat[0] = total
    at = 0
    for step, (places, box) in enumerate(((near, near_in), (far, far_in))):
        copies = [
            remote(stat.at[step], box.at[k], s_send.at[at + k], s_recv.at[at + k], device_at(PAIRED, place))
            for k, place in enumerate(places)
        ]
        at += len(places)
        for copy in copies:
            copy.wait()
        for k in range(len(places)):
            total = total + box[k]
        if step == 0:
            stat[1] = total
    inv = lax.rsqrt(total[0:1, :] / MODEL_DIM + epsilon)
    pull = inv * inv * inv * total[1:2, :] / MODEL_DIM
    across = lambda v: jnp.transpose(v + jnp.zeros((HD, ROWS), f32))
    inv, pull = across(inv), across(pull)
    for j in range(summed.shape[1] // HD):
        cols = slice(j * HD, (j + 1) * HD)
        value = hidden[:, cols]
        normed[:, cols] = (value * inv * gain_ref[:, cols]).astype(bf16)
        weighted = (total_slots ** (-0.5)) * ng_ref[:, cols].astype(f32) * gain_ref[:, cols]
        grads[me, :, cols] = (inv * weighted - value * pull).astype(bf16)
    copies = [
        remote(grads.at[me], grads.at[me], g_send.at[d], g_recv.at[d], member(k))
        for d, k in enumerate(others)
    ]
    swap = Swap(here, normed, normed_out, swap_send, swap_recv, swap_local)
    swap.start()

    def back_through(k):
        rows = contract(grads[k], wo_ref[...], 1, 1).astype(bf16)
        slab(d_part, k)[...] = rows.reshape(2, 2, 2, x_ref.shape[0], x_ref.shape[1])

    back_through(me)
    for d in range(3):
        copies[2 - d].wait_recv()
        back_through(lax.rem(me + 4 - (3 - d), 4))
    for copy in copies:
        copy.wait_send()
    Scatter(here, PAIRED, scatter_pieces, d_part, o_ref, r_send, r_recv, bufs).run()
    swap.wait()


def middle(x, output_weight, normed_gradient, gain, total_slots, collective_id):
    bf16, f32 = jnp.bfloat16, jnp.float32
    rows, cols = x.shape
    width = output_weight.shape[1]
    pieces = cut(rows, cols, ORDERS[PAIRED])
    scatter_pieces, sems, bufs = scatter_plan(rows, cols, PAIRED)
    sizes = [SIZES[a] for a in PAIRED]
    dma = pltpu.SemaphoreType.DMA
    return pl.pallas_call(
        functools.partial(middle_kernel, pieces, scatter_pieces, total_slots),
        out_shape=(
            jax.ShapeDtypeStruct(x.shape, bf16),
            jax.ShapeDtypeStruct(normed_gradient.shape, bf16),
        ),
        in_specs=[VMEM] * 4,
        out_specs=(VMEM, ANY),
        scratch_shapes=[
            pltpu.VMEM((*sizes, rows, cols), bf16),
            pltpu.VMEM((4, ROWS, width), bf16),
            pltpu.VMEM((3, ROWS, width), bf16),
            pltpu.VMEM((ROWS, width), f32),
            pltpu.VMEM((4, ROWS, width), bf16),
            pltpu.VMEM((*sizes, rows, cols), bf16),
            pltpu.VMEM((ROWS, width), bf16),
            pltpu.VMEM((2, 8, ROWS), f32),
            pltpu.VMEM((3, 8, ROWS), f32),
            pltpu.VMEM((7, 8, ROWS), f32),
            *semaphores(9 * len(pieces) + 1),
            dma,
            dma((3,)),
            dma((3,)),
            dma((10,)),
            dma((10,)),
            dma((3,)),
            dma((3,)),
            dma,
            dma,
            dma,
            *sems,
            *bufs,
        ],
        compiler_params=pltpu.CompilerParams(
            collective_id=collective_id, has_side_effects=True, vmem_limit_bytes=32 << 20
        ),
        name="middle",
    )(x, output_weight, normed_gradient, gain)


def group_place(group, here):
    if group == "section":
        return here["m"] * 2 + here["c"], lambda k: device_at("x", {**here, "m": k // 2, "c": k % 2})
    return here["m"] * 2 + here["l"], lambda k: device_at("h", {**here, "m": k // 2, "l": k % 2})

def exchange_kernel(group, count, apart, x_ref, o_ref, send, recv, local):
    me, device = group_place(group, coords(PLAIN))
    others = [lax.rem(me + d, count) for d in range(1, count)]
    greet([device(k) for k in others])
    own = pltpu.make_async_copy(x_ref.at[me] if apart else x_ref, o_ref.at[me], local)
    own.start()
    copies = [
        remote(x_ref.at[k] if apart else x_ref, o_ref.at[me], send.at[d], recv.at[d], device(k))
        for d, k in enumerate(others)
    ]
    own.wait()
    for copy in copies:
        copy.wait()


def exchange(x, group, apart, collective_id, name):
    count = 4
    shape = x.shape[1:] if apart else x.shape
    return pl.pallas_call(
        functools.partial(exchange_kernel, group, count, apart),
        out_shape=jax.ShapeDtypeStruct((count, *shape), x.dtype),
        in_specs=[ANY],
        out_specs=ANY,
        scratch_shapes=[
            pltpu.SemaphoreType.DMA((count - 1,)),
            pltpu.SemaphoreType.DMA((count - 1,)),
            pltpu.SemaphoreType.DMA,
        ],
        compiler_params=pltpu.CompilerParams(
            collective_id=collective_id, has_side_effects=True, vmem_limit_bytes=1 << 20
        ),
        name=name,
    )(x)


def contract(left, right, l, r):
    return lax.dot_general(
        left, right, (((l,), (r,)), ((), ())), preferred_element_type=jnp.float32
    )


def head_rows(ref):
    return jnp.concatenate([ref[:, h * HD : (h + 1) * HD] for h in range(HEADS_HERE)], axis=0)


def key_block(kv_ref, g, cols, context_rows, slots):
    context = kv_ref[pl.ds(g * GROUP, GROUP), :context_rows, cols]
    context = context.reshape(GROUP * context_rows, HD)
    if not slots:
        return context
    memory = kv_ref[pl.ds(g * GROUP, GROUP), context_rows:, cols]
    return jnp.concatenate([context, memory.reshape(GROUP * slots, HD)], axis=0)


def key_docs(g, bounds_ref, context_rows, slots):
    edge = GROUP * context_rows
    token = g * edge + lax.broadcasted_iota(jnp.int32, (edge, HD), 0)
    docs = (token >= 4 * bounds_ref[0:1, :]) & (token < 4 * bounds_ref[1:2, :])
    if slots:
        slot = g * (GROUP * slots) + lax.broadcasted_iota(jnp.int32, (GROUP * slots, HD), 0)
        docs = jnp.concatenate(
            [
                docs.astype(jnp.float32),
                ((slot >= bounds_ref[0:1, :]) & (slot < bounds_ref[1:2, :])).astype(jnp.float32),
            ],
            axis=0,
        )
    return docs.astype(jnp.float32).astype(jnp.bfloat16)


def with_fill(q, rows_ref, bounds_ref):
    low = jnp.transpose(rows_ref[2:3, :].astype(jnp.float32) + jnp.zeros((HD, ROWS), jnp.float32))
    mine = low == bounds_ref[0:1, :].astype(jnp.float32)
    return jnp.concatenate([q, jnp.where(mine, 0.0, mask_fill).astype(jnp.bfloat16)], axis=1)


def group_scores(keys, g, q_wide, rows_ref, bounds_ref, context_rows, slots, causal):
    docs = key_docs(g, bounds_ref, context_rows, slots)
    scores = contract(jnp.concatenate([keys, docs], axis=1), q_wide, 1, 1)
    if not causal:
        return scores
    edge = GROUP * context_rows
    slot = g * (GROUP * slots) + lax.broadcasted_iota(jnp.int32, (GROUP * slots, ROWS), 0)
    return jnp.concatenate(
        [scores[:edge], jnp.where(slot <= rows_ref[3:4, :], scores[edge:], mask_fill)], axis=0
    )


def over_groups(span, step):
    first, own, last = span[0], span[1], span[2]

    def before(g, carry):
        step(g, False, True)
        return carry

    def after(g, carry):
        step(g, False, False)
        return carry

    step(own, True, True)
    lax.fori_loop(first, own, before, 0)
    lax.fori_loop(own + 1, last, after, 0)


def attend_kernel(
    context_rows, span, rows_ref, bounds_ref, q_ref, kv_ref, o_ref, ot_ref, top_ref, mass_ref
):
    slots = kv_ref.shape[1] - context_rows
    q = with_fill(head_rows(q_ref), rows_ref, bounds_ref)
    ot_ref[...] = jnp.zeros_like(ot_ref)
    top_ref[...] = jnp.full_like(top_ref, mask_fill)
    mass_ref[...] = jnp.zeros_like(mass_ref)

    def step(g, masked, with_memory):
        extra = slots if with_memory else 0
        keys = key_block(kv_ref, g, slice(0, HD), context_rows, extra)
        scores = group_scores(keys, g, q, rows_ref, bounds_ref, context_rows, extra, masked)
        before = top_ref[0:1, :]
        top = jnp.maximum(before, jnp.max(scores, axis=0, keepdims=True))
        keep = jnp.exp2((before - top) * exp2_scale)
        weight = jnp.exp2((scores - top) * exp2_scale)
        top_ref[0:1, :] = top
        mass_ref[0:1, :] = mass_ref[0:1, :] * keep + jnp.sum(weight, axis=0, keepdims=True)
        values = key_block(kv_ref, g, slice(HD, 2 * HD), context_rows, extra)
        ot_ref[...] = ot_ref[...] * keep + contract(values, weight.astype(jnp.bfloat16), 0, 0)

    over_groups(span, step)
    ot_ref[...] = ot_ref[...] / mass_ref[0:1, :]
    rows = jnp.transpose(ot_ref[...]).astype(jnp.bfloat16)
    here = q_ref.shape[0]
    for h in range(HEADS_HERE):
        o_ref[:, h * HD : (h + 1) * HD] = rows[h * here : (h + 1) * here]


def backward_kernel(
    context_rows, span, rows_ref, bounds_ref, q_ref, g_ref, kv_ref, ot_ref, top_ref, mass_ref,
    dq_ref, dv_ref, acc,
):
    slots = kv_ref.shape[1] - context_rows
    edge = GROUP * context_rows
    q = with_fill(head_rows(q_ref), rows_ref, bounds_ref)
    grad = head_rows(g_ref)
    center = jnp.sum(jnp.transpose(grad.astype(jnp.float32)) * ot_ref[...], axis=0, keepdims=True)
    top = top_ref[0:1, :]
    share = 1.0 / mass_ref[0:1, :]
    acc[...] = jnp.zeros_like(acc)
    dv_ref[...] = jnp.zeros_like(dv_ref)

    def step(g, masked, with_memory):
        extra = slots if with_memory else 0
        keys = key_block(kv_ref, g, slice(0, HD), context_rows, extra)
        scores = group_scores(keys, g, q, rows_ref, bounds_ref, context_rows, extra, masked)
        probs = jnp.exp2((scores - top) * exp2_scale) * share
        values = key_block(kv_ref, g, slice(HD, 2 * HD), context_rows, extra)
        d_probs = contract(values, grad, 1, 1)
        d_scores = (probs * (d_probs - center)).astype(jnp.bfloat16)
        d_values = contract(probs.astype(jnp.bfloat16), grad, 1, 0).astype(jnp.bfloat16)
        dv_ref[pl.ds(g * GROUP, GROUP), :context_rows, :] = d_values[:edge].reshape(
            GROUP, context_rows, HD
        )
        if with_memory:
            dv_ref[pl.ds(g * GROUP, GROUP), context_rows:, :] = d_values[edge:].reshape(
                GROUP, slots, HD
            )
        acc[...] += contract(keys, d_scores, 0, 0)

    over_groups(span, step)
    rows = jnp.transpose(acc[...] * score_scale).astype(jnp.bfloat16)
    here = q_ref.shape[0]
    for h in range(HEADS_HERE):
        dq_ref[:, h * HD : (h + 1) * HD] = rows[h * here : (h + 1) * here]


SMEM = pl.BlockSpec(memory_space=pltpu.SMEM)
BIG = pltpu.CompilerParams(vmem_limit_bytes=48 << 20)


def attend(span, rows, bounds, q, kv, context_rows):
    f32 = jnp.float32
    return pl.pallas_call(
        functools.partial(attend_kernel, context_rows),
        out_shape=(
            jax.ShapeDtypeStruct(q.shape, jnp.bfloat16),
            jax.ShapeDtypeStruct((HD, ROWS), f32),
            jax.ShapeDtypeStruct((8, ROWS), f32),
            jax.ShapeDtypeStruct((8, ROWS), f32),
        ),
        in_specs=[SMEM] + [VMEM] * 4,
        out_specs=(VMEM, VMEM, VMEM, VMEM),
        compiler_params=BIG,
        name="attend",
    )(span, rows, bounds, q, kv)


def attend_backward(span, rows, bounds, q, grad, kv, ot, top, mass, context_rows):
    return pl.pallas_call(
        functools.partial(backward_kernel, context_rows),
        out_shape=(
            jax.ShapeDtypeStruct(q.shape, jnp.bfloat16),
            jax.ShapeDtypeStruct((*kv.shape[:2], HD), jnp.bfloat16),
        ),
        in_specs=[SMEM] + [VMEM] * 8,
        out_specs=(VMEM, VMEM),
        scratch_shapes=[pltpu.VMEM((HD, ROWS), jnp.float32)],
        compiler_params=BIG,
        name="attend_backward",
    )(span, rows, bounds, q, grad, kv, ot, top, mass)


def row_bounds(document_slots, first, slot_dev, seq_size):
    docs = document_slots.shape[0]
    order = jnp.arange(docs, dtype=jnp.int32)
    ends = jnp.sum(jnp.where(order[None, :] <= order[:, None], document_slots[None, :], 0), axis=1)
    slot = first + jnp.arange(slot_dev, dtype=jnp.int32)
    passed = ends[None, :] <= slot[:, None]
    low = jnp.max(jnp.where(passed, ends[None, :], 0), axis=1)
    high = jnp.min(jnp.where(passed, slot_dev * seq_size, ends[None, :]), axis=1)
    one = jnp.stack([4 * low, 4 * high, low, slot] + [slot] * 4).astype(jnp.int32)
    unit = GROUP * slot_dev
    start, stop = jnp.min(low) // unit, (jnp.max(high) + unit - 1) // unit
    span = jnp.stack([start, first // unit, stop])
    starts = ends - document_slots
    bounds = jnp.stack([starts, ends] + [ends] * 6)
    bounds = jnp.pad(bounds, ((0, 0), (0, HD - docs)))
    return span.astype(jnp.int32), jnp.tile(one, (1, HEADS_HERE)), bounds.astype(jnp.int32)


def body(
    context,
    memory,
    query_weight,
    key_weight,
    value_weight,
    query_down_map,
    query_up_map,
    value_down_map,
    value_up_map,
    output_weight,
    decoder_gain,
    document_slots,
    normed_gradient,
):
    bf16, f32 = jnp.bfloat16, jnp.float32
    tok_dev = context.shape[0]
    slot_dev = memory.shape[0]
    seq_size = lax.axis_size("seq")
    here = coords(PLAIN)
    paired_index = here["y"] * 16 + here["z"] * 4 + here["h"] * 2 + here["c"]
    section_extent = lax.axis_size("section")
    section_index = lax.axis_index("section")
    kv_weight, down, query_sum, output_weight = opening(
        jnp.concatenate([key_weight, value_weight], axis=1),
        value_down_map,
        memory,
        query_weight,
        output_weight,
        1,
    )
    query_low = jnp.dot(memory, query_down_map, preferred_element_type=f32).astype(bf16)
    row_parts = (context, memory)
    value_low = jnp.concatenate(
        [jnp.dot(part, down, preferred_element_type=f32).astype(bf16) for part in row_parts], axis=0
    )
    projected = jnp.concatenate(
        [jnp.dot(part, kv_weight, preferred_element_type=f32) for part in row_parts], axis=0
    )
    queries = (
        query_sum + adapter_scale * jnp.dot(query_low, query_up_map, preferred_element_type=f32)
    ).astype(bf16)
    keys = projected[:, :HD].astype(bf16)
    values = (
        projected[:, HD : 2 * HD]
        + adapter_scale * jnp.dot(value_low, value_up_map, preferred_element_type=f32)
    ).astype(bf16)
    kv, queries_here, normed_gradient, decoder_gain = gather_keys(
        jnp.concatenate([keys, values], axis=1),
        queries,
        normed_gradient,
        decoder_gain.reshape(-1, 128),
        2,
    )
    decoder_gain = decoder_gain.reshape(1, -1)
    span, rows, bounds = row_bounds(document_slots, paired_index * slot_dev, slot_dev, seq_size)
    attended, ot, top, mass = attend(span, rows, bounds, queries_here, kv, tok_dev)
    total_slots = slot_dev * seq_size
    d_attended, normed = middle(
        attended, output_weight, normed_gradient, decoder_gain, total_slots, 3
    )
    d_queries, dv_part = attend_backward(
        span, rows, bounds, queries_here, d_attended, kv, ot, top, mass, tok_dev
    )
    d_values, d_queries = scatter_values(dv_part, d_queries, 8)
    query_up_part = adapter_scale * contract(query_low, d_queries, 0, 0)
    value_up_part = adapter_scale * contract(value_low, d_values, 0, 0)
    query_part = adapter_scale * contract(d_queries, query_up_map, 1, 1)
    value_part = adapter_scale * contract(d_values, value_up_map, 1, 1)
    backs = jnp.sum(
        exchange(
            jnp.concatenate([query_part, value_part], axis=0).astype(bf16),
            "section", False, 9, "sum_backs",
        ).astype(f32),
        axis=0,
    ).astype(bf16)
    width = memory.shape[1] // section_extent
    memory_cols = lax.dynamic_slice_in_dim(memory, section_index * width, width, 1)
    context_cols = lax.dynamic_slice_in_dim(context, section_index * width, width, 1)
    memory_backs = jnp.concatenate([backs[:slot_dev], backs[slot_dev + tok_dev :]], axis=1)
    memory_down = contract(memory_cols, memory_backs, 0, 0)
    down_parts = [
        memory_down[:, :HD],
        memory_down[:, HD:] + contract(context_cols, backs[slot_dev : slot_dev + tok_dev], 0, 0),
    ]
    ups = jnp.concatenate([query_up_part, value_up_part], axis=1)
    lanes = ups.shape[1] // 128
    ups = jnp.moveaxis(ups.reshape(128, lanes, 128), 1, 0).reshape(seq_size, -1, 128)
    up_rows = ups.shape[1]
    down_rows = MODEL_DIM // section_extent // seq_size
    final, ups = scatter_final(
        jnp.concatenate([part.reshape(seq_size, -1, 128).astype(bf16) for part in down_parts], axis=1),
        jnp.pad(ups.astype(bf16), ((0, 0), (0, -up_rows % 16), (0, 0))),
        10,
    )
    grad_qa, grad_va = final[:down_rows], final[down_rows:]
    ups = ups[:, :up_rows]
    ups = jnp.moveaxis(ups.reshape(lanes, 128, 128), 0, 1).reshape(128, lanes * 128)
    split = query_up_part.shape[1]
    return (normed, grad_qa, grad_va, ups[:, :split], ups[:, split:])


def solution(mesh):
    in_specs = (
        P("seq", None),
        P("seq", None),
        P(None, "section"),
        P("seq", "section"),
        P("seq", "section"),
        P(),
        P(None, "section"),
        P("seq", None),
        P(None, "section"),
        P("section", "seq"),
        P("seq"),
        P(),
        P("section", "seq"),
    )
    out_specs = (
        P("section", "seq"),
        P(("section", "seq"), None),
        P(("section", "seq"), None),
        P(None, "section"),
        P(None, "section"),
    )
    return jax.shard_map(body, mesh=mesh, in_specs=in_specs, out_specs=out_specs, check_vma=False)
```

```python
import functools

import jax
import jax.numpy as jnp
from jax import lax
from jax.experimental import pallas as pl
from jax.experimental.pallas import tpu as pltpu
from jax.sharding import PartitionSpec as P

MODEL_DIM = 8192
HEADS_HERE = 8
HD = 128
ROWS = 512
GROUP = 2

adapter_scale = 0.25
epsilon = 1e-05
mask_fill = -1e30
score_scale = HD ** (-0.5)
exp2_scale = score_scale * 1.4426950408889634

MESH = pl.DeviceIdType.MESH
ANY = pl.BlockSpec(memory_space=pl.ANY)
VMEM = pl.BlockSpec(memory_space=pltpu.VMEM)
HBM = pl.BlockSpec(memory_space=pltpu.HBM)

SIZES = {"y": 2, "z": 4, "x": 4, "h": 2, "c": 2}
PLAIN, PAIRED = "yzx", "yzhc"


def coords(axes):
    seq, section = lax.axis_index("seq"), lax.axis_index("section")
    here = {"y": seq // 16, "z": (seq // 4) % 4, "x": seq % 4, "m": section // 2, "c": section % 2}
    here["h"], here["l"] = here["x"] // 2, here["x"] % 2
    return here


def device_at(axes, here):
    x = here["x"] if "x" in axes else here["h"] * 2 + here["l"]
    return (here["m"] * 2 + here["c"], here["y"] * 16 + here["z"] * 4 + x)


def moved(here, axis, step):
    return {**here, axis: lax.rem(here[axis] + step, SIZES[axis])}


def greet(devices, here=None):
    barrier = pltpu.get_barrier_semaphore()
    for device in devices:
        pl.semaphore_signal(barrier, inc=1, device_id=device, device_id_type=MESH)
    if here is not None:

        @pl.when(here["c"] != here["l"])
        def _():
            pl.semaphore_signal(
                barrier, inc=1, device_id=swap_device(here), device_id_type=MESH
            )

    extra = 0 if here is None else lax.rem(here["c"] + here["l"], 2)
    pl.semaphore_wait(barrier, len(devices) + extra)


def swap_device(here):
    return device_at("h", {**here, "c": here["l"], "l": here["c"]})


class Swap:
    def __init__(self, here, source, target, send, recv, local):
        self.apart = here["c"] != here["l"]
        self.there = lambda: pltpu.make_async_remote_copy(
            src_ref=source,
            dst_ref=target,
            send_sem=send,
            recv_sem=recv,
            device_id=swap_device(here),
            device_id_type=MESH,
        )
        self.stays = lambda: pltpu.make_async_copy(source, target, local)

    def start(self):
        @pl.when(self.apart)
        def _():
            self.there().start()

        @pl.when(jnp.logical_not(self.apart))
        def _():
            self.stays().start()

    def wait(self):
        @pl.when(self.apart)
        def _():
            self.there().wait()

        @pl.when(jnp.logical_not(self.apart))
        def _():
            self.stays().wait()


def axis_peers(axes, here):
    return [device_at(axes, moved(here, a, d)) for a in axes for d in range(1, SIZES[a])]


def remote(source, target, send, recv, device):
    copy = pltpu.make_async_remote_copy(
        src_ref=source,
        dst_ref=target,
        send_sem=send,
        recv_sem=recv,
        device_id=device,
        device_id_type=MESH,
    )
    copy.start()
    return copy


class Gather:
    def __init__(self, here, axes, pieces, source, target, sems, base):
        self.here, self.axes, self.pieces, self.base = here, axes, pieces, base
        self.source, self.target = source, target
        self.send, self.recv, self.fore, self.back = sems
        self.place = tuple(here[a] for a in axes)
        self.paired = "c" in axes
        self.partner = device_at(axes, moved(here, "c", 1)) if self.paired else None
        self.copies, self.latest, self.passed = [], {}, []

    def at(self, phase, i, d):
        return self.base + (i * 3 + phase) * 3 + d

    def begin(self):
        if self.paired:
            own = self.target.at[self.place]
            sem = self.base + 9 * len(self.pieces)
            self.passed.append(
                remote(
                    own if self.source is None else self.source,
                    own,
                    self.fore.at[sem],
                    self.back.at[sem],
                    self.partner,
                )
            )

    def arrived(self, phase, i):
        part, order = self.pieces[i]
        axis = order[phase]
        for d, copy in enumerate(self.latest[i]):
            copy.wait_recv()
            if self.paired:
                came = {**self.here, axis: lax.rem(self.here[axis] + SIZES[axis] - d - 1, SIZES[axis])}
                region = self.target.at[
                    tuple(slice(None) if a in order[:phase] else came[a] for a in self.axes)
                    + part
                ]
                at = self.at(phase, i, d)
                self.passed.append(
                    remote(region, region, self.fore.at[at], self.back.at[at], self.partner)
                )

    def launch(self, phase, i):
        part, order = self.pieces[i]
        held = tuple(slice(None) if a in order[:phase] else self.here[a] for a in self.axes)
        region = self.target.at[held + part]
        source = region if phase or self.source is None else self.source.at[part]
        self.latest[i] = []
        for d in range(1, SIZES[order[phase]]):
            at = self.at(phase, i, d - 1)
            device = device_at(self.axes, moved(self.here, order[phase], d))
            self.latest[i].append(remote(source, region, self.send.at[at], self.recv.at[at], device))
        self.copies += self.latest[i]

    def finish(self):
        for i in range(len(self.pieces)):
            self.arrived(2, i)
        for copy in self.passed:
            copy.wait_recv()
        for copy in self.copies + self.passed:
            copy.wait_send()


def run_gathers(gathers, owns, between):
    for gather in gathers:
        gather.begin()
    for phase in range(3):
        for gather in gathers:
            for i in range(len(gather.pieces)):
                if phase:
                    gather.arrived(phase - 1, i)
                    if phase == 1:
                        while owns:
                            owns.pop().wait()
                gather.launch(phase, i)
        between(phase)
    for gather in gathers:
        gather.finish()


def semaphores(count):
    return [pltpu.SemaphoreType.DMA((count,)) for _ in range(4)]


def front_kernel(
    pieces, half_pieces, kv_pieces,
    key_ref, value_ref, down_ref, context_ref, memory_ref, weight_ref, query_down_ref, query_up_ref,
    value_up_ref, wo_ref, ng_ref, gain_ref,
    kv_all, q_out, query_low, value_low, wo_out, ng_out, gain_out,
    shard, w_all, d_all, context, memory, query_down, buffer, acc, projected, kv_own, q_own,
    send, recv, fore, back, k_send, k_recv, k_fore, k_back,
    loads, inputs, local, swap_send, swap_recv, swap_local,
):
    f32, bf16 = jnp.float32, jnp.bfloat16
    here = coords(PLAIN)
    depth = buffer.shape[1]
    count = weight_ref.shape[0] // depth
    half = down_ref.shape[0] // 2
    tok = context_ref.shape[0]

    def load(k):
        return pltpu.make_async_copy(
            weight_ref.at[pl.ds(k * depth, depth)], buffer.at[k % 3], loads.at[k % 3]
        )

    own_half = down_ref.at[pl.ds(here["c"] * half, half)]
    fetches = [
        pltpu.make_async_copy(a, b, inputs.at[i])
        for i, (a, b) in enumerate(
            (
                (key_ref, shard.at[:, pl.ds(0, HD)]),
                (value_ref, shard.at[:, pl.ds(HD, HD)]),
                (memory_ref, memory),
                (query_down_ref, query_down),
                (context_ref, context),
            )
        )
    ]
    for fetch in fetches:
        fetch.start()
    for k in range(2):
        load(k).start()
    greet(axis_peers(PLAIN + "c", here), here)
    swaps = [
        Swap(here, a, b, swap_send.at[i], swap_recv.at[i], swap_local.at[i])
        for i, (a, b) in enumerate(
            (
                (kv_own, kv_all.at[here["y"], here["z"], here["h"], here["l"]]),
                (q_own, q_out),
                (gain_ref, gain_out),
                (ng_ref, ng_out),
                (wo_ref, wo_out),
            )
        )
    ]
    fetches[0].wait()
    fetches[1].wait()
    sems = (send, recv, fore, back)
    plain = Gather(here, PLAIN, pieces, shard, w_all, sems, 0)
    shared = Gather(here, PLAIN + "c", half_pieces, own_half, d_all, sems, 9 * len(pieces) + 1)
    owns = [
        pltpu.make_async_copy(shard, w_all.at[plain.place], local.at[0]),
        pltpu.make_async_copy(own_half, d_all.at[shared.place], local.at[1]),
    ]
    for own in owns:
        own.start()

    def between(phase):
        if phase < 2:
            return
        swaps[4].start()
        fetches[2].wait()
        fetches[3].wait()
        low = jnp.dot(memory[...], query_down[...], preferred_element_type=f32).astype(bf16)
        query_low[...] = low
        acc[...] = adapter_scale * jnp.dot(low, query_up_ref[...], preferred_element_type=f32)
        for k in range(count):
            load(k).wait()
            if k + 2 < count:
                load(k + 2).start()
            acc[...] += jnp.dot(
                memory[:, k * depth : (k + 1) * depth], buffer[k % 3], preferred_element_type=f32
            )
        q_own[...] = acc[...].astype(bf16)
        fetches[4].wait()

    run_gathers([plain, shared], owns, between)
    wide = 4 * shard.shape[0]
    for j in range(8):
        at = (j // 4, j % 4)
        kv_rows = w_all[at].reshape(wide, 2 * HD)
        down_rows = d_all[at].reshape(wide, HD)
        for rows, source in ((slice(0, tok), context), (slice(tok, None), memory)):
            part = source[:, j * wide : (j + 1) * wide]
            for cols, right in ((slice(0, 2 * HD), kv_rows), (slice(2 * HD, None), down_rows)):
                step = jnp.dot(part, right, preferred_element_type=f32)
                projected[rows, cols] = step if j == 0 else projected[rows, cols] + step
    low = projected[:, 2 * HD :].astype(bf16)
    value_low[...] = low
    kv_own[:, :HD] = projected[:, :HD].astype(bf16)
    kv_own[:, HD:] = (
        projected[:, HD : 2 * HD]
        + adapter_scale * jnp.dot(low, value_up_ref[...], preferred_element_type=f32)
    ).astype(bf16)
    swaps[0].start()
    swaps[0].wait()
    gather = Gather(here, PAIRED, kv_pieces, None, kv_all, (k_send, k_recv, k_fore, k_back), 0)

    def rest(phase):
        if phase == 2:
            for swap in swaps[1:4]:
                swap.start()

    run_gathers([gather], [], rest)
    for swap in swaps[1:]:
        swap.wait()


def front(
    key_weight, value_weight, down, context, memory, query_weight, query_down, query_up, value_up,
    output_weight, normed_gradient, gain, collective_id,
):
    f32, bf16 = jnp.float32, jnp.bfloat16
    rows, half = key_weight.shape[0], down.shape[0] // 2
    tok, slots, model = context.shape[0], memory.shape[0], memory.shape[1]
    keys, wide = tok + slots, query_weight.shape[1]
    pieces = cut(rows, 2 * HD, ORDERS[PLAIN])
    half_pieces = cut(half, HD, ORDERS[PLAIN])
    kv_pieces = cut(keys, 2 * HD, ORDERS[PAIRED])
    n = 9 * len(pieces) + 1 + 9 * len(half_pieces) + 1
    like = lambda a: jax.ShapeDtypeStruct(a.shape, a.dtype)
    sizes = [SIZES[a] for a in PAIRED]
    dma = pltpu.SemaphoreType.DMA
    kv, *rest = pl.pallas_call(
        functools.partial(front_kernel, pieces, half_pieces, kv_pieces),
        out_shape=(
            jax.ShapeDtypeStruct((*sizes, keys, 2 * HD), bf16),
            jax.ShapeDtypeStruct((slots, wide), bf16),
            jax.ShapeDtypeStruct((slots, HD), bf16),
            jax.ShapeDtypeStruct((keys, HD), bf16),
            like(output_weight),
            like(normed_gradient),
            like(gain),
        ),
        in_specs=[ANY] * 7 + [VMEM] * 2 + [ANY] * 3,
        out_specs=(ANY, ANY, VMEM, VMEM, ANY, ANY, ANY),
        scratch_shapes=[
            pltpu.VMEM((rows, 2 * HD), bf16),
            pltpu.VMEM((2, 4, 4, rows, 2 * HD), bf16),
            pltpu.VMEM((2, 4, 4, 2, half, HD), bf16),
            pltpu.VMEM((tok, model), bf16),
            pltpu.VMEM((slots, model), bf16),
            pltpu.VMEM((model, HD), bf16),
            pltpu.VMEM((3, 1024, wide), bf16),
            pltpu.VMEM((slots, wide), f32),
            pltpu.VMEM((keys, 3 * HD), f32),
            pltpu.VMEM((keys, 2 * HD), bf16),
            pltpu.VMEM((slots, wide), bf16),
            *semaphores(n),
            *semaphores(9 * len(kv_pieces) + 1),
            dma((3,)),
            dma((5,)),
            dma((2,)),
            dma((5,)),
            dma((5,)),
            dma((5,)),
        ],
        compiler_params=pltpu.CompilerParams(
            collective_id=collective_id, has_side_effects=True, vmem_limit_bytes=61 << 20
        ),
        name="front",
    )(
        key_weight, value_weight, down, context, memory, query_weight, query_down, query_up, value_up,
        output_weight, normed_gradient, gain,
    )
    return kv.reshape(32, keys, 2 * HD), *rest


ORDERS = {
    PLAIN: ("xzy", "zyx", "yxz", "zxy", "yzx", "xyz"),
    PAIRED: ("hzy", "zyh", "yhz", "zhy", "yzh", "hyz"),
}


def cut(rows, cols, orders):
    by_rows = rows // 16 >= 2 * len(orders) or cols == 128
    step = 16 if by_rows else 128
    units = (rows if by_rows else cols) // step
    base, extra = divmod(units, len(orders))
    pieces, at = [], 0
    for i, order in enumerate(orders):
        size = (base + (1 if i < extra else 0)) * step
        if size:
            part = (pl.ds(at, size), pl.ds(0, cols)) if by_rows else (pl.ds(0, rows), pl.ds(at, size))
            pieces.append((part, order))
        at += size
    return pieces


class Scatter:
    def __init__(self, here, axes, pieces, x_ref, o_ref, send, recv, bufs):
        self.here, self.axes, self.pieces, self.x, self.o = here, axes, pieces, x_ref, o_ref
        self.send, self.recv, self.depth = send, recv, len(axes)
        n, depth = len(pieces), len(axes)
        self.inbox = [bufs[depth * i : depth * (i + 1)] for i in range(n)]
        self.partial = [bufs[depth * n + (depth - 1) * i :][: depth - 1] for i in range(n)]
        self.copies, self.latest = [], {}

    def block(self, phase, i, coord):
        part, order = self.pieces[i]
        left = [a for a in self.axes if a not in order[:phase]]
        ref = self.partial[i][phase - 1] if phase else self.x
        tail = () if phase else part
        return ref.at[tuple(coord if a == order[phase] else slice(None) for a in left) + tail]

    def launch(self, phase, i):
        axis = self.pieces[i][1][phase]
        self.latest[i] = []
        for d in range(1, SIZES[axis]):
            at = (i * self.depth + phase) * 3 + d - 1
            self.latest[i].append(
                remote(
                    self.block(phase, i, lax.rem(self.here[axis] + d, SIZES[axis])),
                    self.inbox[i][phase].at[d - 1],
                    self.send.at[at],
                    self.recv.at[at],
                    device_at(self.axes, moved(self.here, axis, d)),
                )
            )
        self.copies.extend(self.latest[i])

    def total(self, phase, i):
        part, order = self.pieces[i]
        axis = order[phase]
        for copy in self.latest[i]:
            copy.wait_recv()
        mine, inbox = self.block(phase, i, self.here[axis]), self.inbox[i][phase]
        left = [SIZES[a] for a in self.axes if a not in order[: phase + 1]]
        count = 1
        for extent in left:
            count *= extent

        def add(k, carry):
            at = ()
            for extent in reversed(left):
                at, k = (k % extent,) + at, k // extent
            whole = mine[at].astype(jnp.float32) if at else mine[...].astype(jnp.float32)
            for d in range(SIZES[axis] - 1):
                whole = whole + inbox[(d,) + at].astype(jnp.float32)
            if phase == self.depth - 1:
                self.o[part] = whole.astype(self.o.dtype)
            else:
                self.partial[i][phase][at] = whole.astype(jnp.bfloat16)
            return carry

        if count == 1:
            add(0, 0)
        else:
            lax.fori_loop(0, count, add, 0)

    def run(self):
        for i in range(len(self.pieces)):
            self.launch(0, i)
        for phase in range(self.depth):
            for i in range(len(self.pieces)):
                self.total(phase, i)
                if phase < self.depth - 1:
                    self.launch(phase + 1, i)
        for copy in self.copies:
            copy.wait_send()


def scatter_plan(rows, cols, axes):
    first = "c" if axes == PAIRED else ""
    pieces = cut(rows, cols, [first + order[::-1] for order in ORDERS[axes]])
    depth = len(axes)
    n = 3 * depth * len(pieces)
    inboxes, partials = [], []
    for part, order in pieces:
        size = tuple(edge.size for edge in part)
        for phase in range(depth):
            left = [SIZES[a] for a in axes if a not in order[: phase + 1]]
            inboxes.append(pltpu.VMEM((SIZES[order[phase]] - 1, *left, *size), jnp.bfloat16))
            if phase < depth - 1:
                partials.append(pltpu.VMEM((*left, *size), jnp.bfloat16))
    sems = [pltpu.SemaphoreType.DMA((n,)), pltpu.SemaphoreType.DMA((n,))]
    return pieces, sems, inboxes + partials


def split_axes(x, axes):
    return x.reshape(*[SIZES[a] for a in axes], *x.shape[1:])


def tail_kernel(
    dv_pieces, pieces, up_pieces, spread,
    dv_ref, dq_ref, query_low, value_low, query_up_ref, value_up_ref, memory_ref, context_ref,
    qa_ref, va_ref, query_up_out, value_up_out,
    dv_own, dv_home, dq_home, context, memory, backs, backs_in, down_x, up_x, own, everyone, result,
    v_send, v_recv, swap_send, swap_recv, swap_local, inputs, b_send, b_recv,
    send, recv, up_send, up_recv, g_send, g_recv, g_fore, g_back, local, *bufs,
):
    f32, bf16 = jnp.float32, jnp.bfloat16
    here = coords(PAIRED)
    slots = memory.shape[0]
    tok = context.shape[0]
    columns = pl.ds(lax.axis_index("section") * memory.shape[1], memory.shape[1])
    fetches = [
        pltpu.make_async_copy(memory_ref.at[:, columns], memory, inputs.at[0]),
        pltpu.make_async_copy(context_ref.at[:, columns], context, inputs.at[1]),
    ]
    for fetch in fetches:
        fetch.start()
    me, member = group_place("section", here)
    others = [lax.rem(me + d, 4) for d in range(1, 4)]
    across = [{**here, "m": 1 - here["m"], "c": lax.rem(here["c"] + d, 2)} for d in range(2)]
    greet(axis_peers(PLAIN + "c", here) + [device_at(PLAIN, place) for place in across], here)

    swaps = [
        Swap(here, a, b, swap_send.at[i], swap_recv.at[i], swap_local.at[i])
        for i, (a, b) in enumerate(((dq_ref, dq_home), (dv_own, dv_home)))
    ]
    at_v, at_up = 7 * len(dv_pieces), 5 * len(up_pieces)
    swaps[0].start()
    Scatter(here, PAIRED, dv_pieces, dv_ref, dv_own, v_send, v_recv, bufs[:at_v]).run()
    swaps[1].start()

    def up_rows(j, block):
        block = (adapter_scale * block).astype(bf16)
        for i in range(8):
            slot, third = divmod(j * 8 + i, 3)
            up_x[slot // 16, (slot // 4) % 4, slot % 4, 16 * third : 16 * third + 16, :] = block[
                16 * i : 16 * i + 16
            ]

    swaps[0].wait()
    for j in range(HEADS_HERE):
        up_rows(j, contract(query_low[...], dq_home[:, j * HD : (j + 1) * HD], 0, 0))
    up_x[1, 2:] = jnp.zeros_like(up_x[1, 2:])
    backs[:slots, :] = (adapter_scale * contract(dq_home[...], query_up_ref[...], 1, 1)).astype(bf16)
    swaps[1].wait()
    up_rows(HEADS_HERE, contract(value_low[...], dv_home[...], 0, 0))
    backs[slots:, :] = (adapter_scale * contract(dv_home[...], value_up_ref[...], 1, 1)).astype(bf16)
    copies = [
        remote(backs, backs_in.at[d], b_send.at[d], b_recv.at[d], member(k))
        for d, k in enumerate(others)
    ]
    up = Scatter(here, PLAIN, up_pieces, up_x, own, up_send, up_recv, bufs[at_v : at_v + at_up])
    down = Scatter(here, PLAIN, pieces, down_x, result, send, recv, bufs[at_v + at_up :])
    gather = Gather(here, PLAIN, spread, own, everyone, (g_send, g_recv, g_fore, g_back), 0)

    def stage(scatter, phase):
        for i in range(len(scatter.pieces)):
            if phase:
                scatter.total(phase - 1, i)
            if phase < 3:
                scatter.launch(phase, i)

    def spread_on(phase):
        for i in range(len(spread)):
            if phase:
                gather.arrived(phase - 1, i)
            gather.launch(phase, i)

    stage(up, 0)
    for copy in copies:
        copy.wait()
    whole = backs[...].astype(f32)
    for d in range(3):
        whole = whole + backs_in[d].astype(f32)
    whole = whole.astype(bf16)
    pair = jnp.concatenate([whole[:slots], whole[slots + tok :]], axis=1)
    for fetch in fetches:
        fetch.wait()
    span = memory.shape[1] // 2
    rows = span // 16
    for y in range(2):
        both = contract(memory[:, y * span : (y + 1) * span], pair, 0, 0)
        more = contract(context[:, y * span : (y + 1) * span], whole[slots : slots + tok], 0, 0)
        down_x[y, :, :, :rows, :] = both[:, :HD].astype(bf16).reshape(4, 4, rows, HD)
        down_x[y, :, :, rows:, :] = (both[:, HD:] + more).astype(bf16).reshape(4, 4, rows, HD)
    stage(down, 0)
    stage(up, 1)
    stage(up, 2)
    stage(down, 1)
    stage(up, 3)
    copy = pltpu.make_async_copy(own, everyone.at[gather.place], local)
    copy.start()
    spread_on(0)
    stage(down, 2)
    copy.wait()
    spread_on(1)
    spread_on(2)
    stage(down, 3)
    qa_ref[...] = result[:rows, :]
    va_ref[...] = result[rows:, :]
    gather.finish()
    for j in range(HEADS_HERE + 1):
        for i in range(8):
            slot, third = divmod(j * 8 + i, 3)
            tile = everyone[slot // 16, (slot // 4) % 4, slot % 4, 16 * third : 16 * third + 16, :]
            if j < HEADS_HERE:
                query_up_out[16 * i : 16 * i + 16, j * HD : (j + 1) * HD] = tile
            else:
                value_up_out[16 * i : 16 * i + 16, :] = tile
    for one in up.copies + down.copies:
        one.wait_send()


def tail(dv_part, d_queries, query_low, value_low, query_up_map, value_up_map, memory, context, collective_id):
    f32, bf16 = jnp.float32, jnp.bfloat16
    _, keys, _ = dv_part.shape
    slots, tok = memory.shape[0], context.shape[0]
    width = memory.shape[1] // 4
    rows = width // 32
    dv_pieces, dv_sems, dv_bufs = scatter_plan(keys, HD, PAIRED)
    pieces, sems, bufs = scatter_plan(2 * rows, HD, PLAIN)
    up_pieces, up_sems, up_bufs = scatter_plan(48, HD, PLAIN)
    spread = cut(48, HD, ORDERS[PLAIN])
    dma = pltpu.SemaphoreType.DMA
    return pl.pallas_call(
        functools.partial(tail_kernel, dv_pieces, pieces, up_pieces, spread),
        out_shape=(
            jax.ShapeDtypeStruct((rows, HD), f32),
            jax.ShapeDtypeStruct((rows, HD), f32),
            jax.ShapeDtypeStruct(query_up_map.shape, f32),
            jax.ShapeDtypeStruct(value_up_map.shape, f32),
        ),
        in_specs=[VMEM, ANY, VMEM, VMEM, VMEM, VMEM, ANY, ANY],
        out_specs=(VMEM,) * 4,
        scratch_shapes=[
            pltpu.VMEM((keys, HD), bf16),
            pltpu.VMEM((keys, HD), bf16),
            pltpu.VMEM(d_queries.shape, bf16),
            pltpu.VMEM((tok, width), bf16),
            pltpu.VMEM((slots, width), bf16),
            pltpu.VMEM((slots + keys, HD), bf16),
            pltpu.VMEM((3, slots + keys, HD), bf16),
            pltpu.VMEM((2, 4, 4, 2 * rows, HD), bf16),
            pltpu.VMEM((2, 4, 4, 48, HD), bf16),
            pltpu.VMEM((48, HD), f32),
            pltpu.VMEM((2, 4, 4, 48, HD), f32),
            pltpu.VMEM((2 * rows, HD), f32),
            *dv_sems,
            dma((2,)),
            dma((2,)),
            dma((2,)),
            dma((2,)),
            dma((3,)),
            dma((3,)),
            *sems,
            *up_sems,
            *semaphores(9 * len(spread) + 1),
            dma,
            *dv_bufs,
            *up_bufs,
            *bufs,
        ],
        compiler_params=pltpu.CompilerParams(
            collective_id=collective_id, has_side_effects=True, vmem_limit_bytes=40 << 20
        ),
        name="tail",
    )(
        split_axes(dv_part, PAIRED), d_queries, query_low, value_low, query_up_map, value_up_map,
        memory, context,
    )


def middle_kernel(
    pieces, scatter_pieces, total_slots, x_ref, wo_ref, ng_ref, gain_ref, o_ref, normed_out,
    everyone, part, inbox, hidden, grads, d_part, normed, stat, near_in, far_in,
    send, recv, fore, back, local, h_send, h_recv, s_send, s_recv, g_send, g_recv,
    swap_send, swap_recv, swap_local, r_send, r_recv, *bufs,
):
    f32, bf16 = jnp.float32, jnp.bfloat16
    here = coords(PAIRED)
    me, member = group_place("paired section", here)
    others = [lax.rem(me + d, 4) for d in range(1, 4)]
    near = [{**here, "h": lax.rem(here["h"] + a, 2), "c": lax.rem(here["c"] + b, 2)} for a, b in ((0, 1), (1, 0), (1, 1))]
    far = [
        {**here, "y": lax.rem(here["y"] + a, 2), "z": lax.rem(here["z"] + b, 4)}
        for a in range(2)
        for b in range(4)
        if a or b
    ]
    devices = [member(k) for k in others] + [device_at(PAIRED, place) for place in near + far]
    greet(devices, here)

    gather = Gather(here, PAIRED, pieces, x_ref, everyone, (send, recv, fore, back), 0)
    own = pltpu.make_async_copy(x_ref, everyone.at[gather.place], local)
    own.start()
    run_gathers([gather], [own], lambda phase: None)

    def slab(ref, k):
        return ref.at[k // 2, pl.ds(2 * (k % 2), 2)]

    copies = []
    for d in (2, 1, 3, 0):
        k = lax.rem(me + d, 4)
        rows = slab(everyone, k)[...].reshape(ROWS, x_ref.shape[1])
        part[k] = jnp.dot(rows, wo_ref[...], preferred_element_type=f32).astype(bf16)
        if d:
            copies.append(
                remote(part.at[k], inbox.at[d - 1], h_send.at[d - 1], h_recv.at[d - 1], member(k))
            )
    scaled = (total_slots ** (-0.5)) * ng_ref[...].astype(f32) * gain_ref[...]
    for copy in copies:
        copy.wait()
    summed = part[me].astype(f32)
    for d in range(3):
        summed = summed + inbox[d].astype(f32)
    hidden[...] = summed

    ones = jnp.ones((8, summed.shape[1]), f32)
    row_sums = lambda v: lax.dot_general(
        ones, v, (((1,), (1,)), ((), ())), preferred_element_type=f32, precision=lax.Precision.HIGHEST
    )
    first = lax.broadcasted_iota(jnp.int32, (8, ROWS), 0) == 0
    total = jnp.where(first, row_sums(summed * summed), row_sums(scaled * summed))
    stat[0] = total
    at = 0
    for step, (places, box) in enumerate(((near, near_in), (far, far_in))):
        copies = [
            remote(stat.at[step], box.at[k], s_send.at[at + k], s_recv.at[at + k], device_at(PAIRED, place))
            for k, place in enumerate(places)
        ]
        at += len(places)
        for copy in copies:
            copy.wait()
        for k in range(len(places)):
            total = total + box[k]
        if step == 0:
            stat[1] = total
    inv = lax.rsqrt(total[0:1, :] / MODEL_DIM + epsilon)
    pull = inv * inv * inv * total[1:2, :] / MODEL_DIM
    across = lambda v: jnp.transpose(v + jnp.zeros((HD, ROWS), f32))
    inv, pull = across(inv), across(pull)
    for j in range(summed.shape[1] // HD):
        cols = slice(j * HD, (j + 1) * HD)
        value = hidden[:, cols]
        normed[:, cols] = (value * inv * gain_ref[:, cols]).astype(bf16)
        weighted = (total_slots ** (-0.5)) * ng_ref[:, cols].astype(f32) * gain_ref[:, cols]
        grads[me, :, cols] = (inv * weighted - value * pull).astype(bf16)
    copies = [
        remote(grads.at[me], grads.at[me], g_send.at[d], g_recv.at[d], member(k))
        for d, k in enumerate(others)
    ]
    swap = Swap(here, normed, normed_out, swap_send, swap_recv, swap_local)
    swap.start()

    def back_through(k):
        rows = contract(grads[k], wo_ref[...], 1, 1).astype(bf16)
        slab(d_part, k)[...] = rows.reshape(2, 2, 2, x_ref.shape[0], x_ref.shape[1])

    back_through(me)
    for d in range(3):
        copies[2 - d].wait_recv()
        back_through(lax.rem(me + 4 - (3 - d), 4))
    for copy in copies:
        copy.wait_send()
    Scatter(here, PAIRED, scatter_pieces, d_part, o_ref, r_send, r_recv, bufs).run()
    swap.wait()


def middle(x, output_weight, normed_gradient, gain, total_slots, collective_id):
    bf16, f32 = jnp.bfloat16, jnp.float32
    rows, cols = x.shape
    width = output_weight.shape[1]
    pieces = cut(rows, cols, ORDERS[PAIRED])
    scatter_pieces, sems, bufs = scatter_plan(rows, cols, PAIRED)
    sizes = [SIZES[a] for a in PAIRED]
    dma = pltpu.SemaphoreType.DMA
    return pl.pallas_call(
        functools.partial(middle_kernel, pieces, scatter_pieces, total_slots),
        out_shape=(
            jax.ShapeDtypeStruct(x.shape, bf16),
            jax.ShapeDtypeStruct(normed_gradient.shape, bf16),
        ),
        in_specs=[VMEM] * 4,
        out_specs=(VMEM, ANY),
        scratch_shapes=[
            pltpu.VMEM((*sizes, rows, cols), bf16),
            pltpu.VMEM((4, ROWS, width), bf16),
            pltpu.VMEM((3, ROWS, width), bf16),
            pltpu.VMEM((ROWS, width), f32),
            pltpu.VMEM((4, ROWS, width), bf16),
            pltpu.VMEM((*sizes, rows, cols), bf16),
            pltpu.VMEM((ROWS, width), bf16),
            pltpu.VMEM((2, 8, ROWS), f32),
            pltpu.VMEM((3, 8, ROWS), f32),
            pltpu.VMEM((7, 8, ROWS), f32),
            *semaphores(9 * len(pieces) + 1),
            dma,
            dma((3,)),
            dma((3,)),
            dma((10,)),
            dma((10,)),
            dma((3,)),
            dma((3,)),
            dma,
            dma,
            dma,
            *sems,
            *bufs,
        ],
        compiler_params=pltpu.CompilerParams(
            collective_id=collective_id, has_side_effects=True, vmem_limit_bytes=32 << 20
        ),
        name="middle",
    )(x, output_weight, normed_gradient, gain)


def group_place(group, here):
    if group == "section":
        return here["m"] * 2 + here["c"], lambda k: device_at("x", {**here, "m": k // 2, "c": k % 2})
    return here["m"] * 2 + here["l"], lambda k: device_at("h", {**here, "m": k // 2, "l": k % 2})

def contract(left, right, l, r):
    return lax.dot_general(
        left, right, (((l,), (r,)), ((), ())), preferred_element_type=jnp.float32
    )


def head_rows(ref):
    return jnp.concatenate([ref[:, h * HD : (h + 1) * HD] for h in range(HEADS_HERE)], axis=0)


def key_block(kv_ref, g, cols, context_rows, slots):
    context = kv_ref[pl.ds(g * GROUP, GROUP), :context_rows, cols]
    context = context.reshape(GROUP * context_rows, HD)
    if not slots:
        return context
    memory = kv_ref[pl.ds(g * GROUP, GROUP), context_rows:, cols]
    return jnp.concatenate([context, memory.reshape(GROUP * slots, HD)], axis=0)


def key_docs(g, bounds, context_rows, slots):
    edge = GROUP * context_rows
    token = g * edge + lax.broadcasted_iota(jnp.int32, (edge, HD), 0)
    docs = (token >= 4 * bounds[0][0:1, :]) & (token < 4 * bounds[1][0:1, :])
    if slots:
        slot = g * (GROUP * slots) + lax.broadcasted_iota(jnp.int32, (GROUP * slots, HD), 0)
        docs = jnp.concatenate(
            [
                docs.astype(jnp.float32),
                ((slot >= bounds[0][0:1, :]) & (slot < bounds[1][0:1, :])).astype(jnp.float32),
            ],
            axis=0,
        )
    return docs.astype(jnp.float32).astype(jnp.bfloat16)


def documents(docs_ref):
    starts, ends, at = [], [], 0
    for k in range(docs_ref.shape[0] - 1):
        starts.append(at)
        at = at + docs_ref[k]
        ends.append(at)
    return starts, ends


def place_rows(docs_ref, here):
    starts, ends = documents(docs_ref)
    first = docs_ref[docs_ref.shape[0] - 1]
    last = first + here - 1
    lane = lax.broadcasted_iota(jnp.int32, (8, HD), 1)
    low_lane, high_lane = jnp.zeros((8, HD), jnp.int32), jnp.zeros((8, HD), jnp.int32)
    slot = first + lax.rem(lax.broadcasted_iota(jnp.int32, (ROWS, HD), 0), here)
    low = jnp.zeros((ROWS, HD), jnp.int32)
    start, stop = 0, ends[-1]
    for k in range(len(starts)):
        low_lane = jnp.where(lane == k, starts[k], low_lane)
        high_lane = jnp.where(lane == k, ends[k], high_lane)
        low = jnp.where(slot >= starts[k], starts[k], low)
        start = jnp.where(first >= starts[k], starts[k], start)
        stop = jnp.where((last >= starts[k]) & (last < ends[k]), ends[k], stop)
    mine = low == low_lane[0:1, :]
    fill = jnp.where(mine, 0.0, mask_fill).astype(jnp.bfloat16)
    row_slot = first + lax.rem(lax.broadcasted_iota(jnp.int32, (8, ROWS), 1), here)
    unit = GROUP * here
    span = (start // unit, first // unit, (stop + unit - 1) // unit)
    return span, row_slot, (low_lane, high_lane), fill


def group_scores(keys, g, q_wide, row_slot, bounds, context_rows, slots, causal):
    docs = key_docs(g, bounds, context_rows, slots)
    scores = contract(jnp.concatenate([keys, docs], axis=1), q_wide, 1, 1)
    if not causal:
        return scores
    edge = GROUP * context_rows
    slot = g * (GROUP * slots) + lax.broadcasted_iota(jnp.int32, (GROUP * slots, ROWS), 0)
    return jnp.concatenate(
        [scores[:edge], jnp.where(slot <= row_slot[0:1, :], scores[edge:], mask_fill)], axis=0
    )


def over_groups(span, step):
    first, own, last = span[0], span[1], span[2]

    def before(g, carry):
        step(g, False, True)
        return carry

    def after(g, carry):
        step(g, False, False)
        return carry

    step(own, True, True)
    lax.fori_loop(first, own, before, 0)
    lax.fori_loop(own + 1, last, after, 0)


def attend_kernel(
    context_rows, docs_ref, q_ref, kv_ref, o_ref, ot_ref, top_ref, mass_ref
):
    slots = kv_ref.shape[1] - context_rows
    span, row_slot, bounds, fill = place_rows(docs_ref, q_ref.shape[0])
    q = jnp.concatenate([head_rows(q_ref), fill], axis=1)
    ot_ref[...] = jnp.zeros_like(ot_ref)
    top_ref[...] = jnp.full_like(top_ref, mask_fill)
    mass_ref[...] = jnp.zeros_like(mass_ref)

    def step(g, masked, with_memory):
        extra = slots if with_memory else 0
        keys = key_block(kv_ref, g, slice(0, HD), context_rows, extra)
        scores = group_scores(keys, g, q, row_slot, bounds, context_rows, extra, masked)
        before = top_ref[0:1, :]
        top = jnp.maximum(before, jnp.max(scores, axis=0, keepdims=True))
        keep = jnp.exp2((before - top) * exp2_scale)
        weight = jnp.exp2((scores - top) * exp2_scale)
        top_ref[0:1, :] = top
        mass_ref[0:1, :] = mass_ref[0:1, :] * keep + jnp.sum(weight, axis=0, keepdims=True)
        values = key_block(kv_ref, g, slice(HD, 2 * HD), context_rows, extra)
        ot_ref[...] = ot_ref[...] * keep + contract(values, weight.astype(jnp.bfloat16), 0, 0)

    over_groups(span, step)
    ot_ref[...] = ot_ref[...] / mass_ref[0:1, :]
    rows = jnp.transpose(ot_ref[...]).astype(jnp.bfloat16)
    here = q_ref.shape[0]
    for h in range(HEADS_HERE):
        o_ref[:, h * HD : (h + 1) * HD] = rows[h * here : (h + 1) * here]


def backward_kernel(
    context_rows, docs_ref, q_ref, g_ref, kv_ref, ot_ref, top_ref, mass_ref,
    dq_ref, dv_ref, acc,
):
    slots = kv_ref.shape[1] - context_rows
    edge = GROUP * context_rows
    span, row_slot, bounds, fill = place_rows(docs_ref, q_ref.shape[0])
    q = jnp.concatenate([head_rows(q_ref), fill], axis=1)
    grad = head_rows(g_ref)
    center = jnp.sum(jnp.transpose(grad.astype(jnp.float32)) * ot_ref[...], axis=0, keepdims=True)
    top = top_ref[0:1, :]
    share = 1.0 / mass_ref[0:1, :]
    acc[...] = jnp.zeros_like(acc)
    dv_ref[...] = jnp.zeros_like(dv_ref)

    def step(g, masked, with_memory):
        extra = slots if with_memory else 0
        keys = key_block(kv_ref, g, slice(0, HD), context_rows, extra)
        scores = group_scores(keys, g, q, row_slot, bounds, context_rows, extra, masked)
        probs = jnp.exp2((scores - top) * exp2_scale) * share
        values = key_block(kv_ref, g, slice(HD, 2 * HD), context_rows, extra)
        d_probs = contract(values, grad, 1, 1)
        d_scores = (probs * (d_probs - center)).astype(jnp.bfloat16)
        d_values = contract(probs.astype(jnp.bfloat16), grad, 1, 0).astype(jnp.bfloat16)
        dv_ref[pl.ds(g * GROUP, GROUP), :context_rows, :] = d_values[:edge].reshape(
            GROUP, context_rows, HD
        )
        if with_memory:
            dv_ref[pl.ds(g * GROUP, GROUP), context_rows:, :] = d_values[edge:].reshape(
                GROUP, slots, HD
            )
        acc[...] += contract(keys, d_scores, 0, 0)

    over_groups(span, step)
    rows = jnp.transpose(acc[...] * score_scale).astype(jnp.bfloat16)
    here = q_ref.shape[0]
    for h in range(HEADS_HERE):
        dq_ref[:, h * HD : (h + 1) * HD] = rows[h * here : (h + 1) * here]


SMEM = pl.BlockSpec(memory_space=pltpu.SMEM)
BIG = pltpu.CompilerParams(vmem_limit_bytes=48 << 20)


def attend(docs, q, kv, context_rows):
    f32 = jnp.float32
    return pl.pallas_call(
        functools.partial(attend_kernel, context_rows),
        out_shape=(
            jax.ShapeDtypeStruct(q.shape, jnp.bfloat16),
            jax.ShapeDtypeStruct((HD, ROWS), f32),
            jax.ShapeDtypeStruct((8, ROWS), f32),
            jax.ShapeDtypeStruct((8, ROWS), f32),
        ),
        in_specs=[SMEM] + [VMEM] * 2,
        out_specs=(VMEM, VMEM, VMEM, VMEM),
        compiler_params=BIG,
        name="attend",
    )(docs, q, kv)


def attend_backward(docs, q, grad, kv, ot, top, mass, context_rows):
    return pl.pallas_call(
        functools.partial(backward_kernel, context_rows),
        out_shape=(
            jax.ShapeDtypeStruct(q.shape, jnp.bfloat16),
            jax.ShapeDtypeStruct((*kv.shape[:2], HD), jnp.bfloat16),
        ),
        in_specs=[SMEM] + [VMEM] * 6,
        out_specs=(VMEM, VMEM),
        scratch_shapes=[pltpu.VMEM((HD, ROWS), jnp.float32)],
        compiler_params=BIG,
        name="attend_backward",
    )(docs, q, grad, kv, ot, top, mass)


def body(
    context,
    memory,
    query_weight,
    key_weight,
    value_weight,
    query_down_map,
    query_up_map,
    value_down_map,
    value_up_map,
    output_weight,
    decoder_gain,
    document_slots,
    normed_gradient,
):
    tok_dev = context.shape[0]
    slot_dev = memory.shape[0]
    here = coords(PLAIN)
    paired_index = here["y"] * 16 + here["z"] * 4 + here["h"] * 2 + here["c"]
    docs = jnp.concatenate([document_slots, (paired_index * slot_dev).reshape(1).astype(jnp.int32)])
    kv, queries, query_low, value_low, output_weight, normed_gradient, decoder_gain = front(
        key_weight, value_weight, value_down_map, context, memory, query_weight, query_down_map,
        query_up_map, value_up_map, output_weight, normed_gradient, decoder_gain.reshape(-1, 128), 1,
    )
    attended, ot, top, mass = attend(docs, queries, kv, tok_dev)
    d_attended, normed = middle(
        attended, output_weight, normed_gradient, decoder_gain.reshape(1, -1),
        slot_dev * lax.axis_size("seq"), 2,
    )
    d_queries, dv_part = attend_backward(docs, queries, d_attended, kv, ot, top, mass, tok_dev)
    grad_qa, grad_va, query_up_gradient, value_up_gradient = tail(
        dv_part, d_queries, query_low, value_low, query_up_map, value_up_map, memory, context, 3
    )
    return (normed, grad_qa, grad_va, query_up_gradient, value_up_gradient)


def solution(mesh):
    in_specs = (
        P("seq", None),
        P("seq", None),
        P(None, "section"),
        P("seq", "section"),
        P("seq", "section"),
        P(),
        P(None, "section"),
        P("seq", None),
        P(None, "section"),
        P("section", "seq"),
        P("seq"),
        P(),
        P("section", "seq"),
    )
    out_specs = (
        P("section", "seq"),
        P(("section", "seq"), None),
        P(("section", "seq"), None),
        P(None, "section"),
        P(None, "section"),
    )
    return jax.shard_map(body, mesh=mesh, in_specs=in_specs, out_specs=out_specs, check_vma=False)
```

```python
import functools

import jax
import jax.numpy as jnp
from jax import lax
from jax.experimental import pallas as pl
from jax.experimental.pallas import tpu as pltpu
from jax.sharding import PartitionSpec as P

MODEL_DIM = 8192
HEADS_HERE = 8
HD = 128
ROWS = 512
GROUP = 2

adapter_scale = 0.25
epsilon = 1e-05
mask_fill = -1e30
score_scale = HD ** (-0.5)
exp2_scale = score_scale * 1.4426950408889634

MESH = pl.DeviceIdType.MESH
ANY = pl.BlockSpec(memory_space=pl.ANY)
VMEM = pl.BlockSpec(memory_space=pltpu.VMEM)
HBM = pl.BlockSpec(memory_space=pltpu.HBM)

SIZES = {"y": 2, "z": 4, "x": 4, "h": 2, "c": 2}
PLAIN, PAIRED = "yzx", "yzhc"


def coords(axes):
    seq, section = lax.axis_index("seq"), lax.axis_index("section")
    here = {"y": seq // 16, "z": (seq // 4) % 4, "x": seq % 4, "m": section // 2, "c": section % 2}
    here["h"], here["l"] = here["x"] // 2, here["x"] % 2
    return here


def device_at(axes, here):
    x = here["x"] if "x" in axes else here["h"] * 2 + here["l"]
    return (here["m"] * 2 + here["c"], here["y"] * 16 + here["z"] * 4 + x)


def moved(here, axis, step):
    return {**here, axis: lax.rem(here[axis] + step, SIZES[axis])}


def greet(devices, here=None):
    barrier = pltpu.get_barrier_semaphore()
    for device in devices:
        pl.semaphore_signal(barrier, inc=1, device_id=device, device_id_type=MESH)
    if here is not None:

        @pl.when(here["c"] != here["l"])
        def _():
            pl.semaphore_signal(
                barrier, inc=1, device_id=swap_device(here), device_id_type=MESH
            )

    extra = 0 if here is None else lax.rem(here["c"] + here["l"], 2)
    pl.semaphore_wait(barrier, len(devices) + extra)


def swap_device(here):
    return device_at("h", {**here, "c": here["l"], "l": here["c"]})


class Swap:
    def __init__(self, here, source, target, send, recv, local):
        self.apart = here["c"] != here["l"]
        self.there = lambda: pltpu.make_async_remote_copy(
            src_ref=source,
            dst_ref=target,
            send_sem=send,
            recv_sem=recv,
            device_id=swap_device(here),
            device_id_type=MESH,
        )
        self.stays = lambda: pltpu.make_async_copy(source, target, local)

    def start(self):
        @pl.when(self.apart)
        def _():
            self.there().start()

        @pl.when(jnp.logical_not(self.apart))
        def _():
            self.stays().start()

    def wait(self):
        @pl.when(self.apart)
        def _():
            self.there().wait()

        @pl.when(jnp.logical_not(self.apart))
        def _():
            self.stays().wait()


def axis_peers(axes, here):
    return [device_at(axes, moved(here, a, d)) for a in axes for d in range(1, SIZES[a])]


def remote(source, target, send, recv, device):
    copy = pltpu.make_async_remote_copy(
        src_ref=source,
        dst_ref=target,
        send_sem=send,
        recv_sem=recv,
        device_id=device,
        device_id_type=MESH,
    )
    copy.start()
    return copy


class Gather:
    def __init__(self, here, axes, pieces, source, target, sems, base):
        self.here, self.axes, self.pieces, self.base = here, axes, pieces, base
        self.source, self.target = source, target
        self.send, self.recv, self.fore, self.back = sems
        self.place = tuple(here[a] for a in axes)
        self.paired = "c" in axes
        self.partner = device_at(axes, moved(here, "c", 1)) if self.paired else None
        self.copies, self.latest, self.passed = [], {}, []

    def at(self, phase, i, d):
        return self.base + (i * 3 + phase) * 3 + d

    def begin(self):
        if self.paired:
            own = self.target.at[self.place]
            sem = self.base + 9 * len(self.pieces)
            self.passed.append(
                remote(
                    own if self.source is None else self.source,
                    own,
                    self.fore.at[sem],
                    self.back.at[sem],
                    self.partner,
                )
            )

    def arrived(self, phase, i):
        part, order = self.pieces[i]
        axis = order[phase]
        for d, copy in enumerate(self.latest[i]):
            copy.wait_recv()
            if self.paired:
                came = {**self.here, axis: lax.rem(self.here[axis] + SIZES[axis] - d - 1, SIZES[axis])}
                region = self.target.at[
                    tuple(slice(None) if a in order[:phase] else came[a] for a in self.axes)
                    + part
                ]
                at = self.at(phase, i, d)
                self.passed.append(
                    remote(region, region, self.fore.at[at], self.back.at[at], self.partner)
                )

    def launch(self, phase, i):
        part, order = self.pieces[i]
        held = tuple(slice(None) if a in order[:phase] else self.here[a] for a in self.axes)
        region = self.target.at[held + part]
        source = region if phase or self.source is None else self.source.at[part]
        self.latest[i] = []
        for d in range(1, SIZES[order[phase]]):
            at = self.at(phase, i, d - 1)
            device = device_at(self.axes, moved(self.here, order[phase], d))
            self.latest[i].append(remote(source, region, self.send.at[at], self.recv.at[at], device))
        self.copies += self.latest[i]

    def finish(self):
        for i in range(len(self.pieces)):
            self.arrived(2, i)
        for copy in self.passed:
            copy.wait_recv()
        for copy in self.copies + self.passed:
            copy.wait_send()


def run_gathers(gathers, owns, between):
    for gather in gathers:
        gather.begin()
    for phase in range(3):
        for gather in gathers:
            for i in range(len(gather.pieces)):
                if phase:
                    gather.arrived(phase - 1, i)
                    if phase == 1:
                        while owns:
                            owns.pop().wait()
                gather.launch(phase, i)
        between(phase)
    for gather in gathers:
        gather.finish()


def semaphores(count):
    return [pltpu.SemaphoreType.DMA((count,)) for _ in range(4)]


def front_kernel(
    pieces, half_pieces, kv_pieces,
    key_ref, value_ref, down_ref, context_ref, memory_ref, weight_ref, query_down_ref, query_up_ref,
    value_up_ref, wo_ref, ng_ref, gain_ref,
    kv_all, q_out, query_low, value_low, wo_out, ng_out, gain_out,
    shard, w_all, d_all, context, memory, query_down, buffer, acc, projected, kv_own, q_own,
    send, recv, fore, back, k_send, k_recv, k_fore, k_back,
    loads, inputs, local, swap_send, swap_recv, swap_local,
):
    f32, bf16 = jnp.float32, jnp.bfloat16
    here = coords(PLAIN)
    depth = buffer.shape[1]
    count = weight_ref.shape[0] // depth
    half = down_ref.shape[0] // 2
    tok = context_ref.shape[0]

    def load(k):
        return pltpu.make_async_copy(
            weight_ref.at[pl.ds(k * depth, depth)], buffer.at[k % 3], loads.at[k % 3]
        )

    own_half = down_ref.at[pl.ds(here["c"] * half, half)]
    fetches = [
        pltpu.make_async_copy(a, b, inputs.at[i])
        for i, (a, b) in enumerate(
            (
                (key_ref, shard.at[:, pl.ds(0, HD)]),
                (value_ref, shard.at[:, pl.ds(HD, HD)]),
                (memory_ref, memory),
                (query_down_ref, query_down),
                (context_ref, context),
            )
        )
    ]
    for fetch in fetches:
        fetch.start()
    for k in range(2):
        load(k).start()
    greet(axis_peers(PLAIN + "c", here), here)
    swaps = [
        Swap(here, a, b, swap_send.at[i], swap_recv.at[i], swap_local.at[i])
        for i, (a, b) in enumerate(
            (
                (kv_own, kv_all.at[here["y"], here["z"], here["h"], here["l"]]),
                (q_own, q_out),
                (gain_ref, gain_out),
                (ng_ref, ng_out),
                (wo_ref, wo_out),
            )
        )
    ]
    fetches[0].wait()
    fetches[1].wait()
    sems = (send, recv, fore, back)
    plain = Gather(here, PLAIN, pieces, shard, w_all, sems, 0)
    shared = Gather(here, PLAIN + "c", half_pieces, own_half, d_all, sems, 9 * len(pieces) + 1)
    owns = [
        pltpu.make_async_copy(shard, w_all.at[plain.place], local.at[0]),
        pltpu.make_async_copy(own_half, d_all.at[shared.place], local.at[1]),
    ]
    for own in owns:
        own.start()

    def between(phase):
        if phase < 2:
            return
        fetches[2].wait()
        fetches[3].wait()
        low = jnp.dot(memory[...], query_down[...], preferred_element_type=f32).astype(bf16)
        query_low[...] = low
        acc[...] = adapter_scale * jnp.dot(low, query_up_ref[...], preferred_element_type=f32)
        for k in range(count):
            load(k).wait()
            if k + 2 < count:
                load(k + 2).start()
            acc[...] += jnp.dot(
                memory[:, k * depth : (k + 1) * depth], buffer[k % 3], preferred_element_type=f32
            )
        q_own[...] = acc[...].astype(bf16)
        fetches[4].wait()

    run_gathers([plain, shared], owns, between)
    swaps[4].start()
    wide = 4 * shard.shape[0]
    for j in range(8):
        at = (j // 4, j % 4)
        kv_rows = w_all[at].reshape(wide, 2 * HD)
        down_rows = d_all[at].reshape(wide, HD)
        for rows, source in ((slice(0, tok), context), (slice(tok, None), memory)):
            part = source[:, j * wide : (j + 1) * wide]
            for cols, right in ((slice(0, 2 * HD), kv_rows), (slice(2 * HD, None), down_rows)):
                step = jnp.dot(part, right, preferred_element_type=f32)
                projected[rows, cols] = step if j == 0 else projected[rows, cols] + step
    low = projected[:, 2 * HD :].astype(bf16)
    value_low[...] = low
    kv_own[:, :HD] = projected[:, :HD].astype(bf16)
    kv_own[:, HD:] = (
        projected[:, HD : 2 * HD]
        + adapter_scale * jnp.dot(low, value_up_ref[...], preferred_element_type=f32)
    ).astype(bf16)
    swaps[0].start()
    swaps[0].wait()
    gather = Gather(here, PAIRED, kv_pieces, None, kv_all, (k_send, k_recv, k_fore, k_back), 0)

    def rest(phase):
        if phase == 2:
            for swap in swaps[1:4]:
                swap.start()

    run_gathers([gather], [], rest)
    for swap in swaps[1:]:
        swap.wait()


def front(
    key_weight, value_weight, down, context, memory, query_weight, query_down, query_up, value_up,
    output_weight, normed_gradient, gain, collective_id,
):
    f32, bf16 = jnp.float32, jnp.bfloat16
    rows, half = key_weight.shape[0], down.shape[0] // 2
    tok, slots, model = context.shape[0], memory.shape[0], memory.shape[1]
    keys, wide = tok + slots, query_weight.shape[1]
    pieces = cut(rows, 2 * HD, ORDERS[PLAIN])
    half_pieces = cut(half, HD, ORDERS[PLAIN][:3])
    kv_pieces = cut(keys, 2 * HD, ORDERS[PAIRED])
    n = 9 * len(pieces) + 1 + 9 * len(half_pieces) + 1
    like = lambda a: jax.ShapeDtypeStruct(a.shape, a.dtype)
    sizes = [SIZES[a] for a in PAIRED]
    dma = pltpu.SemaphoreType.DMA
    kv, *rest = pl.pallas_call(
        functools.partial(front_kernel, pieces, half_pieces, kv_pieces),
        out_shape=(
            jax.ShapeDtypeStruct((*sizes, keys, 2 * HD), bf16),
            jax.ShapeDtypeStruct((slots, wide), bf16),
            jax.ShapeDtypeStruct((slots, HD), bf16),
            jax.ShapeDtypeStruct((keys, HD), bf16),
            like(output_weight),
            like(normed_gradient),
            like(gain),
        ),
        in_specs=[ANY] * 7 + [VMEM] * 2 + [ANY] * 3,
        out_specs=(ANY, ANY, VMEM, VMEM, ANY, ANY, ANY),
        scratch_shapes=[
            pltpu.VMEM((rows, 2 * HD), bf16),
            pltpu.VMEM((2, 4, 4, rows, 2 * HD), bf16),
            pltpu.VMEM((2, 4, 4, 2, half, HD), bf16),
            pltpu.VMEM((tok, model), bf16),
            pltpu.VMEM((slots, model), bf16),
            pltpu.VMEM((model, HD), bf16),
            pltpu.VMEM((3, 1024, wide), bf16),
            pltpu.VMEM((slots, wide), f32),
            pltpu.VMEM((keys, 3 * HD), f32),
            pltpu.VMEM((keys, 2 * HD), bf16),
            pltpu.VMEM((slots, wide), bf16),
            *semaphores(n),
            *semaphores(9 * len(kv_pieces) + 1),
            dma((3,)),
            dma((5,)),
            dma((2,)),
            dma((5,)),
            dma((5,)),
            dma((5,)),
        ],
        compiler_params=pltpu.CompilerParams(
            collective_id=collective_id, has_side_effects=True, vmem_limit_bytes=61 << 20
        ),
        name="front",
    )(
        key_weight, value_weight, down, context, memory, query_weight, query_down, query_up, value_up,
        output_weight, normed_gradient, gain,
    )
    return kv.reshape(32, keys, 2 * HD), *rest


ORDERS = {
    PLAIN: ("xzy", "zyx", "yxz", "zxy", "yzx", "xyz"),
    PAIRED: ("hzy", "zyh", "yhz", "zhy", "yzh", "hyz"),
}


def cut(rows, cols, orders):
    by_rows = rows // 16 >= 2 * len(orders) or cols == 128
    step = 16 if by_rows else 128
    units = (rows if by_rows else cols) // step
    base, extra = divmod(units, len(orders))
    pieces, at = [], 0
    for i, order in enumerate(orders):
        size = (base + (1 if i < extra else 0)) * step
        if size:
            part = (pl.ds(at, size), pl.ds(0, cols)) if by_rows else (pl.ds(0, rows), pl.ds(at, size))
            pieces.append((part, order))
        at += size
    return pieces


class Scatter:
    def __init__(self, here, axes, pieces, x_ref, o_ref, send, recv, bufs):
        self.here, self.axes, self.pieces, self.x, self.o = here, axes, pieces, x_ref, o_ref
        self.send, self.recv, self.depth = send, recv, len(axes)
        n, depth = len(pieces), len(axes)
        self.inbox = [bufs[depth * i : depth * (i + 1)] for i in range(n)]
        self.partial = [bufs[depth * n + (depth - 1) * i :][: depth - 1] for i in range(n)]
        self.copies, self.latest = [], {}

    def block(self, phase, i, coord):
        part, order = self.pieces[i]
        left = [a for a in self.axes if a not in order[:phase]]
        ref = self.partial[i][phase - 1] if phase else self.x
        tail = () if phase else part
        return ref.at[tuple(coord if a == order[phase] else slice(None) for a in left) + tail]

    def launch(self, phase, i):
        axis = self.pieces[i][1][phase]
        self.latest[i] = []
        for d in range(1, SIZES[axis]):
            at = (i * self.depth + phase) * 3 + d - 1
            self.latest[i].append(
                remote(
                    self.block(phase, i, lax.rem(self.here[axis] + d, SIZES[axis])),
                    self.inbox[i][phase].at[d - 1],
                    self.send.at[at],
                    self.recv.at[at],
                    device_at(self.axes, moved(self.here, axis, d)),
                )
            )
        self.copies.extend(self.latest[i])

    def total(self, phase, i):
        part, order = self.pieces[i]
        axis = order[phase]
        for copy in self.latest[i]:
            copy.wait_recv()
        mine, inbox = self.block(phase, i, self.here[axis]), self.inbox[i][phase]
        left = [SIZES[a] for a in self.axes if a not in order[: phase + 1]]
        count = 1
        for extent in left:
            count *= extent

        def add(k, carry):
            at = ()
            for extent in reversed(left):
                at, k = (k % extent,) + at, k // extent
            whole = mine[at].astype(jnp.float32) if at else mine[...].astype(jnp.float32)
            for d in range(SIZES[axis] - 1):
                whole = whole + inbox[(d,) + at].astype(jnp.float32)
            if phase == self.depth - 1:
                self.o[part] = whole.astype(self.o.dtype)
            else:
                self.partial[i][phase][at] = whole.astype(jnp.bfloat16)
            return carry

        if count == 1:
            add(0, 0)
        else:
            lax.fori_loop(0, count, add, 0)

    def run(self):
        for i in range(len(self.pieces)):
            self.launch(0, i)
        for phase in range(self.depth):
            for i in range(len(self.pieces)):
                self.total(phase, i)
                if phase < self.depth - 1:
                    self.launch(phase + 1, i)
        for copy in self.copies:
            copy.wait_send()


def scatter_plan(rows, cols, axes):
    first = "c" if axes == PAIRED else ""
    pieces = cut(rows, cols, [first + order[::-1] for order in ORDERS[axes]])
    depth = len(axes)
    n = 3 * depth * len(pieces)
    inboxes, partials = [], []
    for part, order in pieces:
        size = tuple(edge.size for edge in part)
        for phase in range(depth):
            left = [SIZES[a] for a in axes if a not in order[: phase + 1]]
            inboxes.append(pltpu.VMEM((SIZES[order[phase]] - 1, *left, *size), jnp.bfloat16))
            if phase < depth - 1:
                partials.append(pltpu.VMEM((*left, *size), jnp.bfloat16))
    sems = [pltpu.SemaphoreType.DMA((n,)), pltpu.SemaphoreType.DMA((n,))]
    return pieces, sems, inboxes + partials


def split_axes(x, axes):
    return x.reshape(*[SIZES[a] for a in axes], *x.shape[1:])


def tail_kernel(
    dv_pieces, pieces, up_pieces, spread,
    dv_ref, dq_ref, query_low, value_low, query_up_ref, value_up_ref, memory_ref, context_ref,
    qa_ref, va_ref, query_up_out, value_up_out,
    dv_own, dv_home, dq_home, context, memory, backs, backs_in, down_x, up_x, own, everyone, result,
    v_send, v_recv, swap_send, swap_recv, swap_local, inputs, b_send, b_recv,
    send, recv, up_send, up_recv, g_send, g_recv, g_fore, g_back, local, *bufs,
):
    f32, bf16 = jnp.float32, jnp.bfloat16
    here = coords(PAIRED)
    slots = memory.shape[0]
    tok = context.shape[0]
    columns = pl.ds(lax.axis_index("section") * memory.shape[1], memory.shape[1])
    fetches = [
        pltpu.make_async_copy(memory_ref.at[:, columns], memory, inputs.at[0]),
        pltpu.make_async_copy(context_ref.at[:, columns], context, inputs.at[1]),
    ]
    for fetch in fetches:
        fetch.start()
    me, member = group_place("section", here)
    others = [lax.rem(me + d, 4) for d in range(1, 4)]
    across = [{**here, "m": 1 - here["m"], "c": lax.rem(here["c"] + d, 2)} for d in range(2)]
    greet(axis_peers(PLAIN + "c", here) + [device_at(PLAIN, place) for place in across], here)

    swaps = [
        Swap(here, a, b, swap_send.at[i], swap_recv.at[i], swap_local.at[i])
        for i, (a, b) in enumerate(((dq_ref, dq_home), (dv_own, dv_home)))
    ]
    at_v, at_up = 7 * len(dv_pieces), 5 * len(up_pieces)
    swaps[0].start()
    Scatter(here, PAIRED, dv_pieces, dv_ref, dv_own, v_send, v_recv, bufs[:at_v]).run()
    swaps[1].start()

    def up_rows(j, block):
        block = (adapter_scale * block).astype(bf16)
        for i in range(8):
            slot, third = divmod(j * 8 + i, 3)
            up_x[slot // 16, (slot // 4) % 4, slot % 4, 16 * third : 16 * third + 16, :] = block[
                16 * i : 16 * i + 16
            ]

    swaps[0].wait()
    for j in range(HEADS_HERE):
        up_rows(j, contract(query_low[...], dq_home[:, j * HD : (j + 1) * HD], 0, 0))
    up_x[1, 2:] = jnp.zeros_like(up_x[1, 2:])
    backs[:slots, :] = (adapter_scale * contract(dq_home[...], query_up_ref[...], 1, 1)).astype(bf16)
    swaps[1].wait()
    up_rows(HEADS_HERE, contract(value_low[...], dv_home[...], 0, 0))
    backs[slots:, :] = (adapter_scale * contract(dv_home[...], value_up_ref[...], 1, 1)).astype(bf16)
    copies = [
        remote(backs, backs_in.at[d], b_send.at[d], b_recv.at[d], member(k))
        for d, k in enumerate(others)
    ]
    up = Scatter(here, PLAIN, up_pieces, up_x, own, up_send, up_recv, bufs[at_v : at_v + at_up])
    down = Scatter(here, PLAIN, pieces, down_x, result, send, recv, bufs[at_v + at_up :])
    gather = Gather(here, PLAIN, spread, own, everyone, (g_send, g_recv, g_fore, g_back), 0)

    def stage(scatter, phase):
        for i in range(len(scatter.pieces)):
            if phase:
                scatter.total(phase - 1, i)
            if phase < 3:
                scatter.launch(phase, i)

    def spread_on(phase):
        for i in range(len(spread)):
            if phase:
                gather.arrived(phase - 1, i)
            gather.launch(phase, i)

    stage(up, 0)
    for copy in copies:
        copy.wait()
    whole = backs[...].astype(f32)
    for d in range(3):
        whole = whole + backs_in[d].astype(f32)
    whole = whole.astype(bf16)
    pair = jnp.concatenate([whole[:slots], whole[slots + tok :]], axis=1)
    for fetch in fetches:
        fetch.wait()
    span = memory.shape[1] // 2
    rows = span // 16
    for y in range(2):
        both = contract(memory[:, y * span : (y + 1) * span], pair, 0, 0)
        more = contract(context[:, y * span : (y + 1) * span], whole[slots : slots + tok], 0, 0)
        down_x[y, :, :, :rows, :] = both[:, :HD].astype(bf16).reshape(4, 4, rows, HD)
        down_x[y, :, :, rows:, :] = (both[:, HD:] + more).astype(bf16).reshape(4, 4, rows, HD)
    stage(down, 0)
    stage(up, 1)
    stage(up, 2)
    stage(down, 1)
    stage(up, 3)
    copy = pltpu.make_async_copy(own, everyone.at[gather.place], local)
    copy.start()
    spread_on(0)
    stage(down, 2)
    copy.wait()
    spread_on(1)
    spread_on(2)
    stage(down, 3)
    qa_ref[...] = result[:rows, :]
    va_ref[...] = result[rows:, :]
    gather.finish()
    for j in range(HEADS_HERE + 1):
        for i in range(8):
            slot, third = divmod(j * 8 + i, 3)
            tile = everyone[slot // 16, (slot // 4) % 4, slot % 4, 16 * third : 16 * third + 16, :]
            if j < HEADS_HERE:
                query_up_out[16 * i : 16 * i + 16, j * HD : (j + 1) * HD] = tile
            else:
                value_up_out[16 * i : 16 * i + 16, :] = tile
    for one in up.copies + down.copies:
        one.wait_send()


def tail(dv_part, d_queries, query_low, value_low, query_up_map, value_up_map, memory, context, collective_id):
    f32, bf16 = jnp.float32, jnp.bfloat16
    _, keys, _ = dv_part.shape
    slots, tok = memory.shape[0], context.shape[0]
    width = memory.shape[1] // 4
    rows = width // 32
    dv_pieces, dv_sems, dv_bufs = scatter_plan(keys, HD, PAIRED)
    pieces, sems, bufs = scatter_plan(2 * rows, HD, PLAIN)
    up_pieces, up_sems, up_bufs = scatter_plan(48, HD, PLAIN)
    spread = cut(48, HD, ORDERS[PLAIN])
    dma = pltpu.SemaphoreType.DMA
    return pl.pallas_call(
        functools.partial(tail_kernel, dv_pieces, pieces, up_pieces, spread),
        out_shape=(
            jax.ShapeDtypeStruct((rows, HD), f32),
            jax.ShapeDtypeStruct((rows, HD), f32),
            jax.ShapeDtypeStruct(query_up_map.shape, f32),
            jax.ShapeDtypeStruct(value_up_map.shape, f32),
        ),
        in_specs=[VMEM, ANY, VMEM, VMEM, VMEM, VMEM, ANY, ANY],
        out_specs=(VMEM,) * 4,
        scratch_shapes=[
            pltpu.VMEM((keys, HD), bf16),
            pltpu.VMEM((keys, HD), bf16),
            pltpu.VMEM(d_queries.shape, bf16),
            pltpu.VMEM((tok, width), bf16),
            pltpu.VMEM((slots, width), bf16),
            pltpu.VMEM((slots + keys, HD), bf16),
            pltpu.VMEM((3, slots + keys, HD), bf16),
            pltpu.VMEM((2, 4, 4, 2 * rows, HD), bf16),
            pltpu.VMEM((2, 4, 4, 48, HD), bf16),
            pltpu.VMEM((48, HD), f32),
            pltpu.VMEM((2, 4, 4, 48, HD), f32),
            pltpu.VMEM((2 * rows, HD), f32),
            *dv_sems,
            dma((2,)),
            dma((2,)),
            dma((2,)),
            dma((2,)),
            dma((3,)),
            dma((3,)),
            *sems,
            *up_sems,
            *semaphores(9 * len(spread) + 1),
            dma,
            *dv_bufs,
            *up_bufs,
            *bufs,
        ],
        compiler_params=pltpu.CompilerParams(
            collective_id=collective_id, has_side_effects=True, vmem_limit_bytes=40 << 20
        ),
        name="tail",
    )(
        split_axes(dv_part, PAIRED), d_queries, query_low, value_low, query_up_map, value_up_map,
        memory, context,
    )


def middle_kernel(
    pieces, scatter_pieces, total_slots, x_ref, wo_ref, ng_ref, gain_ref, o_ref, normed_out,
    everyone, part, inbox, hidden, grads, d_part, normed, stat, near_in, far_in,
    send, recv, fore, back, local, h_send, h_recv, s_send, s_recv, g_send, g_recv,
    swap_send, swap_recv, swap_local, r_send, r_recv, *bufs,
):
    f32, bf16 = jnp.float32, jnp.bfloat16
    here = coords(PAIRED)
    me, member = group_place("paired section", here)
    others = [lax.rem(me + d, 4) for d in range(1, 4)]
    near = [{**here, "h": lax.rem(here["h"] + a, 2), "c": lax.rem(here["c"] + b, 2)} for a, b in ((0, 1), (1, 0), (1, 1))]
    far = [
        {**here, "y": lax.rem(here["y"] + a, 2), "z": lax.rem(here["z"] + b, 4)}
        for a in range(2)
        for b in range(4)
        if a or b
    ]
    devices = [member(k) for k in others] + [device_at(PAIRED, place) for place in near + far]
    greet(devices, here)

    gather = Gather(here, PAIRED, pieces, x_ref, everyone, (send, recv, fore, back), 0)
    own = pltpu.make_async_copy(x_ref, everyone.at[gather.place], local)
    own.start()
    run_gathers([gather], [own], lambda phase: None)

    def slab(ref, k):
        return ref.at[k // 2, pl.ds(2 * (k % 2), 2)]

    copies = []
    for d in (2, 1, 3, 0):
        k = lax.rem(me + d, 4)
        rows = slab(everyone, k)[...].reshape(ROWS, x_ref.shape[1])
        part[k] = jnp.dot(rows, wo_ref[...], preferred_element_type=f32).astype(bf16)
        if d:
            copies.append(
                remote(part.at[k], inbox.at[d - 1], h_send.at[d - 1], h_recv.at[d - 1], member(k))
            )
    scaled = (total_slots ** (-0.5)) * ng_ref[...].astype(f32) * gain_ref[...]
    for copy in copies:
        copy.wait()
    summed = part[me].astype(f32)
    for d in range(3):
        summed = summed + inbox[d].astype(f32)
    hidden[...] = summed

    ones = jnp.ones((8, summed.shape[1]), f32)
    row_sums = lambda v: lax.dot_general(
        ones, v, (((1,), (1,)), ((), ())), preferred_element_type=f32, precision=lax.Precision.HIGHEST
    )
    first = lax.broadcasted_iota(jnp.int32, (8, ROWS), 0) == 0
    total = jnp.where(first, row_sums(summed * summed), row_sums(scaled * summed))
    stat[0] = total
    at = 0
    for step, (places, box) in enumerate(((near, near_in), (far, far_in))):
        copies = [
            remote(stat.at[step], box.at[k], s_send.at[at + k], s_recv.at[at + k], device_at(PAIRED, place))
            for k, place in enumerate(places)
        ]
        at += len(places)
        for copy in copies:
            copy.wait()
        for k in range(len(places)):
            total = total + box[k]
        if step == 0:
            stat[1] = total
    inv = lax.rsqrt(total[0:1, :] / MODEL_DIM + epsilon)
    pull = inv * inv * inv * total[1:2, :] / MODEL_DIM
    across = lambda v: jnp.transpose(v + jnp.zeros((HD, ROWS), f32))
    inv, pull = across(inv), across(pull)
    for j in range(summed.shape[1] // HD):
        cols = slice(j * HD, (j + 1) * HD)
        value = hidden[:, cols]
        normed[:, cols] = (value * inv * gain_ref[:, cols]).astype(bf16)
        weighted = (total_slots ** (-0.5)) * ng_ref[:, cols].astype(f32) * gain_ref[:, cols]
        grads[me, :, cols] = (inv * weighted - value * pull).astype(bf16)
    copies = [
        remote(grads.at[me], grads.at[me], g_send.at[d], g_recv.at[d], member(k))
        for d, k in enumerate(others)
    ]
    swap = Swap(here, normed, normed_out, swap_send, swap_recv, swap_local)
    swap.start()

    def back_through(k):
        rows = contract(grads[k], wo_ref[...], 1, 1).astype(bf16)
        slab(d_part, k)[...] = rows.reshape(2, 2, 2, x_ref.shape[0], x_ref.shape[1])

    back_through(me)
    for d in range(3):
        copies[2 - d].wait_recv()
        back_through(lax.rem(me + 4 - (3 - d), 4))
    for copy in copies:
        copy.wait_send()
    Scatter(here, PAIRED, scatter_pieces, d_part, o_ref, r_send, r_recv, bufs).run()
    swap.wait()


def middle(x, output_weight, normed_gradient, gain, total_slots, collective_id):
    bf16, f32 = jnp.bfloat16, jnp.float32
    rows, cols = x.shape
    width = output_weight.shape[1]
    pieces = cut(rows, cols, ORDERS[PAIRED])
    scatter_pieces, sems, bufs = scatter_plan(rows, cols, PAIRED)
    sizes = [SIZES[a] for a in PAIRED]
    dma = pltpu.SemaphoreType.DMA
    return pl.pallas_call(
        functools.partial(middle_kernel, pieces, scatter_pieces, total_slots),
        out_shape=(
            jax.ShapeDtypeStruct(x.shape, bf16),
            jax.ShapeDtypeStruct(normed_gradient.shape, bf16),
        ),
        in_specs=[VMEM] * 4,
        out_specs=(VMEM, ANY),
        scratch_shapes=[
            pltpu.VMEM((*sizes, rows, cols), bf16),
            pltpu.VMEM((4, ROWS, width), bf16),
            pltpu.VMEM((3, ROWS, width), bf16),
            pltpu.VMEM((ROWS, width), f32),
            pltpu.VMEM((4, ROWS, width), bf16),
            pltpu.VMEM((*sizes, rows, cols), bf16),
            pltpu.VMEM((ROWS, width), bf16),
            pltpu.VMEM((2, 8, ROWS), f32),
            pltpu.VMEM((3, 8, ROWS), f32),
            pltpu.VMEM((7, 8, ROWS), f32),
            *semaphores(9 * len(pieces) + 1),
            dma,
            dma((3,)),
            dma((3,)),
            dma((10,)),
            dma((10,)),
            dma((3,)),
            dma((3,)),
            dma,
            dma,
            dma,
            *sems,
            *bufs,
        ],
        compiler_params=pltpu.CompilerParams(
            collective_id=collective_id, has_side_effects=True, vmem_limit_bytes=32 << 20
        ),
        name="middle",
    )(x, output_weight, normed_gradient, gain)


def group_place(group, here):
    if group == "section":
        return here["m"] * 2 + here["c"], lambda k: device_at("x", {**here, "m": k // 2, "c": k % 2})
    return here["m"] * 2 + here["l"], lambda k: device_at("h", {**here, "m": k // 2, "l": k % 2})

def contract(left, right, l, r):
    return lax.dot_general(
        left, right, (((l,), (r,)), ((), ())), preferred_element_type=jnp.float32
    )


def head_rows(ref):
    return jnp.concatenate([ref[:, h * HD : (h + 1) * HD] for h in range(HEADS_HERE)], axis=0)


def key_block(kv_ref, g, cols, context_rows, slots):
    context = kv_ref[pl.ds(g * GROUP, GROUP), :context_rows, cols]
    context = context.reshape(GROUP * context_rows, HD)
    if not slots:
        return context
    memory = kv_ref[pl.ds(g * GROUP, GROUP), context_rows:, cols]
    return jnp.concatenate([context, memory.reshape(GROUP * slots, HD)], axis=0)


def key_docs(g, bounds, context_rows, slots):
    edge = GROUP * context_rows
    token = g * edge + lax.broadcasted_iota(jnp.int32, (edge, HD), 0)
    docs = (token >= 4 * bounds[0][0:1, :]) & (token < 4 * bounds[1][0:1, :])
    if slots:
        slot = g * (GROUP * slots) + lax.broadcasted_iota(jnp.int32, (GROUP * slots, HD), 0)
        docs = jnp.concatenate(
            [
                docs.astype(jnp.float32),
                ((slot >= bounds[0][0:1, :]) & (slot < bounds[1][0:1, :])).astype(jnp.float32),
            ],
            axis=0,
        )
    return docs.astype(jnp.float32).astype(jnp.bfloat16)


def documents(docs_ref):
    starts, ends, at = [], [], 0
    for k in range(docs_ref.shape[0] - 1):
        starts.append(at)
        at = at + docs_ref[k]
        ends.append(at)
    return starts, ends


def place_rows(docs_ref, here):
    starts, ends = documents(docs_ref)
    first = docs_ref[docs_ref.shape[0] - 1]
    last = first + here - 1
    lane = lax.broadcasted_iota(jnp.int32, (8, HD), 1)
    low_lane, high_lane = jnp.zeros((8, HD), jnp.int32), jnp.zeros((8, HD), jnp.int32)
    slot = first + lax.rem(lax.broadcasted_iota(jnp.int32, (ROWS, HD), 0), here)
    low = jnp.zeros((ROWS, HD), jnp.int32)
    start, stop = 0, ends[-1]
    for k in range(len(starts)):
        low_lane = jnp.where(lane == k, starts[k], low_lane)
        high_lane = jnp.where(lane == k, ends[k], high_lane)
        low = jnp.where(slot >= starts[k], starts[k], low)
        start = jnp.where(first >= starts[k], starts[k], start)
        stop = jnp.where((last >= starts[k]) & (last < ends[k]), ends[k], stop)
    mine = low == low_lane[0:1, :]
    fill = jnp.where(mine, 0.0, mask_fill).astype(jnp.bfloat16)
    row_slot = first + lax.rem(lax.broadcasted_iota(jnp.int32, (8, ROWS), 1), here)
    unit = GROUP * here
    span = (start // unit, first // unit, (stop + unit - 1) // unit)
    return span, row_slot, (low_lane, high_lane), fill


HALVES = (slice(0, ROWS // 2), slice(ROWS // 2, ROWS))


def group_scores(keys, docs, g, q_wide, row_slot, context_rows, slots, causal):
    scores = contract(jnp.concatenate([keys, docs], axis=1), q_wide, 1, 1)
    if not causal:
        return scores
    edge = GROUP * context_rows
    slot = g * (GROUP * slots) + lax.broadcasted_iota(
        jnp.int32, (GROUP * slots, q_wide.shape[0]), 0
    )
    return jnp.concatenate(
        [scores[:edge], jnp.where(slot <= row_slot[0:1, :], scores[edge:], mask_fill)], axis=0
    )


def group_copy(kv_hbm, kv_ref, sems, g):
    return pltpu.make_async_copy(
        kv_hbm.at[pl.ds(g * GROUP, GROUP)], kv_ref.at[pl.ds(g * GROUP, GROUP)], sems.at[g]
    )


def over_groups(span, step, fetch):
    first, own, last = span[0], span[1], span[2]

    def ask(g, carry):
        fetch(g).start()
        return carry

    def before(g, carry):
        fetch(g).wait()
        step(g, False, True)
        return carry

    def after(g, carry):
        fetch(g).wait()
        step(g, False, False)
        return carry

    fetch(own).start()
    lax.fori_loop(first, own, ask, 0)
    lax.fori_loop(own + 1, last, ask, 0)
    fetch(own).wait()
    step(own, True, True)
    lax.fori_loop(first, own, before, 0)
    lax.fori_loop(own + 1, last, after, 0)


def attend_kernel(
    context_rows, docs_ref, q_ref, kv_hbm, o_ref, ot_ref, top_ref, mass_ref, kv_ref, sems
):
    slots = kv_ref.shape[1] - context_rows
    span, row_slot, bounds, fill = place_rows(docs_ref, q_ref.shape[0])
    q = jnp.concatenate([head_rows(q_ref), fill], axis=1)
    ot_ref[...] = jnp.zeros_like(ot_ref)
    top_ref[...] = jnp.full_like(top_ref, mask_fill)
    mass_ref[...] = jnp.zeros_like(mass_ref)

    def step(g, masked, with_memory):
        extra = slots if with_memory else 0
        keys = key_block(kv_ref, g, slice(0, HD), context_rows, extra)
        values = key_block(kv_ref, g, slice(HD, 2 * HD), context_rows, extra)
        docs = key_docs(g, bounds, context_rows, extra)
        for cols in (slice(0, ROWS),):
            scores = group_scores(keys, docs, g, q[cols], row_slot[:, cols], context_rows, extra, masked)
            before = top_ref[0:1, cols]
            top = jnp.maximum(before, jnp.max(scores, axis=0, keepdims=True))
            keep = jnp.exp2((before - top) * exp2_scale)
            weight = jnp.exp2((scores - top) * exp2_scale)
            top_ref[0:1, cols] = top
            mass_ref[0:1, cols] = mass_ref[0:1, cols] * keep + jnp.sum(weight, axis=0, keepdims=True)
            ot_ref[:, cols] = ot_ref[:, cols] * keep + contract(
                values, weight.astype(jnp.bfloat16), 0, 0
            )

    over_groups(span, step, functools.partial(group_copy, kv_hbm, kv_ref, sems))
    ot_ref[...] = ot_ref[...] / mass_ref[0:1, :]
    rows = jnp.transpose(ot_ref[...]).astype(jnp.bfloat16)
    here = q_ref.shape[0]
    for h in range(HEADS_HERE):
        o_ref[:, h * HD : (h + 1) * HD] = rows[h * here : (h + 1) * here]


def backward_kernel(
    context_rows, docs_ref, q_ref, g_ref, kv_hbm, ot_ref, top_ref, mass_ref,
    dq_ref, dv_ref, acc, kv_ref, sems,
):
    slots = kv_ref.shape[1] - context_rows
    edge = GROUP * context_rows
    span, row_slot, bounds, fill = place_rows(docs_ref, q_ref.shape[0])
    q = jnp.concatenate([head_rows(q_ref), fill], axis=1)
    grad = head_rows(g_ref)
    center = jnp.sum(jnp.transpose(grad.astype(jnp.float32)) * ot_ref[...], axis=0, keepdims=True)
    top = top_ref[0:1, :]
    share = 1.0 / mass_ref[0:1, :]
    acc[...] = jnp.zeros_like(acc)
    dv_ref[...] = jnp.zeros_like(dv_ref)

    def step(g, masked, with_memory):
        extra = slots if with_memory else 0
        keys = key_block(kv_ref, g, slice(0, HD), context_rows, extra)
        values = key_block(kv_ref, g, slice(HD, 2 * HD), context_rows, extra)
        docs = key_docs(g, bounds, context_rows, extra)
        d_values = 0.0
        for cols in HALVES:
            scores = group_scores(keys, docs, g, q[cols], row_slot[:, cols], context_rows, extra, masked)
            probs = jnp.exp2((scores - top[:, cols]) * exp2_scale) * share[:, cols]
            d_probs = contract(values, grad[cols], 1, 1)
            d_scores = (probs * (d_probs - center[:, cols])).astype(jnp.bfloat16)
            d_values = d_values + contract(probs.astype(jnp.bfloat16), grad[cols], 1, 0)
            acc[:, cols] += contract(keys, d_scores, 0, 0)
        d_values = d_values.astype(jnp.bfloat16)
        dv_ref[pl.ds(g * GROUP, GROUP), :context_rows, :] = d_values[:edge].reshape(
            GROUP, context_rows, HD
        )
        if with_memory:
            dv_ref[pl.ds(g * GROUP, GROUP), context_rows:, :] = d_values[edge:].reshape(
                GROUP, slots, HD
            )

    over_groups(span, step, functools.partial(group_copy, kv_hbm, kv_ref, sems))
    rows = jnp.transpose(acc[...] * score_scale).astype(jnp.bfloat16)
    here = q_ref.shape[0]
    for h in range(HEADS_HERE):
        dq_ref[:, h * HD : (h + 1) * HD] = rows[h * here : (h + 1) * here]


SMEM = pl.BlockSpec(memory_space=pltpu.SMEM)
BIG = pltpu.CompilerParams(vmem_limit_bytes=61 << 20)


def attend(docs, q, kv, context_rows):
    f32 = jnp.float32
    return pl.pallas_call(
        functools.partial(attend_kernel, context_rows),
        out_shape=(
            jax.ShapeDtypeStruct(q.shape, jnp.bfloat16),
            jax.ShapeDtypeStruct((HD, ROWS), f32),
            jax.ShapeDtypeStruct((8, ROWS), f32),
            jax.ShapeDtypeStruct((8, ROWS), f32),
        ),
        in_specs=[SMEM, VMEM, HBM],
        out_specs=(VMEM, VMEM, VMEM, VMEM),
        scratch_shapes=[pltpu.VMEM(kv.shape, kv.dtype), pltpu.SemaphoreType.DMA((kv.shape[0] // GROUP,))],
        compiler_params=BIG,
        name="attend",
    )(docs, q, kv)


def attend_backward(docs, q, grad, kv, ot, top, mass, context_rows):
    return pl.pallas_call(
        functools.partial(backward_kernel, context_rows),
        out_shape=(
            jax.ShapeDtypeStruct(q.shape, jnp.bfloat16),
            jax.ShapeDtypeStruct((*kv.shape[:2], HD), jnp.bfloat16),
        ),
        in_specs=[SMEM, VMEM, VMEM, HBM, VMEM, VMEM, VMEM],
        out_specs=(VMEM, VMEM),
        scratch_shapes=[
            pltpu.VMEM((HD, ROWS), jnp.float32),
            pltpu.VMEM(kv.shape, kv.dtype),
            pltpu.SemaphoreType.DMA((kv.shape[0] // GROUP,)),
        ],
        compiler_params=BIG,
        name="attend_backward",
    )(docs, q, grad, kv, ot, top, mass)


def body(
    context,
    memory,
    query_weight,
    key_weight,
    value_weight,
    query_down_map,
    query_up_map,
    value_down_map,
    value_up_map,
    output_weight,
    decoder_gain,
    document_slots,
    normed_gradient,
):
    tok_dev = context.shape[0]
    slot_dev = memory.shape[0]
    here = coords(PLAIN)
    paired_index = here["y"] * 16 + here["z"] * 4 + here["h"] * 2 + here["c"]
    docs = jnp.concatenate([document_slots, (paired_index * slot_dev).reshape(1).astype(jnp.int32)])
    kv, queries, query_low, value_low, output_weight, normed_gradient, decoder_gain = front(
        key_weight, value_weight, value_down_map, context, memory, query_weight, query_down_map,
        query_up_map, value_up_map, output_weight, normed_gradient, decoder_gain.reshape(-1, 128), 1,
    )
    attended, ot, top, mass = attend(docs, queries, kv, tok_dev)
    d_attended, normed = middle(
        attended, output_weight, normed_gradient, decoder_gain.reshape(1, -1),
        slot_dev * lax.axis_size("seq"), 2,
    )
    d_queries, dv_part = attend_backward(docs, queries, d_attended, kv, ot, top, mass, tok_dev)
    grad_qa, grad_va, query_up_gradient, value_up_gradient = tail(
        dv_part, d_queries, query_low, value_low, query_up_map, value_up_map, memory, context, 3
    )
    return (normed, grad_qa, grad_va, query_up_gradient, value_up_gradient)


def solution(mesh):
    in_specs = (
        P("seq", None),
        P("seq", None),
        P(None, "section"),
        P("seq", "section"),
        P("seq", "section"),
        P(),
        P(None, "section"),
        P("seq", None),
        P(None, "section"),
        P("section", "seq"),
        P("seq"),
        P(),
        P("section", "seq"),
    )
    out_specs = (
        P("section", "seq"),
        P(("section", "seq"), None),
        P(("section", "seq"), None),
        P(None, "section"),
        P(None, "section"),
    )
    return jax.shard_map(body, mesh=mesh, in_specs=in_specs, out_specs=out_specs, check_vma=False)
```

```python
import functools

import jax
import jax.numpy as jnp
from jax import lax
from jax.experimental import pallas as pl
from jax.experimental.pallas import tpu as pltpu
from jax.sharding import PartitionSpec as P

MODEL_DIM = 8192
HEADS_HERE = 8
HD = 128
ROWS = 512
GROUP = 2

adapter_scale = 0.25
epsilon = 1e-05
mask_fill = -1e30
score_scale = HD ** (-0.5)
exp2_scale = score_scale * 1.4426950408889634

MESH = pl.DeviceIdType.MESH
ANY = pl.BlockSpec(memory_space=pl.ANY)
VMEM = pl.BlockSpec(memory_space=pltpu.VMEM)
HBM = pl.BlockSpec(memory_space=pltpu.HBM)

SIZES = {"y": 2, "z": 4, "x": 4, "h": 2, "c": 2}
PLAIN, PAIRED = "yzx", "yzhc"


def coords(axes):
    seq, section = lax.axis_index("seq"), lax.axis_index("section")
    here = {"y": seq // 16, "z": (seq // 4) % 4, "x": seq % 4, "m": section // 2, "c": section % 2}
    here["h"], here["l"] = here["x"] // 2, here["x"] % 2
    return here


def device_at(axes, here):
    x = here["x"] if "x" in axes else here["h"] * 2 + here["l"]
    return (here["m"] * 2 + here["c"], here["y"] * 16 + here["z"] * 4 + x)


def moved(here, axis, step):
    return {**here, axis: lax.rem(here[axis] + step, SIZES[axis])}


def greet(devices, here=None):
    barrier = pltpu.get_barrier_semaphore()
    for device in devices:
        pl.semaphore_signal(barrier, inc=1, device_id=device, device_id_type=MESH)
    if here is not None:

        @pl.when(here["c"] != here["l"])
        def _():
            pl.semaphore_signal(
                barrier, inc=1, device_id=swap_device(here), device_id_type=MESH
            )

    extra = 0 if here is None else lax.rem(here["c"] + here["l"], 2)
    pl.semaphore_wait(barrier, len(devices) + extra)


def swap_device(here):
    return device_at("h", {**here, "c": here["l"], "l": here["c"]})


class Swap:
    def __init__(self, here, source, target, send, recv, local):
        self.apart = here["c"] != here["l"]
        self.there = lambda: pltpu.make_async_remote_copy(
            src_ref=source,
            dst_ref=target,
            send_sem=send,
            recv_sem=recv,
            device_id=swap_device(here),
            device_id_type=MESH,
        )
        self.stays = lambda: pltpu.make_async_copy(source, target, local)

    def start(self):
        @pl.when(self.apart)
        def _():
            self.there().start()

        @pl.when(jnp.logical_not(self.apart))
        def _():
            self.stays().start()

    def wait(self):
        @pl.when(self.apart)
        def _():
            self.there().wait()

        @pl.when(jnp.logical_not(self.apart))
        def _():
            self.stays().wait()


def axis_peers(axes, here):
    return [device_at(axes, moved(here, a, d)) for a in axes for d in range(1, SIZES[a])]


def remote(source, target, send, recv, device):
    copy = pltpu.make_async_remote_copy(
        src_ref=source,
        dst_ref=target,
        send_sem=send,
        recv_sem=recv,
        device_id=device,
        device_id_type=MESH,
    )
    copy.start()
    return copy


class Gather:
    def __init__(self, here, axes, pieces, source, target, sems, base):
        self.here, self.axes, self.pieces, self.base = here, axes, pieces, base
        self.source, self.target = source, target
        self.send, self.recv, self.fore, self.back = sems
        self.place = tuple(here[a] for a in axes)
        self.paired = "c" in axes
        self.partner = device_at(axes, moved(here, "c", 1)) if self.paired else None
        self.copies, self.latest, self.passed = [], {}, []

    def at(self, phase, i, d):
        return self.base + (i * 3 + phase) * 3 + d

    def begin(self):
        if self.paired:
            own = self.target.at[self.place]
            sem = self.base + 9 * len(self.pieces)
            self.passed.append(
                remote(
                    own if self.source is None else self.source,
                    own,
                    self.fore.at[sem],
                    self.back.at[sem],
                    self.partner,
                )
            )

    def arrived(self, phase, i):
        part, order = self.pieces[i]
        axis = order[phase]
        for d, copy in enumerate(self.latest[i]):
            copy.wait_recv()
            if self.paired:
                came = {**self.here, axis: lax.rem(self.here[axis] + SIZES[axis] - d - 1, SIZES[axis])}
                region = self.target.at[
                    tuple(slice(None) if a in order[:phase] else came[a] for a in self.axes)
                    + part
                ]
                at = self.at(phase, i, d)
                self.passed.append(
                    remote(region, region, self.fore.at[at], self.back.at[at], self.partner)
                )

    def launch(self, phase, i):
        part, order = self.pieces[i]
        held = tuple(slice(None) if a in order[:phase] else self.here[a] for a in self.axes)
        region = self.target.at[held + part]
        source = region if phase or self.source is None else self.source.at[part]
        self.latest[i] = []
        for d in range(1, SIZES[order[phase]]):
            at = self.at(phase, i, d - 1)
            device = device_at(self.axes, moved(self.here, order[phase], d))
            self.latest[i].append(remote(source, region, self.send.at[at], self.recv.at[at], device))
        self.copies += self.latest[i]

    def finish(self):
        for i in range(len(self.pieces)):
            self.arrived(2, i)
        for copy in self.passed:
            copy.wait_recv()
        for copy in self.copies + self.passed:
            copy.wait_send()


def run_gathers(gathers, owns, between):
    for gather in gathers:
        gather.begin()
    for phase in range(3):
        for gather in gathers:
            for i in range(len(gather.pieces)):
                if phase:
                    gather.arrived(phase - 1, i)
                    if phase == 1:
                        while owns:
                            owns.pop().wait()
                gather.launch(phase, i)
        between(phase)
    for gather in gathers:
        gather.finish()


def semaphores(count):
    return [pltpu.SemaphoreType.DMA((count,)) for _ in range(4)]


def front_kernel(
    pieces, half_pieces, kv_pieces,
    key_ref, value_ref, down_ref, context_ref, memory_ref, weight_ref, query_down_ref, query_up_ref,
    value_up_ref, wo_ref, ng_ref, gain_ref,
    kv_all, q_out, query_low, value_low, wo_out, ng_out, gain_out,
    shard, w_all, d_all, context, memory, query_down, buffer, acc, projected, kv_own, q_own,
    send, recv, fore, back, k_send, k_recv, k_fore, k_back,
    loads, inputs, local, swap_send, swap_recv, swap_local,
):
    f32, bf16 = jnp.float32, jnp.bfloat16
    here = coords(PLAIN)
    depth = buffer.shape[1]
    count = weight_ref.shape[0] // depth
    half = down_ref.shape[0] // 2
    tok = context_ref.shape[0]

    def load(k):
        return pltpu.make_async_copy(
            weight_ref.at[pl.ds(k * depth, depth)], buffer.at[k % 3], loads.at[k % 3]
        )

    own_half = down_ref.at[pl.ds(here["c"] * half, half)]
    fetches = [
        pltpu.make_async_copy(a, b, inputs.at[i])
        for i, (a, b) in enumerate(
            (
                (key_ref, shard.at[:, pl.ds(0, HD)]),
                (value_ref, shard.at[:, pl.ds(HD, HD)]),
                (memory_ref, memory),
                (query_down_ref, query_down),
                (context_ref, context),
            )
        )
    ]
    for fetch in fetches:
        fetch.start()
    for k in range(2):
        load(k).start()
    greet(axis_peers(PLAIN + "c", here), here)
    swaps = [
        Swap(here, a, b, swap_send.at[i], swap_recv.at[i], swap_local.at[i])
        for i, (a, b) in enumerate(
            (
                (kv_own, kv_all.at[here["y"], here["z"], here["h"], here["l"]]),
                (q_own, q_out),
                (gain_ref, gain_out),
                (ng_ref, ng_out),
                (wo_ref, wo_out),
            )
        )
    ]
    fetches[0].wait()
    fetches[1].wait()
    sems = (send, recv, fore, back)
    plain = Gather(here, PLAIN, pieces, shard, w_all, sems, 0)
    shared = Gather(here, PLAIN + "c", half_pieces, own_half, d_all, sems, 9 * len(pieces) + 1)
    owns = [
        pltpu.make_async_copy(shard, w_all.at[plain.place], local.at[0]),
        pltpu.make_async_copy(own_half, d_all.at[shared.place], local.at[1]),
    ]
    for own in owns:
        own.start()

    def between(phase):
        if phase < 2:
            return
        fetches[2].wait()
        fetches[3].wait()
        low = jnp.dot(memory[...], query_down[...], preferred_element_type=f32).astype(bf16)
        query_low[...] = low
        acc[...] = adapter_scale * jnp.dot(low, query_up_ref[...], preferred_element_type=f32)
        for k in range(count):
            load(k).wait()
            if k + 2 < count:
                load(k + 2).start()
            acc[...] += jnp.dot(
                memory[:, k * depth : (k + 1) * depth], buffer[k % 3], preferred_element_type=f32
            )
        q_own[...] = acc[...].astype(bf16)
        fetches[4].wait()

    run_gathers([plain, shared], owns, between)
    swaps[4].start()
    wide = 4 * shard.shape[0]
    for j in range(8):
        at = (j // 4, j % 4)
        kv_rows = w_all[at].reshape(wide, 2 * HD)
        down_rows = d_all[at].reshape(wide, HD)
        for rows, source in ((slice(0, tok), context), (slice(tok, None), memory)):
            part = source[:, j * wide : (j + 1) * wide]
            for cols, right in ((slice(0, 2 * HD), kv_rows), (slice(2 * HD, None), down_rows)):
                step = jnp.dot(part, right, preferred_element_type=f32)
                projected[rows, cols] = step if j == 0 else projected[rows, cols] + step
    low = projected[:, 2 * HD :].astype(bf16)
    value_low[...] = low
    kv_own[:, :HD] = projected[:, :HD].astype(bf16)
    kv_own[:, HD:] = (
        projected[:, HD : 2 * HD]
        + adapter_scale * jnp.dot(low, value_up_ref[...], preferred_element_type=f32)
    ).astype(bf16)
    swaps[0].start()
    swaps[0].wait()
    gather = Gather(here, PAIRED, kv_pieces, None, kv_all, (k_send, k_recv, k_fore, k_back), 0)

    def rest(phase):
        if phase == 2:
            for swap in swaps[1:4]:
                swap.start()

    run_gathers([gather], [], rest)
    for swap in swaps[1:]:
        swap.wait()


def front(
    key_weight, value_weight, down, context, memory, query_weight, query_down, query_up, value_up,
    output_weight, normed_gradient, gain, collective_id,
):
    f32, bf16 = jnp.float32, jnp.bfloat16
    rows, half = key_weight.shape[0], down.shape[0] // 2
    tok, slots, model = context.shape[0], memory.shape[0], memory.shape[1]
    keys, wide = tok + slots, query_weight.shape[1]
    pieces = cut(rows, 2 * HD, ORDERS[PLAIN])
    half_pieces = cut(half, HD, ORDERS[PLAIN][:3])
    kv_pieces = cut(keys, 2 * HD, ORDERS[PAIRED])
    n = 9 * len(pieces) + 1 + 9 * len(half_pieces) + 1
    like = lambda a: jax.ShapeDtypeStruct(a.shape, a.dtype)
    sizes = [SIZES[a] for a in PAIRED]
    dma = pltpu.SemaphoreType.DMA
    kv, *rest = pl.pallas_call(
        functools.partial(front_kernel, pieces, half_pieces, kv_pieces),
        out_shape=(
            jax.ShapeDtypeStruct((*sizes, keys, 2 * HD), bf16),
            jax.ShapeDtypeStruct((slots, wide), bf16),
            jax.ShapeDtypeStruct((slots, HD), bf16),
            jax.ShapeDtypeStruct((keys, HD), bf16),
            like(output_weight),
            like(normed_gradient),
            like(gain),
        ),
        in_specs=[ANY] * 7 + [VMEM] * 2 + [ANY] * 3,
        out_specs=(ANY, ANY, VMEM, VMEM, ANY, ANY, ANY),
        scratch_shapes=[
            pltpu.VMEM((rows, 2 * HD), bf16),
            pltpu.VMEM((2, 4, 4, rows, 2 * HD), bf16),
            pltpu.VMEM((2, 4, 4, 2, half, HD), bf16),
            pltpu.VMEM((tok, model), bf16),
            pltpu.VMEM((slots, model), bf16),
            pltpu.VMEM((model, HD), bf16),
            pltpu.VMEM((3, 1024, wide), bf16),
            pltpu.VMEM((slots, wide), f32),
            pltpu.VMEM((keys, 3 * HD), f32),
            pltpu.VMEM((keys, 2 * HD), bf16),
            pltpu.VMEM((slots, wide), bf16),
            *semaphores(n),
            *semaphores(9 * len(kv_pieces) + 1),
            dma((3,)),
            dma((5,)),
            dma((2,)),
            dma((5,)),
            dma((5,)),
            dma((5,)),
        ],
        compiler_params=pltpu.CompilerParams(
            collective_id=collective_id, has_side_effects=True, vmem_limit_bytes=61 << 20
        ),
        name="front",
    )(
        key_weight, value_weight, down, context, memory, query_weight, query_down, query_up, value_up,
        output_weight, normed_gradient, gain,
    )
    return kv.reshape(32, keys, 2 * HD), *rest


ORDERS = {
    PLAIN: ("xzy", "zyx", "yxz", "zxy", "yzx", "xyz"),
    PAIRED: ("hzy", "zyh", "yhz", "zhy", "yzh", "hyz"),
}


def cut(rows, cols, orders):
    by_rows = rows // 16 >= 2 * len(orders) or cols == 128
    step = 16 if by_rows else 128
    units = (rows if by_rows else cols) // step
    base, extra = divmod(units, len(orders))
    pieces, at = [], 0
    for i, order in enumerate(orders):
        size = (base + (1 if i < extra else 0)) * step
        if size:
            part = (pl.ds(at, size), pl.ds(0, cols)) if by_rows else (pl.ds(0, rows), pl.ds(at, size))
            pieces.append((part, order))
        at += size
    return pieces


class Scatter:
    def __init__(self, here, axes, pieces, x_ref, o_ref, send, recv, bufs):
        self.here, self.axes, self.pieces, self.x, self.o = here, axes, pieces, x_ref, o_ref
        self.send, self.recv, self.depth = send, recv, len(axes)
        n, depth = len(pieces), len(axes)
        self.inbox = [bufs[depth * i : depth * (i + 1)] for i in range(n)]
        self.partial = [bufs[depth * n + (depth - 1) * i :][: depth - 1] for i in range(n)]
        self.copies, self.latest = [], {}

    def block(self, phase, i, coord):
        part, order = self.pieces[i]
        left = [a for a in self.axes if a not in order[:phase]]
        ref = self.partial[i][phase - 1] if phase else self.x
        tail = () if phase else part
        return ref.at[tuple(coord if a == order[phase] else slice(None) for a in left) + tail]

    def launch(self, phase, i):
        axis = self.pieces[i][1][phase]
        self.latest[i] = []
        for d in range(1, SIZES[axis]):
            at = (i * self.depth + phase) * 3 + d - 1
            self.latest[i].append(
                remote(
                    self.block(phase, i, lax.rem(self.here[axis] + d, SIZES[axis])),
                    self.inbox[i][phase].at[d - 1],
                    self.send.at[at],
                    self.recv.at[at],
                    device_at(self.axes, moved(self.here, axis, d)),
                )
            )
        self.copies.extend(self.latest[i])

    def total(self, phase, i):
        part, order = self.pieces[i]
        axis = order[phase]
        for copy in self.latest[i]:
            copy.wait_recv()
        mine, inbox = self.block(phase, i, self.here[axis]), self.inbox[i][phase]
        left = [SIZES[a] for a in self.axes if a not in order[: phase + 1]]
        count = 1
        for extent in left:
            count *= extent

        def add(k, carry):
            at = ()
            for extent in reversed(left):
                at, k = (k % extent,) + at, k // extent
            whole = mine[at].astype(jnp.float32) if at else mine[...].astype(jnp.float32)
            for d in range(SIZES[axis] - 1):
                whole = whole + inbox[(d,) + at].astype(jnp.float32)
            if phase == self.depth - 1:
                self.o[part] = whole.astype(self.o.dtype)
            else:
                self.partial[i][phase][at] = whole.astype(jnp.bfloat16)
            return carry

        if count == 1:
            add(0, 0)
        else:
            lax.fori_loop(0, count, add, 0)

    def run(self):
        for i in range(len(self.pieces)):
            self.launch(0, i)
        for phase in range(self.depth):
            for i in range(len(self.pieces)):
                self.total(phase, i)
                if phase < self.depth - 1:
                    self.launch(phase + 1, i)
        for copy in self.copies:
            copy.wait_send()


def scatter_plan(rows, cols, axes):
    first = "c" if axes == PAIRED else ""
    pieces = cut(rows, cols, [first + order[::-1] for order in ORDERS[axes]])
    depth = len(axes)
    n = 3 * depth * len(pieces)
    inboxes, partials = [], []
    for part, order in pieces:
        size = tuple(edge.size for edge in part)
        for phase in range(depth):
            left = [SIZES[a] for a in axes if a not in order[: phase + 1]]
            inboxes.append(pltpu.VMEM((SIZES[order[phase]] - 1, *left, *size), jnp.bfloat16))
            if phase < depth - 1:
                partials.append(pltpu.VMEM((*left, *size), jnp.bfloat16))
    sems = [pltpu.SemaphoreType.DMA((n,)), pltpu.SemaphoreType.DMA((n,))]
    return pieces, sems, inboxes + partials


def split_axes(x, axes):
    return x.reshape(*[SIZES[a] for a in axes], *x.shape[1:])


def tail_kernel(
    dv_pieces, pieces, up_pieces, spread,
    dv_ref, dq_ref, query_low, value_low, query_up_ref, value_up_ref, memory_ref, context_ref,
    qa_ref, va_ref, query_up_out, value_up_out,
    dv_own, dv_home, dq_home, context, memory, backs, backs_in, down_x, up_x, own, everyone, result,
    v_send, v_recv, swap_send, swap_recv, swap_local, inputs, b_send, b_recv,
    send, recv, up_send, up_recv, g_send, g_recv, g_fore, g_back, local, *bufs,
):
    f32, bf16 = jnp.float32, jnp.bfloat16
    here = coords(PAIRED)
    slots = memory.shape[0]
    tok = context.shape[0]
    columns = pl.ds(lax.axis_index("section") * memory.shape[1], memory.shape[1])
    fetches = [
        pltpu.make_async_copy(memory_ref.at[:, columns], memory, inputs.at[0]),
        pltpu.make_async_copy(context_ref.at[:, columns], context, inputs.at[1]),
    ]
    for fetch in fetches:
        fetch.start()
    me, member = group_place("section", here)
    others = [lax.rem(me + d, 4) for d in range(1, 4)]
    across = [{**here, "m": 1 - here["m"], "c": lax.rem(here["c"] + d, 2)} for d in range(2)]
    greet(axis_peers(PLAIN + "c", here) + [device_at(PLAIN, place) for place in across], here)

    swaps = [
        Swap(here, a, b, swap_send.at[i], swap_recv.at[i], swap_local.at[i])
        for i, (a, b) in enumerate(((dq_ref, dq_home), (dv_own, dv_home)))
    ]
    at_v, at_up = 7 * len(dv_pieces), 5 * len(up_pieces)
    swaps[0].start()
    Scatter(here, PAIRED, dv_pieces, dv_ref, dv_own, v_send, v_recv, bufs[:at_v]).run()
    swaps[1].start()

    def up_rows(j, block):
        block = (adapter_scale * block).astype(bf16)
        for i in range(8):
            slot, third = divmod(j * 8 + i, 3)
            up_x[slot // 16, (slot // 4) % 4, slot % 4, 16 * third : 16 * third + 16, :] = block[
                16 * i : 16 * i + 16
            ]

    swaps[0].wait()
    for j in range(HEADS_HERE):
        up_rows(j, contract(query_low[...], dq_home[:, j * HD : (j + 1) * HD], 0, 0))
    up_x[1, 2:] = jnp.zeros_like(up_x[1, 2:])
    backs[:slots, :] = (adapter_scale * contract(dq_home[...], query_up_ref[...], 1, 1)).astype(bf16)
    swaps[1].wait()
    up_rows(HEADS_HERE, contract(value_low[...], dv_home[...], 0, 0))
    backs[slots:, :] = (adapter_scale * contract(dv_home[...], value_up_ref[...], 1, 1)).astype(bf16)
    copies = [
        remote(backs, backs_in.at[d], b_send.at[d], b_recv.at[d], member(k))
        for d, k in enumerate(others)
    ]
    up = Scatter(here, PLAIN, up_pieces, up_x, own, up_send, up_recv, bufs[at_v : at_v + at_up])
    down = Scatter(here, PLAIN, pieces, down_x, result, send, recv, bufs[at_v + at_up :])
    gather = Gather(here, PLAIN, spread, own, everyone, (g_send, g_recv, g_fore, g_back), 0)

    def stage(scatter, phase):
        for i in range(len(scatter.pieces)):
            if phase:
                scatter.total(phase - 1, i)
            if phase < 3:
                scatter.launch(phase, i)

    def spread_on(phase):
        for i in range(len(spread)):
            if phase:
                gather.arrived(phase - 1, i)
            gather.launch(phase, i)

    stage(up, 0)
    for copy in copies:
        copy.wait()
    whole = backs[...].astype(f32)
    for d in range(3):
        whole = whole + backs_in[d].astype(f32)
    whole = whole.astype(bf16)
    pair = jnp.concatenate([whole[:slots], whole[slots + tok :]], axis=1)
    for fetch in fetches:
        fetch.wait()
    span = memory.shape[1] // 2
    rows = span // 16
    for y in range(2):
        both = contract(memory[:, y * span : (y + 1) * span], pair, 0, 0)
        more = contract(context[:, y * span : (y + 1) * span], whole[slots : slots + tok], 0, 0)
        down_x[y, :, :, :rows, :] = both[:, :HD].astype(bf16).reshape(4, 4, rows, HD)
        down_x[y, :, :, rows:, :] = (both[:, HD:] + more).astype(bf16).reshape(4, 4, rows, HD)
    stage(down, 0)
    stage(up, 1)
    stage(up, 2)
    stage(down, 1)
    stage(up, 3)
    copy = pltpu.make_async_copy(own, everyone.at[gather.place], local)
    copy.start()
    spread_on(0)
    stage(down, 2)
    copy.wait()
    spread_on(1)
    spread_on(2)
    stage(down, 3)
    qa_ref[...] = result[:rows, :]
    va_ref[...] = result[rows:, :]
    gather.finish()
    for j in range(HEADS_HERE + 1):
        for i in range(8):
            slot, third = divmod(j * 8 + i, 3)
            tile = everyone[slot // 16, (slot // 4) % 4, slot % 4, 16 * third : 16 * third + 16, :]
            if j < HEADS_HERE:
                query_up_out[16 * i : 16 * i + 16, j * HD : (j + 1) * HD] = tile
            else:
                value_up_out[16 * i : 16 * i + 16, :] = tile
    for one in up.copies + down.copies:
        one.wait_send()


def tail(dv_part, d_queries, query_low, value_low, query_up_map, value_up_map, memory, context, collective_id):
    f32, bf16 = jnp.float32, jnp.bfloat16
    _, keys, _ = dv_part.shape
    slots, tok = memory.shape[0], context.shape[0]
    width = memory.shape[1] // 4
    rows = width // 32
    dv_pieces, dv_sems, dv_bufs = scatter_plan(keys, HD, PAIRED)
    pieces, sems, bufs = scatter_plan(2 * rows, HD, PLAIN)
    up_pieces, up_sems, up_bufs = scatter_plan(48, HD, PLAIN)
    spread = cut(48, HD, ORDERS[PLAIN])
    dma = pltpu.SemaphoreType.DMA
    return pl.pallas_call(
        functools.partial(tail_kernel, dv_pieces, pieces, up_pieces, spread),
        out_shape=(
            jax.ShapeDtypeStruct((rows, HD), f32),
            jax.ShapeDtypeStruct((rows, HD), f32),
            jax.ShapeDtypeStruct(query_up_map.shape, f32),
            jax.ShapeDtypeStruct(value_up_map.shape, f32),
        ),
        in_specs=[VMEM, ANY, VMEM, VMEM, VMEM, VMEM, ANY, ANY],
        out_specs=(VMEM,) * 4,
        scratch_shapes=[
            pltpu.VMEM((keys, HD), bf16),
            pltpu.VMEM((keys, HD), bf16),
            pltpu.VMEM(d_queries.shape, bf16),
            pltpu.VMEM((tok, width), bf16),
            pltpu.VMEM((slots, width), bf16),
            pltpu.VMEM((slots + keys, HD), bf16),
            pltpu.VMEM((3, slots + keys, HD), bf16),
            pltpu.VMEM((2, 4, 4, 2 * rows, HD), bf16),
            pltpu.VMEM((2, 4, 4, 48, HD), bf16),
            pltpu.VMEM((48, HD), f32),
            pltpu.VMEM((2, 4, 4, 48, HD), f32),
            pltpu.VMEM((2 * rows, HD), f32),
            *dv_sems,
            dma((2,)),
            dma((2,)),
            dma((2,)),
            dma((2,)),
            dma((3,)),
            dma((3,)),
            *sems,
            *up_sems,
            *semaphores(9 * len(spread) + 1),
            dma,
            *dv_bufs,
            *up_bufs,
            *bufs,
        ],
        compiler_params=pltpu.CompilerParams(
            collective_id=collective_id, has_side_effects=True, vmem_limit_bytes=40 << 20
        ),
        name="tail",
    )(
        split_axes(dv_part, PAIRED), d_queries, query_low, value_low, query_up_map, value_up_map,
        memory, context,
    )


def middle_kernel(
    pieces, scatter_pieces, total_slots, x_ref, wo_ref, ng_ref, gain_ref, o_ref, normed_out,
    everyone, part, inbox, hidden, grads, d_part, normed, stat, near_in, far_in,
    send, recv, fore, back, local, h_send, h_recv, s_send, s_recv, g_send, g_recv,
    swap_send, swap_recv, swap_local, r_send, r_recv, *bufs,
):
    f32, bf16 = jnp.float32, jnp.bfloat16
    here = coords(PAIRED)
    me, member = group_place("paired section", here)
    others = [lax.rem(me + d, 4) for d in range(1, 4)]
    near = [{**here, "h": lax.rem(here["h"] + a, 2), "c": lax.rem(here["c"] + b, 2)} for a, b in ((0, 1), (1, 0), (1, 1))]
    far = [
        {**here, "y": lax.rem(here["y"] + a, 2), "z": lax.rem(here["z"] + b, 4)}
        for a in range(2)
        for b in range(4)
        if a or b
    ]
    devices = [member(k) for k in others] + [device_at(PAIRED, place) for place in near + far]
    greet(devices, here)

    gather = Gather(here, PAIRED, pieces, x_ref, everyone, (send, recv, fore, back), 0)
    own = pltpu.make_async_copy(x_ref, everyone.at[gather.place], local)
    own.start()
    run_gathers([gather], [own], lambda phase: None)

    def slab(ref, k):
        return ref.at[k // 2, pl.ds(2 * (k % 2), 2)]

    copies = []
    for d in (2, 1, 3, 0):
        k = lax.rem(me + d, 4)
        rows = slab(everyone, k)[...].reshape(ROWS, x_ref.shape[1])
        part[k] = jnp.dot(rows, wo_ref[...], preferred_element_type=f32).astype(bf16)
        if d:
            copies.append(
                remote(part.at[k], inbox.at[d - 1], h_send.at[d - 1], h_recv.at[d - 1], member(k))
            )
    scaled = (total_slots ** (-0.5)) * ng_ref[...].astype(f32) * gain_ref[...]
    for copy in copies:
        copy.wait()
    summed = part[me].astype(f32)
    for d in range(3):
        summed = summed + inbox[d].astype(f32)
    hidden[...] = summed

    ones = jnp.ones((8, summed.shape[1]), f32)
    row_sums = lambda v: lax.dot_general(
        ones, v, (((1,), (1,)), ((), ())), preferred_element_type=f32, precision=lax.Precision.HIGHEST
    )
    first = lax.broadcasted_iota(jnp.int32, (8, ROWS), 0) == 0
    total = jnp.where(first, row_sums(summed * summed), row_sums(scaled * summed))
    stat[0] = total
    at = 0
    for step, (places, box) in enumerate(((near, near_in), (far, far_in))):
        copies = [
            remote(stat.at[step], box.at[k], s_send.at[at + k], s_recv.at[at + k], device_at(PAIRED, place))
            for k, place in enumerate(places)
        ]
        at += len(places)
        for copy in copies:
            copy.wait()
        for k in range(len(places)):
            total = total + box[k]
        if step == 0:
            stat[1] = total
    inv = lax.rsqrt(total[0:1, :] / MODEL_DIM + epsilon)
    pull = inv * inv * inv * total[1:2, :] / MODEL_DIM
    across = lambda v: jnp.transpose(v + jnp.zeros((HD, ROWS), f32))
    inv, pull = across(inv), across(pull)
    for j in range(summed.shape[1] // HD):
        cols = slice(j * HD, (j + 1) * HD)
        value = hidden[:, cols]
        normed[:, cols] = (value * inv * gain_ref[:, cols]).astype(bf16)
        weighted = (total_slots ** (-0.5)) * ng_ref[:, cols].astype(f32) * gain_ref[:, cols]
        grads[me, :, cols] = (inv * weighted - value * pull).astype(bf16)
    copies = [
        remote(grads.at[me], grads.at[me], g_send.at[d], g_recv.at[d], member(k))
        for d, k in enumerate(others)
    ]
    swap = Swap(here, normed, normed_out, swap_send, swap_recv, swap_local)
    swap.start()

    def back_through(k):
        rows = contract(grads[k], wo_ref[...], 1, 1).astype(bf16)
        slab(d_part, k)[...] = rows.reshape(2, 2, 2, x_ref.shape[0], x_ref.shape[1])

    back_through(me)
    for d in range(3):
        copies[2 - d].wait_recv()
        back_through(lax.rem(me + 4 - (3 - d), 4))
    for copy in copies:
        copy.wait_send()
    Scatter(here, PAIRED, scatter_pieces, d_part, o_ref, r_send, r_recv, bufs).run()
    swap.wait()


def middle(x, output_weight, normed_gradient, gain, total_slots, collective_id):
    bf16, f32 = jnp.bfloat16, jnp.float32
    rows, cols = x.shape
    width = output_weight.shape[1]
    pieces = cut(rows, cols, ORDERS[PAIRED])
    scatter_pieces, sems, bufs = scatter_plan(rows, cols, PAIRED)
    sizes = [SIZES[a] for a in PAIRED]
    dma = pltpu.SemaphoreType.DMA
    return pl.pallas_call(
        functools.partial(middle_kernel, pieces, scatter_pieces, total_slots),
        out_shape=(
            jax.ShapeDtypeStruct(x.shape, bf16),
            jax.ShapeDtypeStruct(normed_gradient.shape, bf16),
        ),
        in_specs=[VMEM] * 4,
        out_specs=(VMEM, ANY),
        scratch_shapes=[
            pltpu.VMEM((*sizes, rows, cols), bf16),
            pltpu.VMEM((4, ROWS, width), bf16),
            pltpu.VMEM((3, ROWS, width), bf16),
            pltpu.VMEM((ROWS, width), f32),
            pltpu.VMEM((4, ROWS, width), bf16),
            pltpu.VMEM((*sizes, rows, cols), bf16),
            pltpu.VMEM((ROWS, width), bf16),
            pltpu.VMEM((2, 8, ROWS), f32),
            pltpu.VMEM((3, 8, ROWS), f32),
            pltpu.VMEM((7, 8, ROWS), f32),
            *semaphores(9 * len(pieces) + 1),
            dma,
            dma((3,)),
            dma((3,)),
            dma((10,)),
            dma((10,)),
            dma((3,)),
            dma((3,)),
            dma,
            dma,
            dma,
            *sems,
            *bufs,
        ],
        compiler_params=pltpu.CompilerParams(
            collective_id=collective_id, has_side_effects=True, vmem_limit_bytes=32 << 20
        ),
        name="middle",
    )(x, output_weight, normed_gradient, gain)


def group_place(group, here):
    if group == "section":
        return here["m"] * 2 + here["c"], lambda k: device_at("x", {**here, "m": k // 2, "c": k % 2})
    return here["m"] * 2 + here["l"], lambda k: device_at("h", {**here, "m": k // 2, "l": k % 2})

def contract(left, right, l, r):
    return lax.dot_general(
        left, right, (((l,), (r,)), ((), ())), preferred_element_type=jnp.float32
    )


def head_rows(ref):
    return jnp.concatenate([ref[:, h * HD : (h + 1) * HD] for h in range(HEADS_HERE)], axis=0)


def key_block(kv_ref, g, cols, context_rows, slots):
    context = kv_ref[pl.ds(g * GROUP, GROUP), :context_rows, cols]
    context = context.reshape(GROUP * context_rows, HD)
    if not slots:
        return context
    memory = kv_ref[pl.ds(g * GROUP, GROUP), context_rows:, cols]
    return jnp.concatenate([context, memory.reshape(GROUP * slots, HD)], axis=0)


def key_docs(g, bounds, context_rows, slots):
    edge = GROUP * context_rows
    token = g * edge + lax.broadcasted_iota(jnp.int32, (edge, HD), 0)
    docs = (token >= 4 * bounds[0][0:1, :]) & (token < 4 * bounds[1][0:1, :])
    if slots:
        slot = g * (GROUP * slots) + lax.broadcasted_iota(jnp.int32, (GROUP * slots, HD), 0)
        docs = jnp.concatenate(
            [
                docs.astype(jnp.float32),
                ((slot >= bounds[0][0:1, :]) & (slot < bounds[1][0:1, :])).astype(jnp.float32),
            ],
            axis=0,
        )
    return docs.astype(jnp.float32).astype(jnp.bfloat16)


def documents(docs_ref):
    starts, ends, at = [], [], 0
    for k in range(docs_ref.shape[0] - 1):
        starts.append(at)
        at = at + docs_ref[k]
        ends.append(at)
    return starts, ends


def place_rows(docs_ref, here):
    starts, ends = documents(docs_ref)
    first = docs_ref[docs_ref.shape[0] - 1]
    last = first + here - 1
    lane = lax.broadcasted_iota(jnp.int32, (8, HD), 1)
    low_lane, high_lane = jnp.zeros((8, HD), jnp.int32), jnp.zeros((8, HD), jnp.int32)
    slot = first + lax.rem(lax.broadcasted_iota(jnp.int32, (ROWS, HD), 0), here)
    low = jnp.zeros((ROWS, HD), jnp.int32)
    start, stop = 0, ends[-1]
    for k in range(len(starts)):
        low_lane = jnp.where(lane == k, starts[k], low_lane)
        high_lane = jnp.where(lane == k, ends[k], high_lane)
        low = jnp.where(slot >= starts[k], starts[k], low)
        start = jnp.where(first >= starts[k], starts[k], start)
        stop = jnp.where((last >= starts[k]) & (last < ends[k]), ends[k], stop)
    mine = low == low_lane[0:1, :]
    fill = jnp.where(mine, 0.0, mask_fill).astype(jnp.bfloat16)
    row_slot = first + lax.rem(lax.broadcasted_iota(jnp.int32, (8, ROWS), 1), here)
    unit = GROUP * here
    span = (start // unit, first // unit, (stop + unit - 1) // unit)
    return span, row_slot, (low_lane, high_lane), fill


HALVES = (slice(0, ROWS // 2), slice(ROWS // 2, ROWS))


def group_scores(keys, docs, g, q_wide, row_slot, context_rows, slots, causal):
    scores = contract(jnp.concatenate([keys, docs], axis=1), q_wide, 1, 1)
    if not causal:
        return scores
    edge = GROUP * context_rows
    slot = g * (GROUP * slots) + lax.broadcasted_iota(
        jnp.int32, (GROUP * slots, q_wide.shape[0]), 0
    )
    return jnp.concatenate(
        [scores[:edge], jnp.where(slot <= row_slot[0:1, :], scores[edge:], mask_fill)], axis=0
    )


def group_copy(kv_hbm, kv_ref, sems, g):
    return pltpu.make_async_copy(
        kv_hbm.at[pl.ds(g * GROUP, GROUP)], kv_ref.at[pl.ds(g * GROUP, GROUP)], sems.at[g]
    )


def over_groups(span, step, fetch):
    first, own, last = span[0], span[1], span[2]

    def ask(g, carry):
        fetch(g).start()
        return carry

    def before(g, carry):
        fetch(g).wait()
        step(g, False, True)
        return carry

    def after(g, carry):
        fetch(g).wait()
        step(g, False, False)
        return carry

    fetch(own).start()
    lax.fori_loop(first, own, ask, 0)
    lax.fori_loop(own + 1, last, ask, 0)
    fetch(own).wait()
    step(own, True, True)
    lax.fori_loop(first, own, before, 0)
    lax.fori_loop(own + 1, last, after, 0)


def attend_kernel(
    context_rows, docs_ref, q_ref, kv_hbm, o_ref, ot_ref, top_ref, mass_ref, kv_ref, sems
):
    slots = kv_ref.shape[1] - context_rows
    span, row_slot, bounds, fill = place_rows(docs_ref, q_ref.shape[0])
    q = jnp.concatenate([head_rows(q_ref), fill], axis=1)
    ot_ref[...] = jnp.zeros_like(ot_ref)
    top_ref[...] = jnp.full_like(top_ref, mask_fill)
    mass_ref[...] = jnp.zeros_like(mass_ref)

    def step(g, masked, with_memory):
        extra = slots if with_memory else 0
        keys = key_block(kv_ref, g, slice(0, HD), context_rows, extra)
        values = key_block(kv_ref, g, slice(HD, 2 * HD), context_rows, extra)
        docs = key_docs(g, bounds, context_rows, extra)
        for cols in (slice(0, ROWS),):
            scores = group_scores(keys, docs, g, q[cols], row_slot[:, cols], context_rows, extra, masked)
            before = top_ref[0:1, cols]
            top = jnp.maximum(before, jnp.max(scores, axis=0, keepdims=True))
            keep = jnp.exp2((before - top) * exp2_scale)
            weight = jnp.exp2((scores - top) * exp2_scale)
            top_ref[0:1, cols] = top
            mass_ref[0:1, cols] = mass_ref[0:1, cols] * keep + jnp.sum(weight, axis=0, keepdims=True)
            ot_ref[:, cols] = ot_ref[:, cols] * keep + contract(
                values, weight.astype(jnp.bfloat16), 0, 0
            )

    over_groups(span, step, functools.partial(group_copy, kv_hbm, kv_ref, sems))
    ot_ref[...] = ot_ref[...] / mass_ref[0:1, :]
    rows = jnp.transpose(ot_ref[...]).astype(jnp.bfloat16)
    here = q_ref.shape[0]
    for h in range(HEADS_HERE):
        o_ref[:, h * HD : (h + 1) * HD] = rows[h * here : (h + 1) * here]


def backward_kernel(
    context_rows, docs_ref, q_ref, g_ref, kv_hbm, ot_ref, top_ref, mass_ref,
    dq_ref, dv_ref, acc, kv_ref, sems,
):
    slots = kv_ref.shape[1] - context_rows
    edge = GROUP * context_rows
    span, row_slot, bounds, fill = place_rows(docs_ref, q_ref.shape[0])
    q = jnp.concatenate([head_rows(q_ref), fill], axis=1)
    grad = head_rows(g_ref)
    center = jnp.sum(jnp.transpose(grad.astype(jnp.float32)) * ot_ref[...], axis=0, keepdims=True)
    top = top_ref[0:1, :]
    share = 1.0 / mass_ref[0:1, :]
    acc[...] = jnp.zeros_like(acc)
    dv_ref[...] = jnp.zeros_like(dv_ref)

    def step(g, masked, with_memory):
        extra = slots if with_memory else 0
        keys = key_block(kv_ref, g, slice(0, HD), context_rows, extra)
        values = key_block(kv_ref, g, slice(HD, 2 * HD), context_rows, extra)
        docs = key_docs(g, bounds, context_rows, extra)
        d_values = 0.0
        for cols in HALVES:
            scores = group_scores(keys, docs, g, q[cols], row_slot[:, cols], context_rows, extra, masked)
            probs = jnp.exp2((scores - top[:, cols]) * exp2_scale) * share[:, cols]
            d_probs = contract(values, grad[cols], 1, 1)
            d_scores = (probs * (d_probs - center[:, cols])).astype(jnp.bfloat16)
            d_values = d_values + contract(probs.astype(jnp.bfloat16), grad[cols], 1, 0)
            acc[:, cols] += contract(keys, d_scores, 0, 0)
        d_values = d_values.astype(jnp.bfloat16)
        dv_ref[pl.ds(g * GROUP, GROUP), :context_rows, :] = d_values[:edge].reshape(
            GROUP, context_rows, HD
        )
        if with_memory:
            dv_ref[pl.ds(g * GROUP, GROUP), context_rows:, :] = d_values[edge:].reshape(
                GROUP, slots, HD
            )

    over_groups(span, step, functools.partial(group_copy, kv_hbm, kv_ref, sems))
    rows = jnp.transpose(acc[...] * score_scale).astype(jnp.bfloat16)
    here = q_ref.shape[0]
    for h in range(HEADS_HERE):
        dq_ref[:, h * HD : (h + 1) * HD] = rows[h * here : (h + 1) * here]


SMEM = pl.BlockSpec(memory_space=pltpu.SMEM)
BIG = pltpu.CompilerParams(vmem_limit_bytes=48 << 20)


def attend(docs, q, kv, context_rows):
    f32 = jnp.float32
    return pl.pallas_call(
        functools.partial(attend_kernel, context_rows),
        out_shape=(
            jax.ShapeDtypeStruct(q.shape, jnp.bfloat16),
            jax.ShapeDtypeStruct((HD, ROWS), f32),
            jax.ShapeDtypeStruct((8, ROWS), f32),
            jax.ShapeDtypeStruct((8, ROWS), f32),
        ),
        in_specs=[SMEM, VMEM, HBM],
        out_specs=(VMEM, VMEM, VMEM, VMEM),
        scratch_shapes=[pltpu.VMEM(kv.shape, kv.dtype), pltpu.SemaphoreType.DMA((kv.shape[0] // GROUP,))],
        compiler_params=pltpu.CompilerParams(vmem_limit_bytes=61 << 20),
        name="attend",
    )(docs, q, kv)


def attend_backward(docs, q, grad, kv, ot, top, mass, context_rows):
    return pl.pallas_call(
        functools.partial(backward_kernel, context_rows),
        out_shape=(
            jax.ShapeDtypeStruct(q.shape, jnp.bfloat16),
            jax.ShapeDtypeStruct((*kv.shape[:2], HD), jnp.bfloat16),
        ),
        in_specs=[SMEM, VMEM, VMEM, HBM, VMEM, VMEM, VMEM],
        out_specs=(VMEM, VMEM),
        scratch_shapes=[
            pltpu.VMEM((HD, ROWS), jnp.float32),
            pltpu.VMEM(kv.shape, kv.dtype),
            pltpu.SemaphoreType.DMA((kv.shape[0] // GROUP,)),
        ],
        compiler_params=BIG,
        name="attend_backward",
    )(docs, q, grad, kv, ot, top, mass)


def body(
    context,
    memory,
    query_weight,
    key_weight,
    value_weight,
    query_down_map,
    query_up_map,
    value_down_map,
    value_up_map,
    output_weight,
    decoder_gain,
    document_slots,
    normed_gradient,
):
    tok_dev = context.shape[0]
    slot_dev = memory.shape[0]
    here = coords(PLAIN)
    paired_index = here["y"] * 16 + here["z"] * 4 + here["h"] * 2 + here["c"]
    docs = jnp.concatenate([document_slots, (paired_index * slot_dev).reshape(1).astype(jnp.int32)])
    kv, queries, query_low, value_low, output_weight, normed_gradient, decoder_gain = front(
        key_weight, value_weight, value_down_map, context, memory, query_weight, query_down_map,
        query_up_map, value_up_map, output_weight, normed_gradient, decoder_gain.reshape(-1, 128), 1,
    )
    attended, ot, top, mass = attend(docs, queries, kv, tok_dev)
    d_attended, normed = middle(
        attended, output_weight, normed_gradient, decoder_gain.reshape(1, -1),
        slot_dev * lax.axis_size("seq"), 2,
    )
    d_queries, dv_part = attend_backward(docs, queries, d_attended, kv, ot, top, mass, tok_dev)
    grad_qa, grad_va, query_up_gradient, value_up_gradient = tail(
        dv_part, d_queries, query_low, value_low, query_up_map, value_up_map, memory, context, 3
    )
    return (normed, grad_qa, grad_va, query_up_gradient, value_up_gradient)


def solution(mesh):
    in_specs = (
        P("seq", None),
        P("seq", None),
        P(None, "section"),
        P("seq", "section"),
        P("seq", "section"),
        P(),
        P(None, "section"),
        P("seq", None),
        P(None, "section"),
        P("section", "seq"),
        P("seq"),
        P(),
        P("section", "seq"),
    )
    out_specs = (
        P("section", "seq"),
        P(("section", "seq"), None),
        P(("section", "seq"), None),
        P(None, "section"),
        P(None, "section"),
    )
    return jax.shard_map(body, mesh=mesh, in_specs=in_specs, out_specs=out_specs, check_vma=False)
```
